32 devices in a mesh: dp: 4 (over z), row: 2 (over x), col: 4 (over y, core).
Axes of the slice: x: 2, y: 2, z: 4, core: 2. Of those that a mesh axis runs over, the one named last changes fastest.
Arguments:
- tokens: bfloat16 [768, 16384], P(('row', 'col'), 'dp'), may hold values from -6 to 6
- cotangent: bfloat16 [768, 16384], P(('row', 'col'), 'dp'), may hold values from -6 to 6
- holder_of: int32 [8, 4], replicated, may hold values from 0 to 3, each once within a row
- lengths: int32 [8, 4, 4], replicated, may hold values from 0 to 512, as said below
- input_gain: float32 [768], P(('row', 'col')), may hold values from 0.5 to 1.5
- input_shift: float32 [768], P(('row', 'col')), may hold values from -1.5 to 1.5
- attend_weight: bfloat16 [3, 768, 768], P(None, 'col', 'row'), may hold values from -0.21875 to 0.21875
- attend_bias: float32 [2, 768], P(None, 'col'), may hold values from -1.5 to 1.5
- mixed_gain: float32 [768], P('col'), may hold values from 0.5 to 1.5
- mixed_shift: float32 [768], P('col'), may hold values from -1.5 to 1.5
- output_weight: bfloat16 [768, 768], P('col', 'row'), may hold values from -0.375 to 0.375
- output_bias: float32 [768], P(('row', 'col')), may hold values from -1.5 to 1.5
- middle_gain: float32 [768], P(('row', 'col')), may hold values from 0.5 to 1.5
- middle_shift: float32 [768], P(('row', 'col')), may hold values from -1.5 to 1.5
- expand_weight: bfloat16 [768, 3072], P('row', 'col'), may hold values from -0.375 to 0.375
- expand_bias: float32 [3072], P('col'), may hold values from -1.5 to 1.5
- hidden_gain: float32 [3072], P('col'), may hold values from 0.5 to 1.5
- hidden_shift: float32 [3072], P('col'), may hold values from -1.5 to 1.5
- shrink_weight: bfloat16 [3072, 768], P('col', 'row'), may hold values from -0.1875 to 0.1875
- shrink_bias: float32 [768], P(('row', 'col')), may hold values from -1.5 to 1.5
Outputs:
- block_out: bfloat16 [768, 16384], P(('row', 'col'), 'dp')
- input_grad: bfloat16 [768, 16384], P(('row', 'col'), 'dp')
- input_gain_grad: float32 [768], P(('row', 'col'))
- input_shift_grad: float32 [768], P(('row', 'col'))
- attend_weight_grad: float32 [3, 768, 768], P(None, 'col', 'row')
- attend_bias_grad: float32 [2, 768], P(None, 'col')
- mixed_gain_grad: float32 [768], P('col')
- mixed_shift_grad: float32 [768], P('col')
- output_weight_grad: float32 [768, 768], P('col', 'row')
- output_bias_grad: float32 [768], P(('row', 'col'))
- middle_gain_grad: float32 [768], P(('row', 'col'))
- middle_shift_grad: float32 [768], P(('row', 'col'))
- expand_weight_grad: float32 [768, 3072], P('row', 'col')
- expand_bias_grad: float32 [3072], P('col')
- hidden_gain_grad: float32 [3072], P('col')
- hidden_shift_grad: float32 [3072], P('col')
- shrink_weight_grad: float32 [3072, 768], P('col', 'row')
- shrink_bias_grad: float32 [768], P(('row', 'col'))
The draws below stay inside these ranges and needn't reach their ends.
Inputs may be any that keep to these rules, and one draw needn't show every extreme that they name: Each row of holder_of names every holder once. The 4 lengths of a unit add up to 512; a zero length is an empty slot; in every micro-batch one unit is a single sequence of 512 tokens.
All inputs are finite; a program needn't handle non-finite values.
Results may differ from the reference program's by a relative error of at most 0.017.
Values may be sent and summed in bfloat16 or wider, within the bound.
No kernel may reach another device: no remote copies, remote signals or barrier semaphores. Data moves between devices by JAX's collectives and lax.ppermute only.
A program may use at most 128 MiB of HBM per device.

```python
import math
import jax
import jax.numpy as jnp
from jax import lax

D = 768
HEADS = 12
HEAD = 64
FF = 3072
UNIT = 512
MICRO = 8
SEQS = 4
HOLDERS = 4
ROWS = 16
N_DP = 4


def draw_lengths(key, part):
    cut_key, pick_key = jax.random.split(jax.random.fold_in(key, 17))
    cuts = jax.random.randint(cut_key, (MICRO, HOLDERS, SEQS - 1), 0, UNIT + 1)
    cuts = jnp.sort(cuts, axis=2)
    lower = jnp.zeros((MICRO, HOLDERS, 1), jnp.int32)
    upper = jnp.full((MICRO, HOLDERS, 1), UNIT, jnp.int32)
    bounds = jnp.concatenate([lower, cuts.astype(jnp.int32), upper], axis=2)
    ragged = bounds[:, :, 1:] - bounds[:, :, :-1]
    whole_unit = jax.random.randint(pick_key, (MICRO, 1), 0, HOLDERS)
    is_whole = jnp.arange(HOLDERS, dtype=jnp.int32)[None, :] == whole_unit
    single = (jnp.arange(SEQS, dtype=jnp.int32) == 0).astype(jnp.int32) * UNIT
    return jnp.where(is_whole[:, :, None], single[None, None, :], ragged).astype(jnp.int32)


def steps_of(key, extent, cuts, least, largest):
    level = 1.0
    for position, blocks in cuts:
        heights = jax.random.uniform(jax.random.fold_in(jax.random.fold_in(key, 6), position), (blocks,), jnp.float32, least / len(cuts), largest / len(cuts))
        level = level * jnp.repeat(jnp.exp(heights), extent[position] // blocks).reshape((-1,) + (1,) * (len(extent) - 1 - position))
    return level


def normal_values(own_key, extent, deviation, reach, shards=(), kind=jnp.bfloat16):
    result = jax.random.normal(own_key, extent, jnp.float32) * deviation
    if len(shards) > 0:
        result = steps_of(own_key, extent, shards, -0.22, 0.18) * result
    return jnp.clip(result, min=-reach, max=reach).astype(kind)


def setup_inputs(seed: int = 0) -> dict:
    keys = jax.random.split(jax.random.key(seed), 21)
    tokens = normal_values(keys[0], (D, 2 * UNIT * ROWS), 1.0, 6.0, ((0, 8), (1, 4)))
    cotangent = normal_values(keys[1], (D, 2 * UNIT * ROWS), 1.0, 6.0, ((0, 8), (1, 4)))
    holder_of = jax.vmap(lambda own: jax.random.permutation(own, HOLDERS))(jax.random.split(keys[2], MICRO)).reshape((MICRO, HOLDERS)).astype(jnp.int32)
    lengths = draw_lengths(jax.random.fold_in(keys[20], 71), 0)
    input_gain = jnp.clip(1.0 + 0.1 * jax.random.normal(keys[4], (D,), jnp.float32), 0.5, 1.5)
    input_shift = normal_values(keys[5], (D,), 0.3, 1.5, ((0, 8),), jnp.float32)
    attend_weight = normal_values(keys[6], (3, D, D), D ** -0.5, 0.21875, ((1, 4), (2, 2)))
    attend_bias = normal_values(keys[7], (2, D), 0.3, 1.5, ((1, 4),), jnp.float32)
    mixed_gain = jnp.clip(1.0 + 0.1 * jax.random.normal(keys[8], (D,), jnp.float32), 0.5, 1.5)
    mixed_shift = normal_values(keys[9], (D,), 0.3, 1.5, ((0, 4),), jnp.float32)
    output_weight = normal_values(keys[10], (D, D), (D // 3) ** -0.5, 0.375, ((0, 4), (1, 2)))
    output_bias = normal_values(keys[11], (D,), 0.3, 1.5, ((0, 8),), jnp.float32)
    middle_gain = jnp.clip(1.0 + 0.1 * jax.random.normal(keys[12], (D,), jnp.float32), 0.5, 1.5)
    middle_shift = normal_values(keys[13], (D,), 0.3, 1.5, ((0, 8),), jnp.float32)
    expand_weight = normal_values(keys[14], (D, FF), (D // 3) ** -0.5, 0.375, ((0, 2), (1, 4)))
    expand_bias = normal_values(keys[15], (FF,), 0.3, 1.5, ((0, 4),), jnp.float32)
    hidden_gain = jnp.clip(1.0 + 0.1 * jax.random.normal(keys[16], (FF,), jnp.float32), 0.5, 1.5)
    hidden_shift = normal_values(keys[17], (FF,), 0.3, 1.5, ((0, 4),), jnp.float32)
    shrink_weight = normal_values(keys[18], (FF, D), (FF // 3) ** -0.5, 0.1875, ((0, 4), (1, 2)))
    shrink_bias = normal_values(keys[19], (D,), 0.3, 1.5, ((0, 8),), jnp.float32)
    return {"tokens": tokens, "cotangent": cotangent, "holder_of": holder_of, "lengths": lengths, "input_gain": input_gain, "input_shift": input_shift, "attend_weight": attend_weight, "attend_bias": attend_bias, "mixed_gain": mixed_gain, "mixed_shift": mixed_shift, "output_weight": output_weight, "output_bias": output_bias, "middle_gain": middle_gain, "middle_shift": middle_shift, "expand_weight": expand_weight, "expand_bias": expand_bias, "hidden_gain": hidden_gain, "hidden_shift": hidden_shift, "shrink_weight": shrink_weight, "shrink_bias": shrink_bias}


@jax.custom_vjp
def low(v):
    return lax.optimization_barrier(v.astype(jnp.bfloat16)).astype(jnp.float32)

@jax.custom_vjp
def low_back(v):
    return v

def low_keep(v):
    return (low(v), None)

def low_pass(kept, grad):
    return (grad,)

def back_keep(v):
    return (v, None)

def back_low(kept, grad):
    return (low(grad),)
low.defvjp(low_keep, low_pass)
low_back.defvjp(back_keep, back_low)
highest = lax.Precision.HIGHEST
norm_eps = 1e-05
masked_score = -1e+30

def normalize(values, gain_vec, offset):
    center = lax.optimization_barrier(jnp.mean(values, axis=-1, keepdims=True))
    shifted = values - center
    spread = lax.rsqrt(lax.optimization_barrier(jnp.mean(shifted * shifted, axis=-1, keepdims=True)) + norm_eps)
    return shifted * spread * gain_vec + offset

def segment_ids(unit_lengths):
    bounds = jnp.cumsum(unit_lengths)[:-1]
    positions = jnp.arange(UNIT, dtype=jnp.int32)
    return lax.optimization_barrier(jnp.sum((positions[:, None] >= bounds[None, :]).astype(jnp.int32), axis=1))

def unit_forward(params, unit_in, segment):
    input_gain, input_shift, attend_weight, attend_bias, mixed_gain, mixed_shift, output_weight, output_bias, middle_gain, middle_shift, expand_weight, expand_bias, hidden_gain, hidden_shift, shrink_weight, shrink_bias = params
    normed_in = low(normalize(unit_in, input_gain, input_shift))
    attend_matrix = jnp.transpose(attend_weight, (2, 0, 1)).reshape(D, 3 * D)
    triple = jnp.dot(normed_in, attend_matrix, precision=highest).reshape(UNIT, 3, D)
    queries = low(low_back(triple[:, 0] + attend_bias[0])).reshape(UNIT, HEADS, HEAD)
    keys_all = low(low_back(triple[:, 1])).reshape(UNIT, HEADS, HEAD)
    values_all = low(low_back(triple[:, 2] + attend_bias[1])).reshape(UNIT, HEADS, HEAD)
    scores = jnp.einsum('qhe,khe->hqk', queries, keys_all, precision=highest) * (1.0 / math.sqrt(HEAD))
    scores = low_back(scores)
    visible = segment[:, None] == segment[None, :]
    scores = jnp.where(visible[None], scores, masked_score)
    probability = low(jax.nn.softmax(scores, axis=-1))
    mixed = jnp.einsum('hqk,khe->qhe', probability, values_all, precision=highest).reshape(UNIT, D)
    mixed = low_back(mixed)
    mixed_norm = low(normalize(mixed, mixed_gain, mixed_shift))
    attend_branch = low_back(jnp.dot(mixed_norm, output_weight, precision=highest) + output_bias)
    middle = unit_in + attend_branch
    middle_norm = low(normalize(middle, middle_gain, middle_shift))
    expanded = low_back(jnp.dot(middle_norm, expand_weight, precision=highest) + expand_bias)
    hidden_norm = low(normalize(jax.nn.gelu(expanded, approximate=False), hidden_gain, hidden_shift))
    shrunk = low_back(jnp.dot(hidden_norm, shrink_weight, precision=highest) + shrink_bias)
    return middle + shrunk

def forward_all(params, units_in, segments):
    checked = jax.checkpoint(unit_forward)

    def advance(carried, unit_pair):
        return (carried, checked(params, unit_pair[0], unit_pair[1]))
    _, outputs = lax.scan(advance, jnp.zeros((), jnp.float32), (units_in, segments))
    return outputs

def to_units(columns):
    block = 2 * UNIT // N_DP
    rows_major = jnp.transpose(columns).reshape(N_DP, ROWS, block, D)
    return jnp.transpose(rows_major, (1, 0, 2, 3)).reshape(MICRO * HOLDERS, UNIT, D)

def to_columns(units):
    block = 2 * UNIT // N_DP
    pieces = units.reshape(ROWS, N_DP, block, D)
    return jnp.transpose(jnp.transpose(pieces, (1, 0, 2, 3)).reshape(N_DP * ROWS * block, D))

def reference(tokens, cotangent, holder_of, lengths, input_gain, input_shift, attend_weight, attend_bias, mixed_gain, mixed_shift, output_weight, output_bias, middle_gain, middle_shift, expand_weight, expand_bias, hidden_gain, hidden_shift, shrink_weight, shrink_bias):
    units_in = to_units(tokens.astype(jnp.float32))
    units_cot = to_units(cotangent.astype(jnp.float32))
    chosen = jnp.broadcast_to(holder_of[:, :, None], (MICRO, HOLDERS, SEQS)).astype(jnp.int32)
    unit_lengths = jnp.take_along_axis(lengths, chosen, axis=1).reshape(MICRO * HOLDERS, SEQS)
    segments = jax.vmap(segment_ids)(unit_lengths)
    params = tuple((item_value.astype(jnp.float32) for item_value in (input_gain, input_shift, attend_weight, attend_bias, mixed_gain, mixed_shift, output_weight, output_bias, middle_gain, middle_shift, expand_weight, expand_bias, hidden_gain, hidden_shift, shrink_weight, shrink_bias)))

    def forward_fixed(weights_all, inputs_all):
        return forward_all(weights_all, inputs_all, segments)
    outputs, pullback = jax.vjp(forward_fixed, params, units_in)
    grads_params, grad_inputs = pullback(units_cot)
    g_in_gain, g_in_shift, g_attend_w, g_attend_b, g_mix_gain, g_mix_shift, g_out_w, g_out_b, g_mid_gain, g_mid_shift, g_exp_w, g_exp_b, g_hid_gain, g_hid_shift, g_shr_w, g_shr_b = grads_params
    block_out = to_columns(outputs).astype(jnp.bfloat16)
    input_grad = to_columns(grad_inputs).astype(jnp.bfloat16)
    return (block_out, input_grad, g_in_gain, g_in_shift, g_attend_w, g_attend_b, g_mix_gain, g_mix_shift, g_out_w, g_out_b, g_mid_gain, g_mid_shift, g_exp_w, g_exp_b, g_hid_gain, g_hid_shift, g_shr_w, g_shr_b)
```

```python
import math

import jax
import jax.numpy as jnp
from jax import lax
from jax.sharding import PartitionSpec as P

HEAD = 64
eps = 1e-05
masked_score = -1e30
f32 = jnp.float32
bf16 = jnp.bfloat16
RC = ("row", "col")


def mm(spec, a, b):
    return jnp.einsum(spec, a, b, preferred_element_type=f32)


def norm(v, gain, shift):
    mu = jnp.mean(v, axis=0, keepdims=True)
    d = v - mu
    r = lax.rsqrt(jnp.mean(d * d, axis=0, keepdims=True) + eps)
    vh = d * r
    return vh * gain + shift, vh, r


def norm_back(up, vh, r, gain):
    h = up * gain
    m1 = jnp.mean(h, axis=0, keepdims=True)
    m2 = jnp.mean(h * vh, axis=0, keepdims=True)
    return (
        r * (h - m1 - vh * m2),
        jnp.sum(up * vh, axis=1, keepdims=True),
        jnp.sum(up, axis=1, keepdims=True),
    )


def scores_of(q, k, visible):
    s = mm("hek,heq->hkq", k, q) * (1.0 / math.sqrt(HEAD))
    return jnp.where(visible[None], s, masked_score)


def body(
    tokens,
    cotangent,
    holder_of,
    lengths,
    input_gain,
    input_shift,
    attend_weight,
    attend_bias,
    mixed_gain,
    mixed_shift,
    output_weight,
    output_bias,
    middle_gain,
    middle_shift,
    expand_weight,
    expand_bias,
    hidden_gain,
    hidden_shift,
    shrink_weight,
    shrink_bias,
):
    holders = lax.axis_size("dp")
    half = holders // 2
    nr, nc = lax.axis_size("row"), lax.axis_size("col")
    n = nr * nc
    micro = holder_of.shape[0]
    assert micro == n
    fl = tokens.shape[0]
    pairs = micro * half
    blk = tokens.shape[1] // pairs
    unit = half * blk
    dp = lax.axis_index("dp")
    side, pos = dp // half, dp % half
    rc = lax.axis_index("row") * nc + lax.axis_index("col")
    groups = [[s * half + p for p in range(half)] for s in range(2)]

    def to_unit(v):
        v = v.reshape(fl, half, n, blk)
        v = jnp.transpose(v, (1, 2, 0, 3))
        v = lax.all_to_all(v, "dp", 0, 0, axis_index_groups=groups, tiled=True)
        v = jnp.transpose(v, (1, 2, 0, 3)).reshape(n, fl, unit)
        v = lax.all_to_all(v, RC, 0, 0, tiled=True)
        return v.reshape(n * fl, unit)

    def from_unit(v):
        v = lax.all_to_all(v.reshape(n, fl, unit), RC, 0, 0, tiled=True)
        v = jnp.transpose(v.reshape(n, fl, half, blk), (2, 0, 1, 3))
        v = lax.all_to_all(v, "dp", 0, 0, axis_index_groups=groups, tiled=True)
        return jnp.transpose(v, (2, 0, 1, 3)).reshape(tokens.shape)

    def gather(v):
        return lax.all_gather(v, RC, axis=0)

    ga = gather(attend_weight)
    go = gather(output_weight)
    ge = gather(expand_weight)
    gs = gather(shrink_weight)
    hw, rw, fw = output_weight.shape[0], output_weight.shape[1], shrink_weight.shape[0]

    thin = jnp.concatenate(
        [
            v.reshape(-1)
            for v in (
                input_gain, input_shift, output_bias, middle_gain, middle_shift, shrink_bias,
                attend_bias, mixed_gain, mixed_shift, expand_bias, hidden_gain, hidden_shift,
            )
        ]
    )
    thin = lax.all_gather(thin, RC, axis=0)
    sizes = [fl] * 6 + [hw] * 4 + [fw] * 3
    cols, at = [], 0
    for i, size in enumerate(sizes):
        piece = thin[:, at : at + size] if i < 6 else thin[:nc, at : at + size]
        cols.append(piece.reshape(-1, 1))
        at += size
    in_g, in_s, out_b, mid_g, mid_s, shr_b, q_b, v_b, mix_g, mix_s, exp_b, hid_g, hid_s = cols

    k_unit = 2 * (pos * n + rc) + side
    m_of, u_of = k_unit // holders, k_unit % holders
    own = lengths[m_of, holder_of[m_of, u_of]]
    bounds = jnp.cumsum(own)[:-1]
    at_row = jnp.arange(unit, dtype=jnp.int32)
    segment = jnp.sum((at_row[:, None] >= bounds[None, :]).astype(jnp.int32), axis=1)
    visible = segment[:, None] == segment[None, :]

    x = to_unit(tokens).astype(f32)
    e2 = to_unit(cotangent)

    a, vh_in, r_in = norm(x, in_g, in_s)
    a = a.astype(bf16)
    gar = ga.reshape(nr, nc, 3, hw, rw)
    trip = mm("rcjif,rft->jcit", gar, a.reshape(nr, rw, unit)).reshape(3, nc * hw, unit)
    heads = lambda v: v.reshape(-1, HEAD, unit)
    q = heads((trip[0] + q_b).astype(bf16))
    k = heads(trip[1].astype(bf16))
    v = heads((trip[2] + v_b).astype(bf16))
    s = scores_of(q, k, visible)
    top = jnp.max(s, axis=1, keepdims=True)
    ex = jnp.exp(s - top)
    den = jnp.sum(ex, axis=1, keepdims=True)
    prob = ex / den
    o = mm("hek,hkq->heq", v, prob.astype(bf16)).reshape(nc * hw, unit)
    on, vh_mix, r_mix = norm(o, mix_g, mix_s)
    on = on.astype(bf16)
    gor = go.reshape(nr, nc * hw, rw)
    x1 = x + mm("rin,it->rnt", gor, on).reshape(nr * rw, unit) + out_b
    b, vh_mid, r_mid = norm(x1, mid_g, mid_s)
    b = b.astype(bf16)
    ger = ge.reshape(nr, nc, rw, fw)
    f = mm("rckn,rkt->cnt", ger, b.reshape(nr, rw, unit)).reshape(nc * fw, unit) + exp_b
    phi = 0.5 * (1.0 + lax.erf(f * math.sqrt(0.5)))
    g = f * phi
    gn, vh_hid, r_hid = norm(g, hid_g, hid_s)
    gn = gn.astype(bf16)
    gsr = gs.reshape(nr, nc * fw, rw)
    y = x1 + mm("rfn,ft->rnt", gsr, gn).reshape(nr * rw, unit) + shr_b
    block_out = from_unit(y.astype(bf16))

    e2r = e2.reshape(nr, rw, unit)
    d_shr_w = mm("cft,rdt->rcfd", gn.reshape(nc, fw, unit), e2r).astype(bf16)
    dy = e2.astype(f32)
    d_shr_b = jnp.sum(dy, axis=1, keepdims=True)
    dgn = mm("rfd,rdt->ft", gsr, e2r)
    dg, d_hid_g, d_hid_s = norm_back(dgn, vh_hid, r_hid, hid_g)
    slope = phi + f * (jnp.exp(-0.5 * f * f) * (1.0 / math.sqrt(2.0 * math.pi)))
    df = (dg * slope).astype(bf16)
    d_exp_b = jnp.sum(df.astype(f32), axis=1, keepdims=True)
    dfc = df.reshape(nc, fw, unit)
    d_exp_w = mm("rkt,cnt->rckn", b.reshape(nr, rw, unit), dfc).astype(bf16)
    db = mm("rckn,cnt->rkt", ger, dfc).reshape(nr * rw, unit)
    dx1, d_mid_g, d_mid_s = norm_back(db, vh_mid, r_mid, mid_g)
    dx1 = dy + dx1
    e1 = dx1.astype(bf16)
    d_out_b = jnp.sum(e1.astype(f32), axis=1, keepdims=True)
    e1r = e1.reshape(nr, rw, unit)
    d_out_w = mm("cit,rnt->rcin", on.reshape(nc, hw, unit), e1r).astype(bf16)
    don = mm("rin,rnt->it", gor, e1r)
    do, d_mix_g, d_mix_s = norm_back(don, vh_mix, r_mix, mix_g)
    do = heads(do.astype(bf16))
    dprob = mm("hek,heq->hkq", v, do)
    inner = jnp.sum(prob * dprob, axis=1, keepdims=True)
    ds = (prob * (dprob - inner)).astype(bf16)
    scale = 1.0 / math.sqrt(HEAD)
    dq = (mm("hek,hkq->heq", k, ds) * scale).astype(bf16).reshape(nc, hw, unit)
    dk = (mm("heq,hkq->hek", q, ds) * scale).astype(bf16).reshape(nc, hw, unit)
    dv = mm("heq,hkq->hek", do, prob.astype(bf16)).astype(bf16).reshape(nc, hw, unit)
    d_q_b = jnp.sum(dq.astype(f32), axis=2)
    d_v_b = jnp.sum(dv.astype(f32), axis=2)
    dtrip = jnp.stack([dq, dk, dv], axis=1)
    d_att_w = mm("cjit,rft->rcjif", dtrip, a.reshape(nr, rw, unit)).astype(bf16)
    da = mm("rcjif,cjit->rft", gar, dtrip).reshape(nr * rw, unit)
    dx, d_in_g, d_in_s = norm_back(da, vh_in, r_in, in_g)
    input_grad = from_unit((dx1 + dx).astype(bf16))

    def reduce(v):
        v = v.reshape((n,) + v.shape[2:])
        return lax.psum(lax.psum_scatter(v, RC, scatter_dimension=0, tiled=False), "dp")

    shr_w_g = reduce(d_shr_w).astype(f32)
    exp_w_g = reduce(d_exp_w).astype(f32)
    out_w_g = reduce(d_out_w).astype(f32)

    by_rc = [v.reshape(n, fl) for v in (d_in_g, d_in_s, d_out_b, d_mid_g, d_mid_s, d_shr_b)]
    by_c = [
        jnp.broadcast_to(v.reshape(1, nc, -1), (nr, nc, v.size // nc)).reshape(n, -1)
        for v in (d_q_b, d_v_b, d_mix_g, d_mix_s, d_exp_b, d_hid_g, d_hid_s)
    ]
    small = jnp.concatenate(by_rc + by_c, axis=1).astype(bf16)
    width = small.shape[1]
    pad = -width % rw
    small = jnp.pad(small, ((0, 0), (0, pad))).reshape(nr, nc, -1, rw)
    last = jnp.concatenate([d_att_w.reshape(nr, nc, 3 * hw, rw), small], axis=2)
    last = reduce(last).astype(f32)
    att_w_g = last[: 3 * hw].reshape(attend_weight.shape)
    flat = last[3 * hw :].reshape(-1)
    outs, at = [], 0
    for size in sizes:
        outs.append(flat[at : at + size])
        at += size
    in_g_g, in_s_g, out_b_g, mid_g_g, mid_s_g, shr_b_g, q_b_g, v_b_g, mix_g_g, mix_s_g, exp_b_g, hid_g_g, hid_s_g = outs
    return (
        block_out,
        input_grad,
        in_g_g,
        in_s_g,
        att_w_g,
        jnp.stack([q_b_g, v_b_g]),
        mix_g_g,
        mix_s_g,
        out_w_g,
        out_b_g,
        mid_g_g,
        mid_s_g,
        exp_w_g,
        exp_b_g,
        hid_g_g,
        hid_s_g,
        shr_w_g,
        shr_b_g,
    )


def solution(mesh):
    wide, narrow = P(RC), P("col")
    in_specs = (
        P(RC, "dp"), P(RC, "dp"), P(), P(), wide, wide, P(None, "col", "row"), P(None, "col"),
        narrow, narrow, P("col", "row"), wide, wide, wide, P("row", "col"), narrow, narrow, narrow,
        P("col", "row"), wide,
    )
    out_specs = (
        P(RC, "dp"), P(RC, "dp"), wide, wide, P(None, "col", "row"), P(None, "col"), narrow, narrow,
        P("col", "row"), wide, wide, wide, P("row", "col"), narrow, narrow, narrow, P("col", "row"),
        wide,
    )
    return jax.shard_map(body, mesh=mesh, in_specs=in_specs, out_specs=out_specs, check_vma=False)
```

```python
import math

import jax
import jax.numpy as jnp
from jax import lax
from jax.sharding import PartitionSpec as P

HEAD = 64
eps = 1e-05
masked_score = -1e30
f32 = jnp.float32
bf16 = jnp.bfloat16
RC = ("row", "col")


def mm(spec, a, b):
    return jnp.einsum(spec, a, b, preferred_element_type=f32)


def norm(v, gain, shift):
    mu = jnp.mean(v, axis=0, keepdims=True)
    d = v - mu
    r = lax.rsqrt(jnp.mean(d * d, axis=0, keepdims=True) + eps)
    vh = d * r
    return vh * gain + shift, vh, r


def norm_back(up, vh, r, gain):
    h = up * gain
    m1 = jnp.mean(h, axis=0, keepdims=True)
    m2 = jnp.mean(h * vh, axis=0, keepdims=True)
    return (
        r * (h - m1 - vh * m2),
        jnp.sum(up * vh, axis=1, keepdims=True),
        jnp.sum(up, axis=1, keepdims=True),
    )


def scores_of(q, k, visible):
    s = mm("hek,heq->hkq", k, q) * (1.0 / math.sqrt(HEAD))
    return jnp.where(visible[None], s, masked_score)


def body(
    tokens,
    cotangent,
    holder_of,
    lengths,
    input_gain,
    input_shift,
    attend_weight,
    attend_bias,
    mixed_gain,
    mixed_shift,
    output_weight,
    output_bias,
    middle_gain,
    middle_shift,
    expand_weight,
    expand_bias,
    hidden_gain,
    hidden_shift,
    shrink_weight,
    shrink_bias,
):
    holders = lax.axis_size("dp")
    half = holders // 2
    nr, nc = lax.axis_size("row"), lax.axis_size("col")
    n = nr * nc
    micro = holder_of.shape[0]
    assert micro == n
    fl = tokens.shape[0]
    pairs = micro * half
    blk = tokens.shape[1] // pairs
    unit = half * blk
    dp = lax.axis_index("dp")
    side, pos = dp // half, dp % half
    rc = lax.axis_index("row") * nc + lax.axis_index("col")
    groups = [[s * half + p for p in range(half)] for s in range(2)]

    def to_unit(v):
        v = v.reshape(fl, half, n, blk)
        v = jnp.transpose(v, (1, 2, 0, 3))
        v = lax.all_to_all(v, "dp", 0, 0, axis_index_groups=groups, tiled=True)
        v = jnp.transpose(v, (1, 2, 0, 3)).reshape(n, fl, unit)
        v = lax.all_to_all(v, RC, 0, 0, tiled=True)
        return v.reshape(n * fl, unit)

    def from_unit(v):
        v = lax.all_to_all(v.reshape(n, fl, unit), RC, 0, 0, tiled=True)
        v = jnp.transpose(v.reshape(n, fl, half, blk), (2, 0, 1, 3))
        v = lax.all_to_all(v, "dp", 0, 0, axis_index_groups=groups, tiled=True)
        return jnp.transpose(v, (2, 0, 1, 3)).reshape(tokens.shape)

    def flip_row(v):
        return lax.ppermute(v, "row", [(i, i ^ 1) for i in range(nr)])

    def flip_chip(v):
        return lax.ppermute(v, "col", [(i, i ^ 2) for i in range(nc)])

    def flip_core(v):
        return lax.ppermute(v, "col", [(i, i ^ 1) for i in range(nc)])

    def gather(v):
        h = v.shape[0] // 2
        by_row, by_chip = flip_row(v), flip_chip(v)
        far0, far1 = flip_row(by_chip[:h]), flip_chip(by_row[h:])
        own = [v, by_chip, by_row, far0, far1]
        other = [flip_core(p) for p in own]
        v1, c1, r1, f1, g1 = other
        return jnp.concatenate([v, v1, by_chip, c1, by_row, r1, far0, far1, f1, g1], axis=0).reshape((n,) + v.shape)

    hw, rw, fw = output_weight.shape[0], output_weight.shape[1], shrink_weight.shape[0]
    gao = gather(jnp.concatenate([attend_weight.reshape(3 * hw, rw), output_weight], axis=0))
    ga, go = gao[:, : 3 * hw], gao[:, 3 * hw :]
    ge = gather(expand_weight)
    gs = gather(shrink_weight)

    thin = jnp.concatenate(
        [
            v.reshape(-1)
            for v in (
                input_gain, input_shift, output_bias, middle_gain, middle_shift, shrink_bias,
                attend_bias, mixed_gain, mixed_shift, expand_bias, hidden_gain, hidden_shift,
            )
        ]
    )
    thin = thin[None]
    for flip in (flip_core, flip_chip, flip_row):
        thin = jnp.concatenate([thin, flip(thin)], axis=0)
    flat_order = jnp.arange(n) ^ rc
    sizes = [fl] * 6 + [hw] * 4 + [fw] * 3
    cols, at = [], 0
    for i, size in enumerate(sizes):
        piece = thin[flat_order, at : at + size] if i < 6 else thin[:nc, at : at + size]
        cols.append(piece.reshape(-1, 1))
        at += size
    in_g, in_s, out_b, mid_g, mid_s, shr_b, q_b, v_b, mix_g, mix_s, exp_b, hid_g, hid_s = cols

    k_unit = 2 * (pos * n + rc) + side
    m_of, u_of = k_unit // holders, k_unit % holders
    own = lengths[m_of, holder_of[m_of, u_of]]
    bounds = jnp.cumsum(own)[:-1]
    at_row = jnp.arange(unit, dtype=jnp.int32)
    segment = jnp.sum((at_row[:, None] >= bounds[None, :]).astype(jnp.int32), axis=1)
    visible = segment[:, None] == segment[None, :]

    x = to_unit(tokens).astype(f32)
    e2 = to_unit(cotangent)

    a, vh_in, r_in = norm(x, in_g, in_s)
    a = a.astype(bf16)
    my_row = lax.axis_index("row")

    def by_row_rel(v):
        v = v.reshape(nr, rw, unit)
        return jnp.where(my_row == 0, v, v[::-1])

    def by_row_abs(v):
        return jnp.where(my_row == 0, v, v[::-1]).reshape(nr * rw, unit)

    a_rel = by_row_rel(a)
    gar = ga.reshape(nr, nc, 3, hw, rw)
    trip = mm("rcjif,rft->jcit", gar, a_rel).reshape(3, nc * hw, unit)
    heads = lambda v: v.reshape(-1, HEAD, unit)
    q = heads((trip[0] + q_b).astype(bf16))
    k = heads(trip[1].astype(bf16))
    v = heads((trip[2] + v_b).astype(bf16))
    s = scores_of(q, k, visible)
    top = jnp.max(s, axis=1, keepdims=True)
    ex = jnp.exp(s - top)
    den = jnp.sum(ex, axis=1, keepdims=True)
    prob = ex / den
    o = mm("hek,hkq->heq", v, prob.astype(bf16)).reshape(nc * hw, unit)
    on, vh_mix, r_mix = norm(o, mix_g, mix_s)
    on = on.astype(bf16)
    gor = go.reshape(nr, nc * hw, rw)
    x1 = x + by_row_abs(mm("rin,it->rnt", gor, on)) + out_b
    b, vh_mid, r_mid = norm(x1, mid_g, mid_s)
    b = b.astype(bf16)
    ger = ge.reshape(nr, nc, rw, fw)
    b_rel = by_row_rel(b)
    f = mm("rckn,rkt->cnt", ger, b_rel).reshape(nc * fw, unit) + exp_b
    phi = 0.5 * (1.0 + lax.erf(f * math.sqrt(0.5)))
    g = f * phi
    gn, vh_hid, r_hid = norm(g, hid_g, hid_s)
    gn = gn.astype(bf16)
    gsr = gs.reshape(nr, nc * fw, rw)
    y = x1 + by_row_abs(mm("rfn,ft->rnt", gsr, gn)) + shr_b
    block_out = from_unit(y.astype(bf16))

    e2r = by_row_rel(e2)
    d_shr_w = mm("cft,rdt->rcfd", gn.reshape(nc, fw, unit), e2r).astype(bf16)
    dy = e2.astype(f32)
    d_shr_b = jnp.sum(dy, axis=1, keepdims=True)
    dgn = mm("rfd,rdt->ft", gsr, e2r)
    dg, d_hid_g, d_hid_s = norm_back(dgn, vh_hid, r_hid, hid_g)
    slope = phi + f * (jnp.exp(-0.5 * f * f) * (1.0 / math.sqrt(2.0 * math.pi)))
    df = (dg * slope).astype(bf16)
    d_exp_b = jnp.sum(df.astype(f32), axis=1, keepdims=True)
    dfc = df.reshape(nc, fw, unit)
    d_exp_w = mm("rkt,cnt->rckn", b_rel, dfc).astype(bf16)
    db = by_row_abs(mm("rckn,cnt->rkt", ger, dfc))
    dx1, d_mid_g, d_mid_s = norm_back(db, vh_mid, r_mid, mid_g)
    dx1 = dy + dx1
    e1 = dx1.astype(bf16)
    d_out_b = jnp.sum(e1.astype(f32), axis=1, keepdims=True)
    e1r = by_row_rel(e1)
    d_out_w = mm("cit,rnt->rcin", on.reshape(nc, hw, unit), e1r).astype(bf16)
    don = mm("rin,rnt->it", gor, e1r)
    do, d_mix_g, d_mix_s = norm_back(don, vh_mix, r_mix, mix_g)
    do = heads(do.astype(bf16))
    dprob = mm("hek,heq->hkq", v, do)
    inner = jnp.sum(prob * dprob, axis=1, keepdims=True)
    ds = (prob * (dprob - inner)).astype(bf16)
    scale = 1.0 / math.sqrt(HEAD)
    dq = (mm("hek,hkq->heq", k, ds) * scale).astype(bf16).reshape(nc, hw, unit)
    dk = (mm("heq,hkq->hek", q, ds) * scale).astype(bf16).reshape(nc, hw, unit)
    dv = mm("heq,hkq->hek", do, prob.astype(bf16)).astype(bf16).reshape(nc, hw, unit)
    d_q_b = jnp.sum(dq.astype(f32), axis=2)
    d_v_b = jnp.sum(dv.astype(f32), axis=2)
    dtrip = jnp.stack([dq, dk, dv], axis=1)
    d_att_w = mm("cjit,rft->rcjif", dtrip, a_rel).astype(bf16)
    da = by_row_abs(mm("rcjif,cjit->rft", gar, dtrip))
    dx, d_in_g, d_in_s = norm_back(da, vh_in, r_in, in_g)
    input_grad = from_unit((dx1 + dx).astype(bf16))

    def reduce(v):
        v = v.reshape((nr, nc // 2, 2) + v.shape[2:])
        v = v[:, :, 0] + flip_core(v[:, :, 1])
        h = v.shape[2] // 2
        p, q = v[:, :, :h], v[:, :, h:]
        p = p[0] + flip_row(p[1])
        q = q[:, 0] + flip_chip(q[:, 1])
        p = p[0] + flip_chip(p[1])
        q = q[0] + flip_row(q[1])
        v = jnp.concatenate([p, q], axis=0)
        step = 1
        while step < holders:
            v = v + lax.ppermute(v, "dp", [(i, i ^ step) for i in range(holders)])
            step *= 2
        return v

    shr_w_g = reduce(d_shr_w).astype(f32)
    exp_w_g = reduce(d_exp_w).astype(f32)

    by_rc = [v.reshape(n, fl)[flat_order] for v in (d_in_g, d_in_s, d_out_b, d_mid_g, d_mid_s, d_shr_b)]
    by_c = [
        jnp.broadcast_to(v.reshape(1, nc, -1), (nr, nc, v.size // nc)).reshape(n, -1)
        for v in (d_q_b, d_v_b, d_mix_g, d_mix_s, d_exp_b, d_hid_g, d_hid_s)
    ]
    small = jnp.concatenate(by_rc + by_c, axis=1).astype(bf16)
    width = small.shape[1]
    pad = -width % (2 * rw)
    small = jnp.pad(small, ((0, 0), (0, pad))).reshape(nr, nc, -1, rw)
    last = jnp.concatenate([d_att_w.reshape(nr, nc, 3 * hw, rw), d_out_w, small], axis=2)
    last = reduce(last).astype(f32)
    out_w_g = last[3 * hw : 4 * hw]
    att_w_g = last[: 3 * hw].reshape(attend_weight.shape)
    flat = last[4 * hw :].reshape(-1)
    outs, at = [], 0
    for size in sizes:
        outs.append(flat[at : at + size])
        at += size
    in_g_g, in_s_g, out_b_g, mid_g_g, mid_s_g, shr_b_g, q_b_g, v_b_g, mix_g_g, mix_s_g, exp_b_g, hid_g_g, hid_s_g = outs
    return (
        block_out,
        input_grad,
        in_g_g,
        in_s_g,
        att_w_g,
        jnp.stack([q_b_g, v_b_g]),
        mix_g_g,
        mix_s_g,
        out_w_g,
        out_b_g,
        mid_g_g,
        mid_s_g,
        exp_w_g,
        exp_b_g,
        hid_g_g,
        hid_s_g,
        shr_w_g,
        shr_b_g,
    )


def solution(mesh):
    wide, narrow = P(RC), P("col")
    in_specs = (
        P(RC, "dp"), P(RC, "dp"), P(), P(), wide, wide, P(None, "col", "row"), P(None, "col"),
        narrow, narrow, P("col", "row"), wide, wide, wide, P("row", "col"), narrow, narrow, narrow,
        P("col", "row"), wide,
    )
    out_specs = (
        P(RC, "dp"), P(RC, "dp"), wide, wide, P(None, "col", "row"), P(None, "col"), narrow, narrow,
        P("col", "row"), wide, wide, wide, P("row", "col"), narrow, narrow, narrow, P("col", "row"),
        wide,
    )
    return jax.shard_map(body, mesh=mesh, in_specs=in_specs, out_specs=out_specs, check_vma=False)
```

```python
import functools
import math

import jax
import jax.numpy as jnp
from jax import lax
from jax.experimental import pallas as pl
from jax.experimental.pallas import tpu as pltpu
from jax.sharding import PartitionSpec as P

HEAD = 64
eps = 1e-05
masked_score = -1e30
f32 = jnp.float32
bf16 = jnp.bfloat16
RC = ("row", "col")
HBM = pl.BlockSpec(memory_space=pltpu.HBM)
SMEM = pl.BlockSpec(memory_space=pltpu.SMEM)
VMEM = pl.BlockSpec(memory_space=pltpu.VMEM)
root_half = math.sqrt(0.5)
root_tau = 1.0 / math.sqrt(2.0 * math.pi)
score_scale = 1.0 / math.sqrt(HEAD)


def dot(a, b, ca, cb):
    return lax.dot_general(a, b, (((ca,), (cb,)), ((), ())), preferred_element_type=f32)


def up(v):
    return v.astype(f32)


def moments(v):
    mu = jnp.mean(v, axis=0, keepdims=True)
    d = v - mu
    return mu, lax.rsqrt(jnp.mean(d * d, axis=0, keepdims=True) + eps)


def norm(v, gain, shift):
    mu, r = moments(v)
    return (v - mu) * r * gain + shift


def lane_sum(v):
    return jnp.sum(v, axis=1, keepdims=True)


def norm_back(grad, v, gain):
    mu, r = moments(v)
    vh = (v - mu) * r
    h = grad * gain
    m1 = jnp.mean(h, axis=0, keepdims=True)
    m2 = jnp.mean(h * vh, axis=0, keepdims=True)
    return r * (h - m1 - vh * m2), lane_sum(grad * vh), lane_sum(grad)


def put_columns(ref, columns):
    lane = lax.broadcasted_iota(jnp.int32, ref.shape, len(ref.shape) - 1)
    out = jnp.zeros(ref.shape, f32)
    for i, column in enumerate(columns):
        out = jnp.where(lane == i, column, out)
    ref[...] = out


PIECES = ((0, None), (1, None), (2, None), (3, None), (4, None), (5, None), (6, 0), (6, 1), (7, 0), (7, 1))


def fetch(pieces, rows, parts):
    for ref, (block, half) in zip(pieces, PIECES):
        first, last = (0, rows) if half is None else (half * rows // 2, (half + 1) * rows // 2)
        for lo, hi, place, sem in parts:
            a, b = max(lo, first), min(hi, last)
            if a < b:
                pltpu.make_async_copy(
                    ref.at[pl.ds(a - first, b - a)], place(block).at[pl.ds(a - lo, b - a)], sem.at[block]
                ).start()


def arrive(ref, sem):
    pltpu.make_async_copy(ref, ref, sem).wait()


def move(src, dst, sem):
    copy = pltpu.make_async_copy(src, dst, sem)
    copy.start()
    return copy


def call(kernel, outs, in_specs, out_specs, scratch=(), flops=0, moved=0, name=None):
    return pl.pallas_call(
        kernel,
        out_shape=outs,
        in_specs=in_specs,
        out_specs=out_specs,
        scratch_shapes=list(scratch),
        compiler_params=pltpu.CompilerParams(vmem_limit_bytes=52 * 2**20),
        cost_estimate=pl.CostEstimate(flops=flops, bytes_accessed=moved, transcendentals=0),
        name=name,
    )


def sds(shape, dtype):
    return jax.ShapeDtypeStruct(shape, dtype)


def segment_rows(info, unit):
    t = lax.broadcasted_iota(jnp.int32, (16, unit), 1)
    slot = lax.broadcasted_iota(jnp.int32, (16, unit), 0)
    one = lambda b: jnp.where(t >= b, 1, 0)
    seg = one(info[2]) + one(info[3]) + one(info[4])
    same = seg == slot
    for_keys = jnp.where(same, 1.0, 0.0)
    for_queries = jnp.where(jnp.logical_and(slot < 4, jnp.logical_not(same)), masked_score, 0.0)
    return for_keys, for_queries


def split3(v):
    hi = v.astype(bf16)
    v = v - up(hi)
    mid = v.astype(bf16)
    return hi, mid, (v - up(mid)).astype(bf16)


def three_rows(base, v, first):
    row = lax.broadcasted_iota(jnp.int32, base.shape, 0)
    for i, part in enumerate(split3(v)):
        base = jnp.where(row == first + i, up(part), base)
    return base


def join(ref):
    return jnp.concatenate([ref[i] for i in range(ref.shape[0])], axis=1)


def apart(ref, value):
    width = ref.shape[2]
    for i in range(ref.shape[0]):
        ref[i] = value[:, i * width : (i + 1) * width]


def attend_kernel(nc, hw, rw, fl, fw, info, xs_ref, even, odd, *refs):
    pieces = refs[:10]
    a_out, qkv_out, lse_out, o_ref, pd, pf = refs[10:16]
    a_ref, qkv_ref, lse_ref, ga, ka, qa, ga_sem, out_sem = refs[16:]
    unit = o_ref.shape[1]
    fetch(pieces, 4 * hw, ((0, 3 * hw, lambda i: ga.at[i], ga_sem),))
    for i in range(2 * nc):
        tile = (even, odd)[i % 2][i // 2]
        pd[pl.ds(pl.multiple_of(jnp.bitwise_xor(info[0], i) * fl, fl), fl), 0:6] = tile[:, 0:6]
        if i < nc:
            for k in range(hw // fl):
                pd[i * hw + k * fl : i * hw + (k + 1) * fl, 6:10] = tile[:, 6 + 4 * k : 10 + 4 * k]
            for k in range(fw // fl):
                first = 6 + 4 * (hw // fl) + 3 * k
                pf[i, k * fl : (k + 1) * fl, 0:3] = tile[:, first : first + 3]
    a_ref[...] = norm(up(join(xs_ref)), pd[:, 0:1], pd[:, 1:2]).astype(bf16)
    for_keys, for_queries = segment_rows(info, unit)
    ka[HEAD:, :] = for_keys.astype(bf16)
    qa[HEAD:, :] = for_queries.astype(bf16)
    my_row = info[1]
    outs = [move(a_ref, a_out, out_sem.at[0])]

    def per_block(c, carry):
        arrive(ga.at[c], ga_sem.at[c])
        arrive(ga.at[nc + c], ga_sem.at[nc + c])
        trip = dot(ga[my_row * nc + c], a_ref[0:rw, :], 1, 0) + dot(ga[(1 - my_row) * nc + c], a_ref[rw:, :], 1, 0)
        at = pl.multiple_of(c * hw, hw)
        qkv_ref[c, 0:hw, :] = (trip[0:hw] + pd[pl.ds(at, hw), 6:7]).astype(bf16)
        qkv_ref[c, hw : 2 * hw, :] = trip[hw : 2 * hw].astype(bf16)
        qkv_ref[c, 2 * hw :, :] = (trip[2 * hw :] + pd[pl.ds(at, hw), 7:8]).astype(bf16)
        for h in range(hw // HEAD):
            qa[0:HEAD, :] = qkv_ref[c, h * HEAD : (h + 1) * HEAD, :] * jnp.bfloat16(score_scale)
            ka[0:HEAD, :] = qkv_ref[c, hw + h * HEAD : hw + (h + 1) * HEAD, :]
            v = qkv_ref[c, 2 * hw + h * HEAD : 2 * hw + (h + 1) * HEAD, :]
            s = dot(ka[...], qa[...], 0, 0)
            top = jnp.max(s, axis=0, keepdims=True)
            e = jnp.exp(s - top)
            den = jnp.sum(e, axis=0, keepdims=True)
            o = dot(v, e.astype(bf16), 1, 0) * (1.0 / den)
            o_ref[pl.ds(pl.multiple_of(c * hw + h * HEAD, HEAD), HEAD), :] = o
            lse_ref[c, h : h + 1, :] = top + jnp.log(den)
        return carry

    lax.fori_loop(0, nc, per_block, 0)
    outs += [move(qkv_ref, qkv_out, out_sem.at[1]), move(lse_ref, lse_out, out_sem.at[2])]
    for copy in outs:
        copy.wait()


def output_kernel(nc, hw, rw, info, xs_ref, o_ref, pd, *refs):
    pieces = refs[:10]
    on_ref, x1_ref, b_ref, go, go_sem = refs[10:]
    fetch(pieces, 4 * hw, ((3 * hw, 4 * hw, lambda i: go.at[i // nc, pl.ds(i % nc * hw, hw)], go_sem),))
    my_row = info[1]
    on_ref[...] = norm(o_ref[...], pd[:, 8:9], pd[:, 9:10]).astype(bf16)
    on = on_ref[...]
    for i in range(2 * nc):
        arrive(go.at[i // nc, pl.ds(i % nc * hw, hw)], go_sem.at[i])
    for r in range(2):
        part = dot(go[jnp.bitwise_xor(my_row, r)], on, 0, 0)
        rows = slice(r * rw, (r + 1) * rw)
        x1_ref[rows, :] = up(join(xs_ref.at[:, rows, :])) + part + pd[rows, 2:3]
    b_ref[...] = norm(x1_ref[...], pd[:, 3:4], pd[:, 4:5]).astype(bf16)


def expand_kernel(nc, rw, fw, info, b_ref, pf, *refs):
    pieces = refs[:10]
    gn_ref, vh_out, slope_out, st_ref = refs[10:14]
    vh_ref, slope_ref, g_ref, ge, ge_sem, out_sem = refs[14:]
    fetch(pieces, rw, ((0, rw, lambda i: ge.at[i], ge_sem),))
    my_row = info[1]
    unit = b_ref.shape[2]
    total = nc * fw

    def first(c, s):
        arrive(ge.at[c], ge_sem.at[c])
        arrive(ge.at[nc + c], ge_sem.at[nc + c])
        f = dot(ge[my_row * nc + c], b_ref[0], 0, 0) + dot(ge[(1 - my_row) * nc + c], b_ref[1], 0, 0)
        f = f + pf[c, :, 0:1]
        phi = 0.5 * (1.0 + lax.erf(f * root_half))
        g = f * phi
        g_ref[c] = g
        slope_ref[c] = (phi + f * (jnp.exp(-0.5 * f * f) * root_tau)).astype(bf16)
        move(slope_ref.at[c], slope_out.at[c], out_sem.at[c])
        return s + jnp.sum(g, axis=0, keepdims=True)

    mu = lax.fori_loop(0, nc, first, jnp.zeros((1, unit), f32)) * (1.0 / total)

    def second(c, s):
        d = g_ref[c] - mu
        return s + jnp.sum(d * d, axis=0, keepdims=True)

    r = lax.rsqrt(lax.fori_loop(0, nc, second, jnp.zeros((1, unit), f32)) * (1.0 / total) + eps)
    st_ref[...] = jnp.broadcast_to(r, st_ref.shape)

    def third(c, carry):
        vh = (g_ref[c] - mu) * r
        vh_ref[c] = vh.astype(bf16)
        gn_ref[c] = (vh * pf[c, :, 1:2] + pf[c, :, 2:3]).astype(bf16)
        move(vh_ref.at[c], vh_out.at[c], out_sem.at[nc + c])
        return carry

    lax.fori_loop(0, nc, third, 0)
    for c in range(nc):
        arrive(slope_ref.at[c], out_sem.at[c])
        arrive(vh_ref.at[c], out_sem.at[nc + c])


def store_blocks(nc, block, keep_ref, send_ref, keep_out, send_out, sem):
    def one(j, carry):
        row, chip = j // (nc // 2), j % (nc // 2)
        block(row, 2 * chip + 1, send_ref.at[row, chip])
        move(send_ref.at[row, chip], send_out.at[row, chip], sem.at[nc + j])
        block(row, 2 * chip, keep_ref.at[row, chip])
        move(keep_ref.at[row, chip], keep_out.at[row, chip], sem.at[j])
        return carry

    lax.fori_loop(0, nc, one, 0)


def stored_blocks(nc, keep_ref, send_ref, sem):
    for c in range(nc):
        arrive(keep_ref.at[c // 2, c % 2], sem.at[c])
        arrive(send_ref.at[c // 2, c % 2], sem.at[nc + c])


def shrink_grads_kernel(nc, rw, info, gn_ref, e2s_ref, e2_ref, keep_out, send_out, keep_ref, send_ref, out_sem):
    my_row = info[1]
    for i in range(2):
        e2_ref[i] = join(e2s_ref.at[:, pl.ds(i * rw, rw), :])

    def block(row, c, ref):
        ref[...] = dot(gn_ref[c], e2_ref[jnp.bitwise_xor(row, my_row)], 1, 1).astype(bf16)

    store_blocks(nc, block, keep_ref, send_ref, keep_out, send_out, out_sem)
    stored_blocks(nc, keep_ref, send_ref, out_sem)


def start_add(left, right, left_ref, right_ref, sem):
    for j in range(4):
        move(left.at[j // 2, j % 2], left_ref.at[j // 2, j % 2], sem.at[2 * j])
        move(right.at[j // 2, j % 2], right_ref.at[j // 2, j % 2], sem.at[2 * j + 1])


def finish_add(outs, left_ref, right_ref, sem, out_sem):
    copies = []
    h = left_ref.shape[2] // 2
    for k, j in enumerate((3, 2, 1, 0)):
        r, c = j // 2, j % 2
        arrive(left_ref.at[r, c], sem.at[2 * j])
        arrive(right_ref.at[r, c], sem.at[2 * j + 1])
        left_ref[r, c] = (up(left_ref[r, c]) + up(right_ref[r, c])).astype(bf16)
        copies.append(move(left_ref.at[r, c, pl.ds(0, h)], outs[r].at[c], out_sem.at[2 * k]))
        copies.append(move(left_ref.at[r, c, pl.ds(h, h)], outs[2 + c].at[r], out_sem.at[2 * k + 1]))
    for copy in copies:
        copy.wait()


def hidden_back_kernel(nc, fw, info, st_ref, e2_ref, pf, vh_in, slope_in, *refs):
    pieces = refs[:10]
    df_ref, gf_ref, vh_ref, slope_ref, gs, dgn, gs_sem, vh_sem, slope_sem = refs[10:]
    fetch(pieces, fw, ((0, fw, lambda i: gs.at[i], gs_sem),))
    for c in range(nc):
        move(vh_in.at[c], vh_ref.at[c], vh_sem.at[c])
    for c in range(nc):
        move(slope_in.at[c], slope_ref.at[c], slope_sem.at[c])
    my_row = info[1]
    r = st_ref[0:1, :]
    unit = e2_ref.shape[2]
    total = nc * fw

    def first(c, s):
        arrive(gs.at[c], gs_sem.at[c])
        arrive(gs.at[nc + c], gs_sem.at[nc + c])
        arrive(vh_ref.at[c], vh_sem.at[c])
        d = dot(gs[my_row * nc + c], e2_ref[0], 1, 0) + dot(gs[(1 - my_row) * nc + c], e2_ref[1], 1, 0)
        dgn[c] = d
        dv = d * up(vh_ref[c])
        gf_ref[c, :, 0:1] = lane_sum(dv)
        gf_ref[c, :, 1:2] = lane_sum(d)
        gain = pf[c, :, 1:2]
        return s[0] + jnp.sum(d * gain, axis=0, keepdims=True), s[1] + jnp.sum(dv * gain, axis=0, keepdims=True)

    zero = jnp.zeros((1, unit), f32)
    m1, m2 = lax.fori_loop(0, nc, first, (zero, zero))
    m1, m2 = m1 * (1.0 / total), m2 * (1.0 / total)

    def second(c, carry):
        arrive(slope_ref.at[c], slope_sem.at[c])
        dg = r * (dgn[c] * pf[c, :, 1:2] - m1 - up(vh_ref[c]) * m2)
        df = (dg * up(slope_ref[c])).astype(bf16)
        df_ref[c] = df
        gf_ref[c, :, 2:3] = lane_sum(up(df))
        return carry

    lax.fori_loop(0, nc, second, 0)


def middle_back_kernel(nc, rw, fw, info, df_ref, x1_ref, e2_ref, pd, *refs):
    pieces = refs[:10]
    dx1_ref, e1_ref, gd_ref, ge, db, ge_sem = refs[10:]
    fetch(pieces, rw, ((0, rw, lambda i: ge.at[i], ge_sem),))
    my_row = info[1]
    for i in range(2 * nc):
        arrive(ge.at[i], ge_sem.at[i])
    for r in range(2):
        start = jnp.bitwise_xor(my_row, r) * nc
        part = dot(ge[start], df_ref[0], 1, 0)
        for c in range(1, nc):
            part = part + dot(ge[start + c], df_ref[c], 1, 0)
        db[r * rw : (r + 1) * rw, :] = part
    dx, gain, shift = norm_back(db[...], x1_ref[...], pd[:, 3:4])
    for r in range(2):
        rows = slice(r * rw, (r + 1) * rw)
        dy = up(e2_ref[r])
        dx1 = dy + dx[rows]
        dx1_ref[rows, :] = dx1
        e1 = dx1.astype(bf16)
        e1_ref[r] = e1
        put_columns(gd_ref.at[rows], (gain[rows], shift[rows], lane_sum(up(e1)), lane_sum(dy)))


def middle_grads_kernel(
    nc, hw, rw, fw, info, b_ref, df_ref, on_ref, e1_ref, left, right, keep_out, send_out, p0, p1, q0, q1,
    keep_ref, send_ref, left_ref, right_ref, add_in, add_out, out_sem,
):
    my_row = info[1]
    start_add(left, right, left_ref, right_ref, add_in)

    def block(row, c, ref):
        r = jnp.bitwise_xor(row, my_row)
        half = fw // 2
        for k in range(2):
            ref[k * rw : (k + 1) * rw, :] = dot(b_ref[r], df_ref[c, k * half : (k + 1) * half, :], 1, 1).astype(bf16)
        ref[2 * rw :, :] = dot(on_ref[c], e1_ref[r], 1, 1).astype(bf16)

    store_blocks(nc, block, keep_ref, send_ref, keep_out, send_out, out_sem)
    finish_add((p0, p1, q0, q1), left_ref, right_ref, add_in, add_out)
    stored_blocks(nc, keep_ref, send_ref, out_sem)


def mixed_back(nc, hw, info, e1_ref, o_ref, pd, go, go_sem, do_ref, gd_ref):
    my_row = info[1]
    for i in range(2 * nc):
        arrive(go.at[i // nc, pl.ds(i % nc * hw, hw)], go_sem.at[i])
    don = dot(go[my_row], e1_ref[0], 1, 0) + dot(go[1 - my_row], e1_ref[1], 1, 0)
    do, gain, shift = norm_back(don, o_ref[...], pd[:, 8:9])
    do_ref[...] = do.astype(bf16)
    put_columns(gd_ref, (gain, shift))


def heads_back(first, last, hw, info, qkv_ref, lse_ref, o_ref, do_ref, dqkv_ref, gh_ref, ka, qa, va, oa):
    unit = o_ref.shape[1]
    for_keys, for_queries = segment_rows(info, unit)
    slot = lax.broadcasted_iota(jnp.int32, (16, unit), 0)
    ka[HEAD:, :] = jnp.where(jnp.logical_and(slot >= 4, slot < 7), 1.0, for_keys).astype(bf16)
    va[HEAD:, :] = jnp.where(slot < 3, 1.0, 0.0).astype(bf16)
    nothing = jnp.zeros((16, unit), f32)

    def per_block(c, carry):
        at = c - first
        for h in range(hw // HEAD):
            rows = pl.ds(pl.multiple_of(c * hw + h * HEAD, HEAD), HEAD)
            q = qkv_ref[c, h * HEAD : (h + 1) * HEAD, :] * jnp.bfloat16(score_scale)
            k = qkv_ref[c, hw + h * HEAD : hw + (h + 1) * HEAD, :]
            d = do_ref[rows, :]
            inner = jnp.sum(up(d) * o_ref[rows, :], axis=0, keepdims=True)
            qa[0:HEAD, :] = q
            qa[HEAD:, :] = three_rows(for_queries, -lse_ref[c, h : h + 1, :], 4).astype(bf16)
            ka[0:HEAD, :] = k
            va[0:HEAD, :] = qkv_ref[c, 2 * hw + h * HEAD : 2 * hw + (h + 1) * HEAD, :]
            oa[0:HEAD, :] = d
            oa[HEAD:, :] = three_rows(nothing, -inner, 0).astype(bf16)
            p = jnp.exp(dot(ka[...], qa[...], 0, 0))
            ds = (p * dot(va[...], oa[...], 0, 0)).astype(bf16)
            dv = dot(d, p.astype(bf16), 1, 1).astype(bf16)
            dq = (dot(k, ds, 1, 0) * score_scale).astype(bf16)
            dk = dot(q, ds, 1, 1).astype(bf16)
            dqkv_ref[at, h * HEAD : (h + 1) * HEAD, :] = dq
            dqkv_ref[at, hw + h * HEAD : hw + (h + 1) * HEAD, :] = dk
            dqkv_ref[at, 2 * hw + h * HEAD : 2 * hw + (h + 1) * HEAD, :] = dv
            gh_ref[at, h * HEAD : (h + 1) * HEAD, 0:1] = lane_sum(up(dq))
            gh_ref[at, h * HEAD : (h + 1) * HEAD, 1:2] = lane_sum(up(dv))
        return carry

    lax.fori_loop(first, last, per_block, 0)


def attend_back_kernel(nc, hw, info, e1_ref, o_ref, qkv_ref, lse_ref, pd, left, right, *refs):
    pieces = refs[:10]
    dqkv_ref, gd_ref, gh_ref, do_ref, p0, p1, q0, q1 = refs[10:18]
    left_ref, right_ref, go, ka, qa, va, oa, go_sem, add_in, add_out = refs[18:]
    fetch(pieces, 4 * hw, ((3 * hw, 4 * hw, lambda i: go.at[i // nc, pl.ds(i % nc * hw, hw)], go_sem),))
    start_add(left, right, left_ref, right_ref, add_in)
    mixed_back(nc, hw, info, e1_ref, o_ref, pd, go, go_sem, do_ref, gd_ref)
    heads_back(0, nc // 2, hw, info, qkv_ref, lse_ref, o_ref, do_ref, dqkv_ref, gh_ref, ka, qa, va, oa)
    finish_add((p0, p1, q0, q1), left_ref, right_ref, add_in, add_out)


def attend_back_rest_kernel(nc, hw, info, o_ref, qkv_ref, lse_ref, do_ref, dqkv_ref, gh_ref, ka, qa, va, oa):
    heads_back(nc // 2, nc, hw, info, qkv_ref, lse_ref, o_ref, do_ref, dqkv_ref, gh_ref, ka, qa, va, oa)


def input_back_kernel(nc, hw, rw, info, dqkv0, dqkv1, xs_ref, dx1_ref, pd, *refs):
    pieces = refs[:10]
    outs_ref, gd_ref, ga, da, ga_sem = refs[10:]
    fetch(pieces, 4 * hw, ((0, 3 * hw, lambda i: ga.at[i], ga_sem),))
    my_row = info[1]
    for i in range(2 * nc):
        arrive(ga.at[i], ga_sem.at[i])
    blocks = [dqkv0.at[i] for i in range(nc // 2)] + [dqkv1.at[i] for i in range(nc // 2)]
    for r in range(2):
        start = jnp.bitwise_xor(my_row, r) * nc
        part = dot(ga[start], blocks[0][...], 0, 0)
        for c in range(1, nc):
            part = part + dot(ga[start + c], blocks[c][...], 0, 0)
        da[r * rw : (r + 1) * rw, :] = part
    dx, gain, shift = norm_back(da[...], up(join(xs_ref)), pd[:, 0:1])
    put_columns(gd_ref, (gain, shift))
    apart(outs_ref, (dx1_ref[...] + dx).astype(bf16))


def attend_grads_kernel(
    nc, hw, fl, fw, info, dqkv0, dqkv1, a_ref, gd_in, gd_mid, gd_mix, gh0, gh1, gf_ref, keep_out, send_out,
    keep_ref, send_ref, wide, thin, out_sem,
):
    my_row = info[1]
    put_columns(
        wide, (gd_in[:, 0:1], gd_in[:, 1:2], gd_mid[:, 2:3], gd_mid[:, 0:1], gd_mid[:, 1:2], gd_mid[:, 3:4])
    )
    lane = lax.broadcasted_iota(jnp.int32, (fl, 128), 1)
    for c in range(nc):
        tile = jnp.zeros((fl, 128), f32)
        at = 6
        gh = (gh0, gh1)[c // 2].at[c % 2]
        for k in range(hw // fl):
            rows = slice(k * fl, (k + 1) * fl)
            deep = slice(c * hw + k * fl, c * hw + (k + 1) * fl)
            for column in (gh[rows, 0:1], gh[rows, 1:2], gd_mix[deep, 0:1], gd_mix[deep, 1:2]):
                tile = jnp.where(lane == at, column, tile)
                at += 1
        for k in range(fw // fl):
            rows = slice(k * fl, (k + 1) * fl)
            for column in (gf_ref[c, rows, 2:3], gf_ref[c, rows, 0:1], gf_ref[c, rows, 1:2]):
                tile = jnp.where(lane == at, column, tile)
                at += 1
        thin[c] = tile

    for row in range(2):
        a = a_ref[jnp.bitwise_xor(my_row, row)]
        for c in (1, 3, 0, 2):
            chip, ref, hbm, sem = c // 2, (keep_ref, send_ref)[c % 2], (keep_out, send_out)[c % 2], (0, nc)[c % 2]
            ref[row, chip, 0 : 3 * hw, :] = dot((dqkv0, dqkv1)[c // 2][c % 2], a, 1, 1).astype(bf16)
            block = jnp.bitwise_xor(info[0], row * nc + c)
            tile = (thin[c] + wide[pl.ds(pl.multiple_of(block * fl, fl), fl), :]).astype(bf16)
            third = fl // 3
            ref[row, chip, 3 * hw :, :] = jnp.concatenate([tile[k * third : (k + 1) * third] for k in range(3)], axis=1)
            move(ref.at[row, chip], hbm.at[row, chip], out_sem.at[sem + row * 2 + chip])
    stored_blocks(nc, keep_ref, send_ref, out_sem)


def shrink_kernel(nc, rw, fw, info, pd, gn_in, x1_in, *refs):
    pieces = refs[:10]
    y_ref, gn_ref, x1_ref, gs, gs_sem, in_sem = refs[10:]
    copy = move(gn_in, gn_ref, in_sem.at[0])
    x1_copy = move(x1_in, x1_ref, in_sem.at[1])
    fetch(pieces, fw, ((0, fw, lambda i: gs.at[i // nc, pl.ds(i % nc * fw, fw)], gs_sem),))
    my_row = info[1]
    copy.wait()
    for i in range(2 * nc):
        arrive(gs.at[i // nc, pl.ds(i % nc * fw, fw)], gs_sem.at[i])
    gn = gn_ref[...]
    for r in range(2):
        part = dot(gs[jnp.bitwise_xor(my_row, r)], gn, 0, 0)
        rows = slice(r * rw, (r + 1) * rw)
        if r == 0:
            x1_copy.wait()
        apart(y_ref.at[:, rows], (x1_ref[rows, :] + part + pd[rows, 5:6]).astype(bf16))


def body(
    tokens,
    cotangent,
    holder_of,
    lengths,
    input_gain,
    input_shift,
    attend_weight,
    attend_bias,
    mixed_gain,
    mixed_shift,
    output_weight,
    output_bias,
    middle_gain,
    middle_shift,
    expand_weight,
    expand_bias,
    hidden_gain,
    hidden_shift,
    shrink_weight,
    shrink_bias,
):
    holders = lax.axis_size("dp")
    half = holders // 2
    nr, nc = lax.axis_size("row"), lax.axis_size("col")
    n = nr * nc
    micro = holder_of.shape[0]
    assert micro == n and nr == 2 and nc == 4
    fl = tokens.shape[0]
    pairs = micro * half
    blk = tokens.shape[1] // pairs
    unit = half * blk
    dp = lax.axis_index("dp")
    side, pos = dp // half, dp % half
    my_row, my_col = lax.axis_index("row"), lax.axis_index("col")
    rc = my_row * nc + my_col
    groups = [list(range(s * half * n, (s + 1) * half * n)) for s in range(2)]
    hw, rw, fw = output_weight.shape[0], output_weight.shape[1], shrink_weight.shape[0]

    def flip_row(v):
        return lax.ppermute(v, "row", [(i, i ^ 1) for i in range(nr)])

    def flip_chip(v):
        return lax.ppermute(v, "col", [(i, i ^ 2) for i in range(nc)])

    def flip_core(v):
        return lax.ppermute(v, "col", [(i, i ^ 1) for i in range(nc)])

    def flip_dp(v, step):
        return lax.ppermute(v, "dp", [(i, i ^ step) for i in range(holders)])

    def exchange(v):
        return lax.all_to_all(v, ("dp",) + RC, 0, 0, axis_index_groups=groups, tiled=True)

    lanes = blk % 128 == 0

    def to_unit(v):
        v = jnp.transpose(v.reshape(2, fl, half * n, blk), (2, 0, 1, 3))
        v = exchange(v.reshape(half * n, 2 * fl, blk)).reshape(half, n, 2, fl, blk)
        v = jnp.transpose(v, (2, 0, 1, 3, 4)).reshape(2, half, n * fl, blk)
        return tuple(v) if lanes else tuple(jnp.transpose(v, (0, 2, 1, 3)).reshape(2, 1, n * fl, unit))

    def from_unit(v):
        if not lanes:
            v = jnp.transpose(v.reshape(n * fl, half, blk), (1, 0, 2))
        v = exchange(v.reshape(half * n, fl, blk))
        return jnp.transpose(v, (1, 0, 2)).reshape(tokens.shape)

    def tie(*values):
        return lax.optimization_barrier(values)

    def near(v):
        return flip_row(v), flip_chip(v)

    def far(v, by_row, by_chip):
        h = v.shape[0] // 2
        return flip_row(by_chip[:h]), flip_chip(by_row[h:])

    def pieces_of(v, near_v, far_v):
        own = (v, near_v[1], near_v[0]) + far_v
        v1, c1, r1, f1, g1 = (flip_core(p) for p in own)
        return (v, v1, near_v[1], c1, near_v[0], r1, far_v[0], far_v[1], f1, g1)

    w1 = jnp.concatenate([attend_weight.reshape(3 * hw, rw), output_weight], axis=0)
    near1 = near(w1)
    both = to_unit(jnp.concatenate([tokens, cotangent], axis=0))
    tile = jnp.concatenate(
        [
            jnp.stack([input_gain, input_shift, output_bias, middle_gain, middle_shift, shrink_bias]),
            jnp.transpose(
                jnp.stack([attend_bias[0], attend_bias[1], mixed_gain, mixed_shift]).reshape(4, -1, fl), (1, 0, 2)
            ).reshape(-1, fl),
            jnp.transpose(jnp.stack([expand_bias, hidden_gain, hidden_shift]).reshape(3, -1, fl), (1, 0, 2)).reshape(-1, fl),
        ]
    )
    tile = jnp.transpose(jnp.pad(tile, ((0, 128 - tile.shape[0]), (0, 0))))
    tile_row, tile_chip = near(tile)
    far1 = far(w1, *near1)
    g1 = pieces_of(w1, near1, far1)
    even = jnp.stack([tile, tile_chip, tile_row, flip_row(tile_chip)])
    odd = flip_core(even)
    far1, both, w2 = tie(far1, both, expand_weight)
    near2 = near(w2)
    x, e2 = both

    k_unit = 2 * (pos * n + rc) + side
    own = lengths[k_unit // holders, holder_of[k_unit // holders, k_unit % holders]]
    info = jnp.concatenate([jnp.stack([rc, my_row]), jnp.cumsum(own)[:-1]]).astype(jnp.int32)

    d = n * fl
    split = lambda v: v.reshape(nr, rw, unit)
    dma = pltpu.SemaphoreType.DMA
    weight_flops = 2 * unit * d * nc * fw

    dp_odd = dp % 2 == 1

    def reduce_rest(v):
        step = 2
        while step < holders:
            v = v + flip_dp(v, step)
            step *= 2
        return v

    def spread(v):
        got = flip_dp(v, 1)
        return jnp.concatenate([jnp.where(dp_odd, got, v), jnp.where(dp_odd, v, got)], axis=0).astype(f32)

    vm = lambda shape, dtype=bf16: pltpu.VMEM(shape, dtype)
    act, act32, hid = (d, unit), (nc * hw, unit), (nc, fw, unit)
    part1, part2, part3 = (nr, nc // 2, 4 * hw, rw), (nr, nc // 2, rw, fw), (nr, nc // 2, fw, rw)

    def time_us(t):
        return dict(flops=int(t * 1e9), moved=int(t * 1e6))

    extra = vm((HEAD + 16, unit))
    a, qkv, lse, o, pd, pf = call(
        functools.partial(attend_kernel, nc, hw, rw, fl, fw),
        (
            sds(act, bf16), sds((nc, 3 * hw, unit), bf16), sds((nc, 8, unit), f32), sds(act, f32),
            sds((d, 16), f32), sds((nc, fw, 8), f32),
        ),
        [SMEM, VMEM, VMEM, VMEM] + [HBM] * 10,
        [HBM] * 3 + [VMEM] * 3,
        [
            vm(act), vm((nc, 3 * hw, unit)), vm((nc, 8, unit), f32), vm((n, 3 * hw, rw)), extra, extra,
            dma((n,)), dma((3,)),
        ],
        **time_us(13), name="attend",
    )(info, x, even, odd, *g1)

    o, near2 = tie(o, near2)
    far2 = far(w2, *near2)

    on, x1, b = call(
        functools.partial(output_kernel, nc, hw, rw),
        (sds(act, bf16), sds(act, f32), sds(act, bf16)),
        [SMEM] + [VMEM] * 3 + [HBM] * 10,
        [VMEM] * 3,
        [vm((nr, nc * hw, rw)), dma((n,))],
        **time_us(5), name="output",
    )(info, x, o, pd, *g1)

    b, far2, w3 = tie(b, far2, shrink_weight)
    near3 = near(w3)
    g2 = pieces_of(w2, near2, far2)

    gn, vh, slope, st = call(
        functools.partial(expand_kernel, nc, rw, fw),
        (sds(hid, bf16), sds(hid, bf16), sds(hid, bf16), sds((8, unit), f32)),
        [SMEM, VMEM, VMEM] + [HBM] * 10,
        [VMEM, HBM, HBM, VMEM],
        [vm(hid), vm(hid), vm(hid, f32), vm((n, rw, fw)), dma((n,)), dma((2 * nc,))],
        **time_us(11), name="expand",
    )(info, split(b), pf, *g2)

    gn, near3 = tie(gn, near3)
    far3 = far(w3, *near3)

    e2, shr_keep, shr_send = call(
        functools.partial(shrink_grads_kernel, nc, rw),
        (sds((nr, rw, unit), bf16), sds(part3, bf16), sds(part3, bf16)),
        [SMEM] + [VMEM] * 2,
        [VMEM, HBM, HBM],
        [vm(part3), vm(part3), dma((2 * nc,))],
        **time_us(7), name="shrink_grads",
    )(info, gn, e2)

    shr_send, far3 = tie(shr_send, far3)
    g3 = pieces_of(w3, near3, far3)
    shr_got = flip_core(shr_send)

    df, gf = call(
        functools.partial(hidden_back_kernel, nc, fw),
        (sds(hid, bf16), sds((nc, fw, 8), f32)),
        [SMEM] + [VMEM] * 3 + [HBM] * 12,
        [VMEM, VMEM],
        [vm(hid), vm(hid), vm((n, fw, rw)), vm(hid, f32), dma((n,)), dma((nc,)), dma((nc,))],
        **time_us(13), name="hidden_back",
    )(info, st, e2, pf, vh, slope, *g3)

    dx1, e1, gd_mid = call(
        functools.partial(middle_back_kernel, nc, rw, fw),
        (sds(act, f32), sds((nr, rw, unit), bf16), sds((d, 8), f32)),
        [SMEM] + [VMEM] * 4 + [HBM] * 10,
        [VMEM] * 3,
        [vm((n, rw, fw)), vm(act, f32), dma((n,))],
        **time_us(6), name="middle_back",
    )(info, df, x1, e2, pd, *g2)

    rows2 = 2 * rw + hw
    part2 = (nr, nc // 2, rows2, rw)
    sum2, sum3 = (nc // 2, rows2 // 2, rw), (nc // 2, fw // 2, rw)
    mid_keep, mid_send, *shr = call(
        functools.partial(middle_grads_kernel, nc, hw, rw, fw),
        (sds(part2, bf16), sds(part2, bf16)) + (sds(sum3, bf16),) * 4,
        [SMEM] + [VMEM] * 4 + [HBM] * 2,
        [HBM] * 6,
        [vm(part2), vm(part2), vm(part3), vm(part3), dma((8,)), dma((8,)), dma((2 * nc,))],
        **time_us(9), name="middle_grads",
    )(info, split(b), df, on.reshape(nc, hw, unit), e1, shr_keep, shr_got)

    def reduce_near(v):
        return flip_row(v[1]), flip_chip(v[3])

    def reduce_far(v, got):
        p, q = v[0] + got[0], v[2] + got[1]
        return (p[0], q[0]), (flip_chip(p[1]), flip_row(q[1]))

    def reduce_dp(v, got):
        p, q = v[0] + got[0], v[1] + got[1]
        return jnp.where(dp_odd, q, p), flip_dp(jnp.where(dp_odd, p, q), 1)

    mid_got = flip_core(mid_send)
    shr_near = reduce_near(shr)

    dqkv0, gd_mix, gh0, do, *mid = call(
        functools.partial(attend_back_kernel, nc, hw),
        (
            sds((nc // 2, 3 * hw, unit), bf16), sds((d, 8), f32), sds((nc // 2, hw, 8), f32), sds(act, bf16),
        ) + (sds(sum2, bf16),) * 4,
        [SMEM] + [VMEM] * 5 + [HBM] * 12,
        [VMEM] * 4 + [HBM] * 4,
        [
            vm(part2), vm(part2), vm((nr, nc * hw, rw)), extra, extra, extra, extra,
            dma((n,)), dma((8,)), dma((8,)),
        ],
        **time_us(11), name="attend_back",
    )(info, e1, o, qkv, lse, pd, mid_keep, mid_got, *g1)

    do, shr_near, mid = tie(do, shr_near, mid)
    shr_stay, shr_far = reduce_far(shr, shr_near)
    mid_near = reduce_near(mid)

    dqkv1, gh1 = call(
        functools.partial(attend_back_rest_kernel, nc, hw),
        (sds((nc // 2, 3 * hw, unit), bf16), sds((nc // 2, hw, 8), f32)),
        [SMEM] + [VMEM] * 4,
        [VMEM] * 2,
        [extra, extra, extra, extra],
        **time_us(8), name="attend_back_rest",
    )(info, o, qkv, lse, do)

    dqkv1, shr_far = tie(dqkv1, shr_far)
    shr, shr_dp = reduce_dp(shr_stay, shr_far)

    input_grad, gd_in = call(
        functools.partial(input_back_kernel, nc, hw, rw),
        (sds(x.shape, bf16), sds((d, 8), f32)),
        [SMEM] + [VMEM] * 5 + [HBM] * 10,
        [VMEM] * 2,
        [vm((n, 3 * hw, rw)), vm(act, f32), dma((n,))],
        **time_us(7), name="input_back",
    )(info, dqkv0, dqkv1, x, dx1, pd, *g1)

    gd_in, shr_dp, mid_near = tie(gd_in, shr_dp, mid_near)
    shr = reduce_rest(shr + shr_dp)
    mid_stay, mid_far = reduce_far(mid, mid_near)

    rows1 = 3 * hw + fl // 3
    part1 = (nr, nc // 2, rows1, rw)
    att_keep, att_send = call(
        functools.partial(attend_grads_kernel, nc, hw, fl, fw),
        (sds(part1, bf16), sds(part1, bf16)),
        [SMEM] + [VMEM] * 9,
        [HBM] * 2,
        [vm(part1), vm(part1), vm((d, 128), f32), vm((nc, fl, 128), f32), dma((2 * nc,))],
        **time_us(7), name="attend_grads",
    )(info, dqkv0, dqkv1, split(a), gd_in, gd_mid, gd_mix, gh0, gh1, gf)

    att_send, shr, mid_far = tie(att_send, shr, mid_far)
    att_got = flip_core(att_send)
    mid, mid_dp = reduce_dp(mid_stay, mid_far)
    h = rows1 // 2
    p_row = flip_row(att_keep[1, :, :h] + att_got[1, :, :h])
    q_chip = flip_chip(att_keep[:, 1, h:] + att_got[:, 1, h:])
    p = att_keep[0, :, :h] + att_got[0, :, :h] + p_row
    q = att_keep[:, 0, h:] + att_got[:, 0, h:] + q_chip

    y = call(
        functools.partial(shrink_kernel, nc, rw, fw),
        sds(x.shape, bf16),
        [SMEM, VMEM] + [HBM] * 12,
        VMEM,
        [vm((nc * fw, unit)), vm(act, f32), vm((nr, nc * fw, rw)), dma((n,)), dma((2,))],
        **time_us(8), name="shrink",
    )(info, pd, gn.reshape(nc * fw, unit), x1, *g3)

    input_grad = from_unit(input_grad)
    block_out = from_unit(y)

    shr_w_g = spread(shr)
    mid = spread(reduce_rest(mid + mid_dp))
    exp_w_g = jnp.concatenate([mid[:rw], mid[rw : 2 * rw]], axis=1)
    att, att_dp = reduce_dp((p[0], q[0]), (flip_chip(p[1]), flip_row(q[1])))
    att = spread(reduce_rest(att + att_dp))

    thin = att[3 * hw :]
    thin = jnp.transpose(jnp.concatenate([thin[:, k * 128 : (k + 1) * 128] for k in range(3)], axis=0))
    in_g_g, in_s_g, out_b_g, mid_g_g, mid_s_g, shr_b_g = (thin[i] for i in range(6))
    at = 6 + 4 * (hw // fl)
    heads_g = jnp.transpose(thin[6:at].reshape(-1, 4, fl), (1, 0, 2)).reshape(4, hw)
    hidden_g = jnp.transpose(thin[at : at + 3 * (fw // fl)].reshape(-1, 3, fl), (1, 0, 2)).reshape(3, fw)
    q_b_g, v_b_g, mix_g_g, mix_s_g = heads_g
    exp_b_g, hid_g_g, hid_s_g = hidden_g
    return (
        block_out,
        input_grad,
        in_g_g,
        in_s_g,
        att[: 3 * hw].reshape(attend_weight.shape),
        jnp.stack([q_b_g, v_b_g]),
        mix_g_g,
        mix_s_g,
        mid[2 * rw :],
        out_b_g,
        mid_g_g,
        mid_s_g,
        exp_w_g,
        exp_b_g,
        hid_g_g,
        hid_s_g,
        shr_w_g,
        shr_b_g,
    )


def solution(mesh):
    wide, narrow = P(RC), P("col")
    in_specs = (
        P(RC, "dp"), P(RC, "dp"), P(), P(), wide, wide, P(None, "col", "row"), P(None, "col"),
        narrow, narrow, P("col", "row"), wide, wide, wide, P("row", "col"), narrow, narrow, narrow,
        P("col", "row"), wide,
    )
    out_specs = (
        P(RC, "dp"), P(RC, "dp"), wide, wide, P(None, "col", "row"), P(None, "col"), narrow, narrow,
        P("col", "row"), wide, wide, wide, P("row", "col"), narrow, narrow, narrow, P("col", "row"),
        wide,
    )
    return jax.shard_map(body, mesh=mesh, in_specs=in_specs, out_specs=out_specs, check_vma=False)
```

```python
import functools
import math

import jax
import jax.numpy as jnp
from jax import lax
from jax.experimental import pallas as pl
from jax.experimental.pallas import tpu as pltpu
from jax.sharding import PartitionSpec as P

HEAD = 64
eps = 1e-05
masked_score = -1e30
f32 = jnp.float32
bf16 = jnp.bfloat16
RC = ("row", "col")
HBM = pl.BlockSpec(memory_space=pltpu.HBM)
SMEM = pl.BlockSpec(memory_space=pltpu.SMEM)
VMEM = pl.BlockSpec(memory_space=pltpu.VMEM)
root_half = math.sqrt(0.5)
root_tau = 1.0 / math.sqrt(2.0 * math.pi)
score_scale = 1.0 / math.sqrt(HEAD)


def dot(a, b, ca, cb):
    return lax.dot_general(a, b, (((ca,), (cb,)), ((), ())), preferred_element_type=f32)


def up(v):
    return v.astype(f32)


def lane_sum(v):
    return jnp.sum(v, axis=1, keepdims=True)


def token_sum(v):
    return jnp.sum(v, axis=0, keepdims=True)


CHUNK = 768
ROOM = 8


def over(rows, step, init=0):
    def one(i, carry):
        return step(pl.ds(pl.multiple_of(i * CHUNK, CHUNK), CHUNK), carry)

    return lax.fori_loop(0, rows // CHUNK, one, init)


def moments(ref):
    rows, unit = ref.shape
    zero = jnp.zeros((1, unit), f32)
    mu = over(rows, lambda at, s: s + token_sum(up(ref[at, :])), zero) * (1.0 / rows)

    def square(at, s):
        d = up(ref[at, :]) - mu
        return s + token_sum(d * d)

    return mu, lax.rsqrt(over(rows, square, zero) * (1.0 / rows) + eps)


def norm(out, ref, pd, gain, shift):
    mu, r = moments(ref)

    def one(at, carry):
        out[at, :] = ((up(ref[at, :]) - mu) * r * pd[at, gain : gain + 1] + pd[at, shift : shift + 1]).astype(bf16)
        return carry

    over(ref.shape[0], one)


def norm_back(grad, ref, pd, gain, gd, emit):
    rows, unit = ref.shape
    mu, r = moments(ref)
    zero = jnp.zeros((1, unit), f32)

    def first(at, s):
        g = grad[at, :]
        gv = g * ((up(ref[at, :]) - mu) * r)
        gd[at, 0:1] = lane_sum(gv)
        gd[at, 1:2] = lane_sum(g)
        k = pd[at, gain : gain + 1]
        return s[0] + token_sum(g * k), s[1] + token_sum(gv * k)

    m1, m2 = over(rows, first, (zero, zero))
    m1, m2 = m1 * (1.0 / rows), m2 * (1.0 / rows)

    def second(at, carry):
        vh = (up(ref[at, :]) - mu) * r
        emit(at, r * (grad[at, :] * pd[at, gain : gain + 1] - m1 - vh * m2))
        return carry

    over(rows, second)


PIECES = ((0, None), (1, None), (2, None), (3, None), (4, None), (5, None), (6, 0), (6, 1), (7, 0), (7, 1))


def fetch(pieces, rows, parts):
    for ref, (block, half) in zip(pieces, PIECES):
        first, last = (0, rows) if half is None else (half * rows // 2, (half + 1) * rows // 2)
        for lo, hi, place, sem in parts:
            a, b = max(lo, first), min(hi, last)
            if a < b:
                pltpu.make_async_copy(
                    ref.at[pl.ds(a - first, b - a)], place(block).at[pl.ds(a - lo, b - a)], sem.at[block]
                ).start()


def arrive(ref, sem):
    pltpu.make_async_copy(ref, ref, sem).wait()


def move(src, dst, sem):
    copy = pltpu.make_async_copy(src, dst, sem)
    copy.start()
    return copy


def vmem_bytes(shape, dtype):
    size = jnp.dtype(dtype).itemsize
    sublanes, lanes = 32 // size, 128
    *lead, rows, columns = (1,) * max(0, 2 - len(shape)) + tuple(shape)
    return math.prod(lead) * (-(-rows // sublanes) * sublanes) * (-(-columns // lanes) * lanes) * size


def pinned(spec):
    return pltpu.VMEM if spec is VMEM else pltpu.HBM


def call(kernel, outs, in_specs, out_specs, scratch=(), flops=0, moved=0, name=None):
    held = [v for v in scratch if v.memory_space == pltpu.VMEM]
    limit = sum(vmem_bytes(v.shape, v.dtype) for v in held) + (ROOM << 20)
    single = not isinstance(outs, tuple)
    places = [pinned(spec)(v.shape, v.dtype) for v, spec in zip((outs,) if single else outs, (out_specs,) if single else out_specs)]

    def run(*args):
        args = [v if spec is SMEM else pltpu.with_memory_space_constraint(v, pinned(spec)) for v, spec in zip(args, in_specs)]
        return pl.pallas_call(
            kernel,
            out_shape=places[0] if single else tuple(places),
            in_specs=in_specs,
            out_specs=out_specs,
            scratch_shapes=list(scratch),
            compiler_params=pltpu.CompilerParams(vmem_limit_bytes=limit),
            cost_estimate=pl.CostEstimate(flops=flops, bytes_accessed=moved, transcendentals=0),
            name=name,
        )(*args)

    return run


def sds(shape, dtype):
    return jax.ShapeDtypeStruct(shape, dtype)


def segment_rows(info, unit):
    t = lax.broadcasted_iota(jnp.int32, (16, unit), 1)
    slot = lax.broadcasted_iota(jnp.int32, (16, unit), 0)
    one = lambda b: jnp.where(t >= b, 1, 0)
    seg = one(info[2]) + one(info[3]) + one(info[4])
    same = seg == slot
    for_keys = jnp.where(same, 1.0, 0.0)
    for_queries = jnp.where(jnp.logical_and(slot < 4, jnp.logical_not(same)), masked_score, 0.0)
    return for_keys, for_queries


def split3(v):
    hi = v.astype(bf16)
    v = v - up(hi)
    mid = v.astype(bf16)
    return hi, mid, (v - up(mid)).astype(bf16)


def three_rows(base, v, first):
    row = lax.broadcasted_iota(jnp.int32, base.shape, 0)
    for i, part in enumerate(split3(v)):
        base = jnp.where(row == first + i, up(part), base)
    return base


def unit_of(ref, which):
    blocks, n, rows, _ = ref.shape
    rows //= 2
    return jnp.concatenate(
        [
            jnp.concatenate([ref[k, i, which * rows : (which + 1) * rows, :] for i in range(n)], axis=0)
            for k in range(blocks)
        ],
        axis=1,
    )


def apart(ref, at, value):
    width = ref.shape[2]
    for i in range(ref.shape[0]):
        ref[i, at, :] = value[:, i * width : (i + 1) * width]


def beside(ref, info, nc, rw):
    def place(i):
        row = jnp.bitwise_xor(info[1], i // nc)
        return ref.at[i % nc, :, pl.ds(pl.multiple_of(row * rw, rw), rw)]

    return place


def below(ref, info, nc, rw):
    def place(i):
        row = jnp.bitwise_xor(info[1], i // nc)
        return ref.at[i % nc, pl.ds(pl.multiple_of(row * rw, rw), rw)]

    return place


def attend_kernel(nc, hw, rw, fl, fw, info, both, even, odd, *refs):
    pieces = refs[:10]
    x_ref, a_ref, qkv_out, lse_ref, o_ref, pd, pf = refs[10:17]
    qkv_ref, ga, ka, qa, ga_sem, out_sem = refs[17:]
    unit = o_ref.shape[1]
    fetch(pieces, 4 * hw, ((0, 3 * hw, beside(ga, info, nc, rw), ga_sem),))
    for i in range(2 * nc):
        tile = (even, odd)[i % 2][i // 2]
        pd[pl.ds(pl.multiple_of(jnp.bitwise_xor(info[0], i) * fl, fl), fl), 0:6] = tile[:, 0:6]
        if i < nc:
            for k in range(hw // fl):
                pd[i * hw + k * fl : i * hw + (k + 1) * fl, 6:10] = tile[:, 6 + 4 * k : 10 + 4 * k]
            for k in range(fw // fl):
                first = 6 + 4 * (hw // fl) + 3 * k
                pf[i, k * fl : (k + 1) * fl, 0:3] = tile[:, first : first + 3]
    x_ref[...] = unit_of(both, 0)
    norm(a_ref, x_ref, pd, 0, 1)
    for_keys, for_queries = segment_rows(info, unit)
    ka[HEAD:, :] = for_keys.astype(bf16)
    qa[HEAD:, :] = for_queries.astype(bf16)

    def per_block(c, carry):
        for i in (c, nc + c):
            arrive(ga.at[c, :, pl.ds(0, rw)], ga_sem.at[i])
        trip = dot(ga[c], a_ref[...], 1, 0)
        at = pl.multiple_of(c * hw, hw)
        qkv_ref[c, 0:hw, :] = (trip[0:hw] + pd[pl.ds(at, hw), 6:7]).astype(bf16)
        qkv_ref[c, hw : 2 * hw, :] = trip[hw : 2 * hw].astype(bf16)
        qkv_ref[c, 2 * hw :, :] = (trip[2 * hw :] + pd[pl.ds(at, hw), 7:8]).astype(bf16)
        move(qkv_ref.at[c], qkv_out.at[c], out_sem.at[c])
        for h in range(hw // HEAD):
            qa[0:HEAD, :] = qkv_ref[c, h * HEAD : (h + 1) * HEAD, :] * jnp.bfloat16(score_scale)
            ka[0:HEAD, :] = qkv_ref[c, hw + h * HEAD : hw + (h + 1) * HEAD, :]
            v = qkv_ref[c, 2 * hw + h * HEAD : 2 * hw + (h + 1) * HEAD, :]
            s = dot(ka[...], qa[...], 0, 0)
            top = jnp.max(s, axis=0, keepdims=True)
            e = jnp.exp(s - top)
            den = token_sum(e)
            o = dot(v, e.astype(bf16), 1, 0) * (1.0 / den)
            o_ref[pl.ds(pl.multiple_of(c * hw + h * HEAD, HEAD), HEAD), :] = o
            lse_ref[c, h : h + 1, :] = top + jnp.log(den)
        return carry

    lax.fori_loop(0, nc, per_block, 0)
    for c in range(nc):
        arrive(qkv_ref.at[c], out_sem.at[c])


def output_kernel(nc, hw, rw, info, x_ref, o_ref, pd, *refs):
    pieces = refs[:10]
    on_ref, x1_ref, b_ref, go, go_sem = refs[10:]
    fetch(pieces, 4 * hw, ((3 * hw, 4 * hw, lambda i: go.at[i // nc, pl.ds(i % nc * hw, hw)], go_sem),))
    my_row = info[1]
    norm(on_ref, o_ref, pd, 8, 9)
    on = on_ref[...]
    for i in range(2 * nc):
        arrive(go.at[i // nc, pl.ds(i % nc * hw, hw)], go_sem.at[i])
    for r in range(2):
        rows = slice(r * rw, (r + 1) * rw)
        x1_ref[rows, :] = dot(go[jnp.bitwise_xor(my_row, r)], on, 0, 0) + up(x_ref[rows, :]) + pd[rows, 2:3]
    norm(b_ref, x1_ref, pd, 3, 4)


def expand_kernel(nc, rw, fw, info, b_ref, pf, *refs):
    pieces = refs[:10]
    gn_ref, vh_out, slope_out, st_ref = refs[10:14]
    vh_ref, slope_ref, g_ref, ge, ge_sem, out_sem = refs[14:]
    fetch(pieces, rw, ((0, rw, below(ge, info, nc, rw), ge_sem),))
    unit = b_ref.shape[1]
    total = nc * fw

    def first(c, s):
        for i in (c, nc + c):
            arrive(ge.at[c, pl.ds(0, rw)], ge_sem.at[i])
        f = dot(ge[c], b_ref[...], 0, 0) + pf[c, :, 0:1]
        phi = 0.5 * (1.0 + lax.erf(f * root_half))
        g = f * phi
        g_ref[c] = g
        slope_ref[c] = (phi + f * (jnp.exp(-0.5 * f * f) * root_tau)).astype(bf16)
        move(slope_ref.at[c], slope_out.at[c], out_sem.at[c])
        return s + token_sum(g)

    mu = lax.fori_loop(0, nc, first, jnp.zeros((1, unit), f32)) * (1.0 / total)

    def second(c, s):
        def square(at, t):
            d = g_ref[c, at, :] - mu
            return t + token_sum(d * d)

        return over(fw, square, s)

    r = lax.rsqrt(lax.fori_loop(0, nc, second, jnp.zeros((1, unit), f32)) * (1.0 / total) + eps)
    st_ref[...] = jnp.broadcast_to(r, st_ref.shape)

    def third(c, carry):
        def one(at, t):
            vh = (g_ref[c, at, :] - mu) * r
            vh_ref[c, at, :] = vh.astype(bf16)
            gn_ref[c, at, :] = (vh * pf[c, at, 1:2] + pf[c, at, 2:3]).astype(bf16)
            return t

        over(fw, one)
        move(vh_ref.at[c], vh_out.at[c], out_sem.at[nc + c])
        return carry

    lax.fori_loop(0, nc, third, 0)
    for c in range(nc):
        arrive(slope_ref.at[c], out_sem.at[c])
        arrive(vh_ref.at[c], out_sem.at[nc + c])


def store_blocks(nc, blocks, keep, send):
    def one(k, carry):
        for ref, c in ((send, 2 * k + 1), (keep, 2 * k)):
            blocks(c, lambda row: ref.at[row, k])
        return carry

    lax.fori_loop(0, nc // 2, one, 0)


def shrink_grads_kernel(nc, rw, info, gn_ref, both, e2_ref, keep, send):
    my_row = info[1]
    e2_ref[...] = unit_of(both, 1)

    def blocks(c, place):
        grad = dot(gn_ref[c], e2_ref[...], 1, 1).astype(bf16)
        for r in range(2):
            place(jnp.bitwise_xor(my_row, r))[...] = grad[:, r * rw : (r + 1) * rw]

    store_blocks(nc, blocks, keep, send)


def add_blocks(left, right, outs):
    h = left.shape[2] // 2
    for j in range(4):
        r, c = j // 2, j % 2
        outs[r][c] = (up(left[r, c, :h]) + up(right[r, c, :h])).astype(bf16)
        outs[2 + c][r] = (up(left[r, c, h:]) + up(right[r, c, h:])).astype(bf16)


def hidden_back_kernel(nc, rw, fw, info, st_ref, e2_ref, pf, left, right, vh_in, slope_in, *refs):
    pieces = refs[:10]
    df_ref, gf_ref, p0, p1, q0, q1 = refs[10:16]
    vh_ref, slope_ref, gs, dgn, gs_sem, vh_sem, slope_sem = refs[16:]
    fetch(pieces, fw, ((0, fw, beside(gs, info, nc, rw), gs_sem),))
    for c in range(nc):
        move(vh_in.at[c], vh_ref.at[c], vh_sem.at[c])
    for c in range(nc):
        move(slope_in.at[c], slope_ref.at[c], slope_sem.at[c])
    add_blocks(left, right, (p0, p1, q0, q1))
    r = st_ref[0:1, :]
    unit = e2_ref.shape[1]
    total = nc * fw

    def first(c, s):
        for i in (c, nc + c):
            arrive(gs.at[c, :, pl.ds(0, rw)], gs_sem.at[i])
        arrive(vh_ref.at[c], vh_sem.at[c])
        dgn[c] = dot(gs[c], e2_ref[...], 1, 0)

        def one(at, t):
            d = dgn[c, at, :]
            dv = d * up(vh_ref[c, at, :])
            gf_ref[c, at, 0:1] = lane_sum(dv)
            gf_ref[c, at, 1:2] = lane_sum(d)
            gain = pf[c, at, 1:2]
            return t[0] + token_sum(d * gain), t[1] + token_sum(dv * gain)

        return over(fw, one, s)

    zero = jnp.zeros((1, unit), f32)
    m1, m2 = lax.fori_loop(0, nc, first, (zero, zero))
    m1, m2 = m1 * (1.0 / total), m2 * (1.0 / total)

    def second(c, carry):
        arrive(slope_ref.at[c], slope_sem.at[c])

        def one(at, t):
            dg = r * (dgn[c, at, :] * pf[c, at, 1:2] - m1 - up(vh_ref[c, at, :]) * m2)
            df = (dg * up(slope_ref[c, at, :])).astype(bf16)
            df_ref[c, at, :] = df
            gf_ref[c, at, 2:3] = lane_sum(up(df))
            return t

        over(fw, one)
        return carry

    lax.fori_loop(0, nc, second, 0)


def middle_back_kernel(nc, rw, fw, info, df_ref, x1_ref, e2_ref, pd, *refs):
    pieces = refs[:10]
    dx1_ref, e1_ref, gd_ref, ge, db, ge_sem = refs[10:]
    fetch(pieces, rw, ((0, rw, below(ge, info, nc, rw), ge_sem),))
    db[...] = jnp.zeros(db.shape, f32)

    def one(c, carry):
        for i in (c, nc + c):
            arrive(ge.at[c, pl.ds(0, rw)], ge_sem.at[i])
        db[...] += dot(ge[c], df_ref[c], 1, 0)
        return carry

    lax.fori_loop(0, nc, one, 0)

    def emit(at, dx):
        dy = up(e2_ref[at, :])
        dx1 = dy + dx
        dx1_ref[at, :] = dx1
        e1 = dx1.astype(bf16)
        e1_ref[at, :] = e1
        gd_ref[at, 2:3] = lane_sum(up(e1))
        gd_ref[at, 3:4] = lane_sum(dy)

    norm_back(db, x1_ref, pd, 3, gd_ref, emit)


def middle_grads_kernel(
    nc, hw, rw, fw, info, b_ref, df_ref, on_ref, e1_ref, keep, send,
):
    my_row = info[1]

    def blocks(c, place):
        grad = dot(b_ref[...], df_ref[c], 1, 1).astype(bf16)
        out_grad = dot(on_ref[c], e1_ref[...], 1, 1).astype(bf16)
        half = fw // 2
        for r in range(2):
            ref = place(jnp.bitwise_xor(my_row, r))
            for k in range(2):
                ref[k * rw : (k + 1) * rw, :] = grad[r * rw : (r + 1) * rw, k * half : (k + 1) * half]
            ref[2 * rw :, :] = out_grad[:, r * rw : (r + 1) * rw]

    store_blocks(nc, blocks, keep, send)


def heads_back(first, last, hw, info, qkv_ref, lse_ref, o_ref, do_ref, dqkv_ref, gh_ref, ka, qa, va, oa):
    unit = o_ref.shape[1]
    for_keys, for_queries = segment_rows(info, unit)
    slot = lax.broadcasted_iota(jnp.int32, (16, unit), 0)
    ka[HEAD:, :] = jnp.where(jnp.logical_and(slot >= 4, slot < 7), 1.0, for_keys).astype(bf16)
    va[HEAD:, :] = jnp.where(slot < 3, 1.0, 0.0).astype(bf16)
    nothing = jnp.zeros((16, unit), f32)

    def per_block(c, carry):
        at = c - first
        to = lambda j, h: pl.ds(pl.multiple_of(at * 3 * hw + j * hw + h * HEAD, HEAD), HEAD)
        for h in range(hw // HEAD):
            rows = pl.ds(pl.multiple_of(c * hw + h * HEAD, HEAD), HEAD)
            q = qkv_ref[c, h * HEAD : (h + 1) * HEAD, :] * jnp.bfloat16(score_scale)
            k = qkv_ref[c, hw + h * HEAD : hw + (h + 1) * HEAD, :]
            d = do_ref[rows, :]
            inner = jnp.sum(up(d) * o_ref[rows, :], axis=0, keepdims=True)
            qa[0:HEAD, :] = q
            qa[HEAD:, :] = three_rows(for_queries, -lse_ref[c, h : h + 1, :], 4).astype(bf16)
            ka[0:HEAD, :] = k
            va[0:HEAD, :] = qkv_ref[c, 2 * hw + h * HEAD : 2 * hw + (h + 1) * HEAD, :]
            oa[0:HEAD, :] = d
            oa[HEAD:, :] = three_rows(nothing, -inner, 0).astype(bf16)
            p = jnp.exp(dot(ka[...], qa[...], 0, 0))
            ds = (p * dot(va[...], oa[...], 0, 0)).astype(bf16)
            dv = dot(d, p.astype(bf16), 1, 1).astype(bf16)
            dq = (dot(k, ds, 1, 0) * score_scale).astype(bf16)
            dk = dot(q, ds, 1, 1).astype(bf16)
            dqkv_ref[to(0, h), :] = dq
            dqkv_ref[to(1, h), :] = dk
            dqkv_ref[to(2, h), :] = dv
            gh_ref[at, h * HEAD : (h + 1) * HEAD, 0:1] = lane_sum(up(dq))
            gh_ref[at, h * HEAD : (h + 1) * HEAD, 1:2] = lane_sum(up(dv))
        return carry

    lax.fori_loop(first, last, per_block, 0)


def attend_back_kernel(nc, hw, rw, info, e1_ref, o_ref, lse_ref, pd, left, right, qkv_in, *refs):
    pieces = refs[:10]
    dqkv_ref, gd_ref, gh_ref, do_ref, qkv_ref, p0, p1, q0, q1, go, don, ka, qa, va, oa, go_sem, in_sem = refs[10:]
    qkv_copy = move(qkv_in, qkv_ref, in_sem)

    def place(i):
        row = jnp.bitwise_xor(info[1], i // nc)
        return go.at[pl.ds(i % nc * hw, hw), pl.ds(pl.multiple_of(row * rw, rw), rw)]

    fetch(pieces, 4 * hw, ((3 * hw, 4 * hw, place, go_sem),))
    add_blocks(left, right, (p0, p1, q0, q1))
    for i in range(2 * nc):
        arrive(go.at[pl.ds(0, hw), pl.ds(0, rw)], go_sem.at[i])
    don[...] = dot(go[...], e1_ref[...], 1, 0)

    def emit(at, dx):
        do_ref[at, :] = dx.astype(bf16)

    norm_back(don, o_ref, pd, 8, gd_ref, emit)
    qkv_copy.wait()
    heads_back(0, nc // 2, hw, info, qkv_ref, lse_ref, o_ref, do_ref, dqkv_ref, gh_ref, ka, qa, va, oa)


def attend_back_rest_kernel(nc, hw, info, o_ref, qkv_ref, lse_ref, do_ref, dqkv_ref, gh_ref, ka, qa, va, oa):
    heads_back(nc // 2, nc, hw, info, qkv_ref, lse_ref, o_ref, do_ref, dqkv_ref, gh_ref, ka, qa, va, oa)


def input_back_kernel(nc, hw, rw, info, dqkv0, dqkv1, x_ref, dx1_ref, pd, *refs):
    pieces = refs[:10]
    outs_ref, gd_ref, ga, da, ga_sem = refs[10:]

    def place(i):
        row = jnp.bitwise_xor(info[1], i // nc)
        c = i % nc
        rows = pl.ds(c % 2 * 3 * hw, 3 * hw)
        return ga.at[c // 2, rows, pl.ds(pl.multiple_of(row * rw, rw), rw)]

    fetch(pieces, 4 * hw, ((0, 3 * hw, place, ga_sem),))
    for k, dqkv in enumerate((dqkv0, dqkv1)):
        for i in range(2 * nc):
            if i % nc // 2 == k:
                arrive(ga.at[0, pl.ds(0, 3 * hw), pl.ds(0, rw)], ga_sem.at[i])
        part = dot(ga[k], dqkv[...], 0, 0)
        da[...] = part if k == 0 else da[...] + part

    def emit(at, dx):
        apart(outs_ref, at, (dx1_ref[at, :] + dx).astype(bf16))

    norm_back(da, x_ref, pd, 0, gd_ref, emit)


def attend_grads_kernel(
    nc, hw, rw, fl, fw, info, dqkv0, dqkv1, a_ref, gd_in, gd_mid, gd_mix, gh0, gh1, gf_ref, keep, send,
    wide, thin, gh,
):
    my_row = info[1]
    gh[0:2] = gh0[...]
    gh[2:4] = gh1[...]
    lane = lax.broadcasted_iota(jnp.int32, (fl, 128), 1)

    def own(i, carry):
        at = pl.ds(pl.multiple_of(i * fl, fl), fl)
        tile = jnp.zeros((fl, 128), f32)
        for k, (ref, j) in enumerate(((gd_in, 0), (gd_in, 1), (gd_mid, 2), (gd_mid, 0), (gd_mid, 1), (gd_mid, 3))):
            tile = jnp.where(lane == k, ref[at, j : j + 1], tile)
        wide[at, :] = tile
        return carry

    lax.fori_loop(0, 2 * nc, own, 0)

    def columns(c, carry):
        tile = jnp.zeros((fl, 128), f32)
        at = 6
        for k in range(hw // fl):
            rows = slice(k * fl, (k + 1) * fl)
            deep = pl.ds(pl.multiple_of(c * hw + k * fl, fl), fl)
            for column in (gh[c, rows, 0:1], gh[c, rows, 1:2], gd_mix[deep, 0:1], gd_mix[deep, 1:2]):
                tile = jnp.where(lane == at, column, tile)
                at += 1
        for k in range(fw // fl):
            rows = slice(k * fl, (k + 1) * fl)
            for column in (gf_ref[c, rows, 2:3], gf_ref[c, rows, 0:1], gf_ref[c, rows, 1:2]):
                tile = jnp.where(lane == at, column, tile)
                at += 1
        thin[c] = tile
        return carry

    lax.fori_loop(0, nc, columns, 0)
    for k, dqkv in enumerate((dqkv0, dqkv1)):
        for ref, c in ((send, 1), (keep, 0)):
            grad = dot(dqkv[c * 3 * hw : (c + 1) * 3 * hw, :], a_ref[...], 1, 1).astype(bf16)
            for row in range(2):
                ref[jnp.bitwise_xor(my_row, row), k, 0 : 3 * hw, :] = grad[:, row * rw : (row + 1) * rw]
            for row in range(2):
                block = jnp.bitwise_xor(info[0], row * nc + 2 * k + c)
                tile = thin[2 * k + c] + wide[pl.ds(pl.multiple_of(block * fl, fl), fl), :]
                third = fl // 3
                tile = jnp.concatenate([tile[m * third : (m + 1) * third] for m in range(3)], axis=1)
                ref[row, k, 3 * hw :, :] = tile.astype(bf16)


def shrink_kernel(nc, rw, fw, info, pd, gn_ref, x1_ref, *refs):
    pieces = refs[:10]
    y_ref, gs, gs_sem = refs[10:]
    fetch(pieces, fw, ((0, fw, lambda i: gs.at[i // nc, pl.ds(i % nc * fw, fw)], gs_sem),))
    my_row = info[1]
    for i in range(2 * nc):
        arrive(gs.at[i // nc, pl.ds(i % nc * fw, fw)], gs_sem.at[i])
    for r in range(2):
        rows = slice(r * rw, (r + 1) * rw)
        part = dot(gs[jnp.bitwise_xor(my_row, r)], gn_ref[...], 0, 0)
        apart(y_ref, rows, (x1_ref[rows, :] + part + pd[rows, 5:6]).astype(bf16))


def body(
    tokens,
    cotangent,
    holder_of,
    lengths,
    input_gain,
    input_shift,
    attend_weight,
    attend_bias,
    mixed_gain,
    mixed_shift,
    output_weight,
    output_bias,
    middle_gain,
    middle_shift,
    expand_weight,
    expand_bias,
    hidden_gain,
    hidden_shift,
    shrink_weight,
    shrink_bias,
):
    holders = lax.axis_size("dp")
    half = holders // 2
    nr, nc = lax.axis_size("row"), lax.axis_size("col")
    n = nr * nc
    micro = holder_of.shape[0]
    assert micro == n and nr == 2 and nc == 4
    fl = tokens.shape[0]
    pairs = micro * half
    blk = tokens.shape[1] // pairs
    unit = half * blk
    dp = lax.axis_index("dp")
    side, pos = dp // half, dp % half
    my_row, my_col = lax.axis_index("row"), lax.axis_index("col")
    rc = my_row * nc + my_col
    groups = [list(range(s * half * n, (s + 1) * half * n)) for s in range(2)]
    hw, rw, fw = output_weight.shape[0], output_weight.shape[1], shrink_weight.shape[0]

    def flip_row(v):
        return lax.ppermute(v, "row", [(i, i ^ 1) for i in range(nr)])

    def flip_chip(v):
        return lax.ppermute(v, "col", [(i, i ^ 2) for i in range(nc)])

    def flip_core(v):
        return lax.ppermute(v, "col", [(i, i ^ 1) for i in range(nc)])

    def flip_dp(v, step):
        return lax.ppermute(v, "dp", [(i, i ^ step) for i in range(holders)])

    def exchange(v):
        return lax.all_to_all(v, ("dp",) + RC, 0, 0, axis_index_groups=groups, tiled=True)

    lanes = blk % 128 == 0

    def by_target(v):
        v = jnp.transpose(v.reshape(2, fl, half * n, blk), (2, 0, 1, 3))
        return v.reshape(half * n, 2 * fl, blk)

    def exchange_units(v):
        v = exchange(v).reshape(half, n, 2 * fl, blk)
        return v if lanes else jnp.transpose(v, (1, 2, 0, 3)).reshape(1, n, 2 * fl, unit)

    def from_unit(v):
        if not lanes:
            v = jnp.transpose(v.reshape(n * fl, half, blk), (1, 0, 2))
        v = exchange(v.reshape(half * n, fl, blk))
        return jnp.transpose(v, (1, 0, 2)).reshape(tokens.shape)

    def tie(*values):
        return lax.optimization_barrier(values)

    def near(v):
        return flip_row(v), flip_chip(v)

    def far(v, by_row, by_chip):
        h = v.shape[0] // 2
        return flip_row(by_chip[:h]), flip_chip(by_row[h:])

    def near_flips(v, near_v):
        return tuple(flip_core(p) for p in (v, near_v[1], near_v[0]))

    def pieces_of(v, near_v, flips, far_v):
        v1, c1, r1 = flips
        f1, g1 = (flip_core(p) for p in far_v)
        return (v, v1, near_v[1], c1, near_v[0], r1, far_v[0], far_v[1], f1, g1)

    w1 = jnp.concatenate([attend_weight.reshape(3 * hw, rw), output_weight], axis=0)
    near1 = near(w1)
    tile = jnp.concatenate(
        [
            jnp.stack([input_gain, input_shift, output_bias, middle_gain, middle_shift, shrink_bias]),
            jnp.transpose(
                jnp.stack([attend_bias[0], attend_bias[1], mixed_gain, mixed_shift]).reshape(4, -1, fl), (1, 0, 2)
            ).reshape(-1, fl),
            jnp.transpose(jnp.stack([expand_bias, hidden_gain, hidden_shift]).reshape(3, -1, fl), (1, 0, 2)).reshape(-1, fl),
        ]
    )
    tile = jnp.transpose(jnp.pad(tile, ((0, 128 - tile.shape[0]), (0, 0))))
    tile_row, tile_chip = near(tile)
    ready = by_target(jnp.concatenate([tokens, cotangent], axis=0))
    near1, tile_row, tile_chip, ready = tie(near1, tile_row, tile_chip, ready)
    far1 = far(w1, *near1)
    both = exchange_units(ready)
    even = jnp.stack([tile, tile_chip, tile_row, flip_row(tile_chip)])
    odd = flip_core(even)
    flips1 = near_flips(w1, near1)
    far1, flips1, both, odd, w2 = tie(far1, flips1, both, odd, expand_weight)
    near2 = near(w2)
    g1 = pieces_of(w1, near1, flips1, far1)

    k_unit = 2 * (pos * n + rc) + side
    own = lengths[k_unit // holders, holder_of[k_unit // holders, k_unit % holders]]
    info = jnp.concatenate([jnp.stack([rc, my_row]), jnp.cumsum(own)[:-1]]).astype(jnp.int32)

    d = n * fl
    split = lambda v: v.reshape(nr, rw, unit)
    dma = pltpu.SemaphoreType.DMA
    weight_flops = 2 * unit * d * nc * fw

    dp_odd = dp % 2 == 1

    def reduce_rest(v):
        step = 2
        while 2 * step < holders:
            v = v + flip_dp(v, step)
            step *= 2
        return v, flip_dp(v, step) if step < holders else jnp.zeros_like(v)

    def spread(v):
        return v, flip_dp(v, 1)

    def whole(v, got):
        return jnp.concatenate([jnp.where(dp_odd, got, v), jnp.where(dp_odd, v, got)], axis=0).astype(f32)

    vm = lambda shape, dtype=bf16: pltpu.VMEM(shape, dtype)
    act, act32, hid = (d, unit), (nc * hw, unit), (nc, fw, unit)
    part1, part2, part3 = (nr, nc // 2, 4 * hw, rw), (nr, nc // 2, rw, fw), (nr, nc // 2, fw, rw)

    def time_us(t):
        return dict(flops=int(t * 1e9), moved=int(t * 1e6))

    extra = vm((HEAD + 16, unit))
    x, a, qkv, lse, o, pd, pf = call(
        functools.partial(attend_kernel, nc, hw, rw, fl, fw),
        (
            sds(act, bf16), sds(act, bf16), sds((nc, 3 * hw, unit), bf16), sds((nc, 8, unit), f32), sds(act, f32),
            sds((d, 16), f32), sds((nc, fw, 8), f32),
        ),
        [SMEM] + [VMEM] * 3 + [HBM] * 10,
        [VMEM, VMEM, HBM, VMEM, VMEM, VMEM, VMEM],
        [
            vm((nc, 3 * hw, unit)), vm((nc, 3 * hw, nr * rw)), extra, extra,
            dma((n,)), dma((nc,)),
        ],
        **time_us(13), name="attend",
    )(info, both, even, odd, *g1)

    o, near2 = tie(o, near2)
    far2 = far(w2, *near2)
    flips2 = near_flips(w2, near2)

    on, x1, b = call(
        functools.partial(output_kernel, nc, hw, rw),
        (sds(act, bf16), sds(act, f32), sds(act, bf16)),
        [SMEM] + [VMEM] * 3 + [HBM] * 10,
        [VMEM] * 3,
        [vm((nr, nc * hw, rw)), dma((n,))],
        **time_us(5), name="output",
    )(info, x, o, pd, *g1)

    b, far2, flips2, w3 = tie(b, far2, flips2, shrink_weight)
    near3 = near(w3)
    g2 = pieces_of(w2, near2, flips2, far2)

    gn, vh, slope, st = call(
        functools.partial(expand_kernel, nc, rw, fw),
        (sds(hid, bf16), sds(hid, bf16), sds(hid, bf16), sds((8, unit), f32)),
        [SMEM, VMEM, VMEM] + [HBM] * 10,
        [VMEM, HBM, HBM, VMEM],
        [vm(hid), vm(hid), vm(hid, f32), vm((nc, nr * rw, fw)), dma((n,)), dma((2 * nc,))],
        **time_us(13), name="expand",
    )(info, b, pf, *g2)

    gn, near3 = tie(gn, near3)
    far3 = far(w3, *near3)
    flips3 = near_flips(w3, near3)

    e2, shr_keep, shr_send = call(
        functools.partial(shrink_grads_kernel, nc, rw),
        (sds(act, bf16), sds(part3, bf16), sds(part3, bf16)),
        [SMEM] + [VMEM] * 2,
        [VMEM] * 3,
        **time_us(7), name="shrink_grads",
    )(info, gn, both)

    shr_send, far3, flips3 = tie(shr_send, far3, flips3)
    g3 = pieces_of(w3, near3, flips3, far3)
    shr_got = flip_core(shr_send)

    def reduce_near(v):
        return flip_row(v[1]), flip_chip(v[3])

    def reduce_far(v, got):
        p, q = v[0] + got[0], v[2] + got[1]
        return (p[0], q[0]), (flip_chip(p[1]), flip_row(q[1]))

    def reduce_dp(v, got):
        p, q = v[0] + got[0], v[1] + got[1]
        return jnp.where(dp_odd, q, p), flip_dp(jnp.where(dp_odd, p, q), 1)

    sum3 = (nc // 2, fw // 2, rw)
    df, gf, *shr = call(
        functools.partial(hidden_back_kernel, nc, rw, fw),
        (sds(hid, bf16), sds((nc, fw, 8), f32)) + (sds(sum3, bf16),) * 4,
        [SMEM] + [VMEM] * 5 + [HBM] * 12,
        [VMEM] * 6,
        [vm(hid), vm(hid), vm((nc, fw, nr * rw)), vm(hid, f32), dma((n,)), dma((nc,)), dma((nc,))],
        **time_us(13), name="hidden_back",
    )(info, st, e2, pf, shr_keep, shr_got, vh, slope, *g3)

    shr_near = reduce_near(shr)

    dx1, e1, gd_mid = call(
        functools.partial(middle_back_kernel, nc, rw, fw),
        (sds(act, f32), sds(act, bf16), sds((d, 8), f32)),
        [SMEM] + [VMEM] * 4 + [HBM] * 10,
        [VMEM] * 3,
        [vm((nc, nr * rw, fw)), vm(act, f32), dma((n,))],
        **time_us(8), name="middle_back",
    )(info, df, x1, e2, pd, *g2)

    rows2 = 2 * rw + hw
    part2 = (nr, nc // 2, rows2, rw)
    sum2 = (nc // 2, rows2 // 2, rw)
    mid_keep, mid_send = call(
        functools.partial(middle_grads_kernel, nc, hw, rw, fw),
        (sds(part2, bf16), sds(part2, bf16)),
        [SMEM] + [VMEM] * 4,
        [VMEM] * 2,
        **time_us(7), name="middle_grads",
    )(info, b, df, on.reshape(nc, hw, unit), e1)

    e1, mid_send, shr_near = tie(e1, mid_send, shr_near)
    mid_got = flip_core(mid_send)
    shr_stay, shr_far = reduce_far(shr, shr_near)

    half_heads = (nc // 2 * 3 * hw, unit)
    dqkv0, gd_mix, gh0, do, qkv, *mid = call(
        functools.partial(attend_back_kernel, nc, hw, rw),
        (sds(half_heads, bf16), sds((d, 8), f32), sds((nc // 2, hw, 8), f32), sds(act, bf16), sds(qkv.shape, bf16))
        + (sds(sum2, bf16),) * 4,
        [SMEM] + [VMEM] * 6 + [HBM] * 11,
        [VMEM] * 9,
        [vm((nc * hw, nr * rw)), vm(act, f32), extra, extra, extra, extra, dma((n,)), dma(())],
        **time_us(11), name="attend_back",
    )(info, e1, o, lse, pd, mid_keep, mid_got, qkv, *g1)

    do, shr_far, mid = tie(do, shr_far, mid)
    shr, shr_dp = reduce_dp(shr_stay, shr_far)
    mid_near = reduce_near(mid)

    dqkv1, gh1 = call(
        functools.partial(attend_back_rest_kernel, nc, hw),
        (sds(half_heads, bf16), sds((nc // 2, hw, 8), f32)),
        [SMEM] + [VMEM] * 4,
        [VMEM] * 2,
        [extra, extra, extra, extra],
        **time_us(8), name="attend_back_rest",
    )(info, o, qkv, lse, do)

    dqkv1, shr_dp = tie(dqkv1, shr_dp)
    shr, shr_rest = reduce_rest(shr + shr_dp)

    input_grad, gd_in = call(
        functools.partial(input_back_kernel, nc, hw, rw),
        (sds((half if lanes else 1, d, blk if lanes else unit), bf16), sds((d, 8), f32)),
        [SMEM] + [VMEM] * 5 + [HBM] * 10,
        [VMEM] * 2,
        [vm((2, nc // 2 * 3 * hw, nr * rw)), vm(act, f32), dma((n,))],
        **time_us(7), name="input_back",
    )(info, dqkv0, dqkv1, x, dx1, pd, *g1)

    gd_in, mid_near = tie(gd_in, mid_near)
    mid_stay, mid_far = reduce_far(mid, mid_near)

    rows1 = 3 * hw + fl // 3
    part1 = (nr, nc // 2, rows1, rw)
    att_keep, att_send = call(
        functools.partial(attend_grads_kernel, nc, hw, rw, fl, fw),
        (sds(part1, bf16), sds(part1, bf16)),
        [SMEM] + [VMEM] * 9,
        [VMEM] * 2,
        [vm((d, 128), f32), vm((nc, fl, 128), f32), vm((nc, hw, 8), f32)],
        **time_us(7), name="attend_grads",
    )(info, dqkv0, dqkv1, a, gd_in, gd_mid, gd_mix, gh0, gh1, gf)

    att_send, shr_rest, mid_far = tie(att_send, shr_rest, mid_far)
    att_got = flip_core(att_send)
    mid, mid_dp = reduce_dp(mid_stay, mid_far)
    shr, shr_got = spread(shr + shr_rest)
    h = rows1 // 2
    p1, q1 = att_keep[1, :, :h] + att_got[1, :, :h], att_keep[:, 1, h:] + att_got[:, 1, h:]
    p1, q1, y_in = tie(p1, q1, gn)
    p_row, q_chip = flip_row(p1), flip_chip(q1)

    y = call(
        functools.partial(shrink_kernel, nc, rw, fw),
        sds(input_grad.shape, bf16),
        [SMEM] + [VMEM] * 3 + [HBM] * 10,
        VMEM,
        [vm((nr, nc * fw, rw)), dma((n,))],
        **time_us(8), name="shrink",
    )(info, pd, y_in.reshape(nc * fw, unit), x1, *g3)

    y, mid_dp, shr_got, input_grad = tie(y, mid_dp, shr_got, input_grad)
    mid, mid_rest = reduce_rest(mid + mid_dp)
    mid, p_row, q_chip = tie(mid, p_row, q_chip)
    p = att_keep[0, :, :h] + att_got[0, :, :h] + p_row
    q = att_keep[:, 0, h:] + att_got[:, 0, h:] + q_chip
    att_far = flip_chip(p[1]), flip_row(q[1])
    input_grad = from_unit(input_grad)
    att, att_dp = reduce_dp((p[0], q[0]), att_far)
    att_dp, mid_rest, y = tie(att_dp, mid_rest, y)
    block_out = from_unit(y)
    att, att_rest = reduce_rest(att + att_dp)
    mid, mid_got = spread(mid + mid_rest)
    att, att_got = spread(att + att_rest)
    att_got, mid_got, shr_got = tie(att_got, mid_got, shr_got)
    att, mid, shr_w_g = whole(att, att_got), whole(mid, mid_got), whole(shr, shr_got)
    exp_w_g = jnp.concatenate([mid[:rw], mid[rw : 2 * rw]], axis=1)

    thin = att[3 * hw :]
    thin = jnp.transpose(jnp.concatenate([thin[:, k * 128 : (k + 1) * 128] for k in range(3)], axis=0))
    in_g_g, in_s_g, out_b_g, mid_g_g, mid_s_g, shr_b_g = (thin[i] for i in range(6))
    at = 6 + 4 * (hw // fl)
    heads_g = jnp.transpose(thin[6:at].reshape(-1, 4, fl), (1, 0, 2)).reshape(4, hw)
    hidden_g = jnp.transpose(thin[at : at + 3 * (fw // fl)].reshape(-1, 3, fl), (1, 0, 2)).reshape(3, fw)
    q_b_g, v_b_g, mix_g_g, mix_s_g = heads_g
    exp_b_g, hid_g_g, hid_s_g = hidden_g
    return (
        block_out,
        input_grad,
        in_g_g,
        in_s_g,
        att[: 3 * hw].reshape(attend_weight.shape),
        jnp.stack([q_b_g, v_b_g]),
        mix_g_g,
        mix_s_g,
        mid[2 * rw :],
        out_b_g,
        mid_g_g,
        mid_s_g,
        exp_w_g,
        exp_b_g,
        hid_g_g,
        hid_s_g,
        shr_w_g,
        shr_b_g,
    )


def solution(mesh):
    wide, narrow = P(RC), P("col")
    in_specs = (
        P(RC, "dp"), P(RC, "dp"), P(), P(), wide, wide, P(None, "col", "row"), P(None, "col"),
        narrow, narrow, P("col", "row"), wide, wide, wide, P("row", "col"), narrow, narrow, narrow,
        P("col", "row"), wide,
    )
    out_specs = (
        P(RC, "dp"), P(RC, "dp"), wide, wide, P(None, "col", "row"), P(None, "col"), narrow, narrow,
        P("col", "row"), wide, wide, wide, P("row", "col"), narrow, narrow, narrow, P("col", "row"),
        wide,
    )
    return jax.shard_map(body, mesh=mesh, in_specs=in_specs, out_specs=out_specs, check_vma=False)
```

```python
import functools
import math

import jax
import jax.numpy as jnp
from jax import lax
from jax.experimental import pallas as pl
from jax.experimental.pallas import tpu as pltpu
from jax.sharding import PartitionSpec as P

HEAD = 64
eps = 1e-05
masked_score = -1e30
f32 = jnp.float32
bf16 = jnp.bfloat16
RC = ("row", "col")
HBM = pl.BlockSpec(memory_space=pltpu.HBM)
SMEM = pl.BlockSpec(memory_space=pltpu.SMEM)
VMEM = pl.BlockSpec(memory_space=pltpu.VMEM)
root_half = math.sqrt(0.5)
root_tau = 1.0 / math.sqrt(2.0 * math.pi)
score_scale = 1.0 / math.sqrt(HEAD)


def dot(a, b, ca, cb):
    return lax.dot_general(a, b, (((ca,), (cb,)), ((), ())), preferred_element_type=f32)


def up(v):
    return v.astype(f32)


def lane_sum(v):
    return jnp.sum(v, axis=1, keepdims=True)


def token_sum(v):
    return jnp.sum(v, axis=0, keepdims=True)


CHUNK = 768
ROOM = 8


def over(rows, step, init=0, chunk=CHUNK):
    def one(i, carry):
        return step(pl.ds(pl.multiple_of(i * chunk, chunk), chunk), carry)

    return lax.fori_loop(0, rows // chunk, one, init)


def moments(ref, chunk=CHUNK):
    rows, unit = ref.shape
    zero = jnp.zeros((1, unit), f32)
    mu = over(rows, lambda at, s: s + token_sum(up(ref[at, :])), zero, chunk) * (1.0 / rows)

    def square(at, s):
        d = up(ref[at, :]) - mu
        return s + token_sum(d * d)

    return mu, lax.rsqrt(over(rows, square, zero, chunk) * (1.0 / rows) + eps)


def norm(out, ref, pd, gain, shift):
    mu, r = moments(ref, CHUNK // 2)

    def one(at, carry):
        out[at, :] = ((up(ref[at, :]) - mu) * r * pd[at, gain : gain + 1] + pd[at, shift : shift + 1]).astype(bf16)
        return carry

    over(ref.shape[0], one, chunk=CHUNK // 2)


def norm_back(grad, ref, pd, gain, gd, emit):
    rows, unit = ref.shape
    mu, r = moments(ref, CHUNK // 2)
    zero = jnp.zeros((1, unit), f32)

    def first(at, s):
        g = grad[at, :]
        gv = g * ((up(ref[at, :]) - mu) * r)
        gd[at, 0:1] = lane_sum(gv)
        gd[at, 1:2] = lane_sum(g)
        k = pd[at, gain : gain + 1]
        return s[0] + token_sum(g * k), s[1] + token_sum(gv * k)

    m1, m2 = over(rows, first, (zero, zero))
    m1, m2 = m1 * (1.0 / rows), m2 * (1.0 / rows)

    def second(at, carry):
        vh = (up(ref[at, :]) - mu) * r
        emit(at, r * (grad[at, :] * pd[at, gain : gain + 1] - m1 - vh * m2))
        return carry

    over(rows, second)


PIECES = ((0, None), (1, None), (2, None), (3, None), (4, None), (5, None), (6, 0), (6, 1), (7, 0), (7, 1))


def fetch(pieces, rows, parts):
    for ref, (block, half) in zip(pieces, PIECES):
        first, last = (0, rows) if half is None else (half * rows // 2, (half + 1) * rows // 2)
        for lo, hi, place, sem in parts:
            a, b = max(lo, first), min(hi, last)
            if a < b:
                pltpu.make_async_copy(
                    ref.at[pl.ds(a - first, b - a)], place(block).at[pl.ds(a - lo, b - a)], sem.at[block]
                ).start()


def arrive(ref, sem):
    pltpu.make_async_copy(ref, ref, sem).wait()


def move(src, dst, sem):
    copy = pltpu.make_async_copy(src, dst, sem)
    copy.start()
    return copy


def vmem_bytes(shape, dtype):
    size = jnp.dtype(dtype).itemsize
    sublanes, lanes = 32 // size, 128
    *lead, rows, columns = (1,) * max(0, 2 - len(shape)) + tuple(shape)
    return math.prod(lead) * (-(-rows // sublanes) * sublanes) * (-(-columns // lanes) * lanes) * size


def pinned(spec):
    return pltpu.VMEM if spec is VMEM else pltpu.HBM


def call(kernel, outs, in_specs, out_specs, scratch=(), flops=0, moved=0, name=None, aliases=None):
    held = [v for v in scratch if v.memory_space == pltpu.VMEM]
    limit = sum(vmem_bytes(v.shape, v.dtype) for v in held) + (ROOM << 20)
    single = not isinstance(outs, tuple)
    places = [pinned(spec)(v.shape, v.dtype) for v, spec in zip((outs,) if single else outs, (out_specs,) if single else out_specs)]

    def run(*args):
        args = [v if spec is SMEM else pltpu.with_memory_space_constraint(v, pinned(spec)) for v, spec in zip(args, in_specs)]
        return pl.pallas_call(
            kernel,
            out_shape=places[0] if single else tuple(places),
            in_specs=in_specs,
            out_specs=out_specs,
            scratch_shapes=list(scratch),
            compiler_params=pltpu.CompilerParams(vmem_limit_bytes=limit),
            cost_estimate=pl.CostEstimate(flops=flops, bytes_accessed=moved, transcendentals=0),
            name=name,
            input_output_aliases=aliases or {},
        )(*args)

    return run


def sds(shape, dtype):
    return jax.ShapeDtypeStruct(shape, dtype)


def segment_rows(info, unit):
    t = lax.broadcasted_iota(jnp.int32, (16, unit), 1)
    slot = lax.broadcasted_iota(jnp.int32, (16, unit), 0)
    one = lambda b: jnp.where(t >= b, 1, 0)
    seg = one(info[2]) + one(info[3]) + one(info[4])
    same = seg == slot
    for_keys = jnp.where(same, 1.0, 0.0)
    for_queries = jnp.where(jnp.logical_and(slot < 4, jnp.logical_not(same)), masked_score, 0.0)
    return for_keys, for_queries


def split3(v):
    hi = v.astype(bf16)
    v = v - up(hi)
    mid = v.astype(bf16)
    return hi, mid, (v - up(mid)).astype(bf16)


def three_rows(base, v, first):
    row = lax.broadcasted_iota(jnp.int32, base.shape, 0)
    for i, part in enumerate(split3(v)):
        base = jnp.where(row == first + i, up(part), base)
    return base


def unit_of(ref, which):
    blocks, n, rows, _ = ref.shape
    rows //= 2
    return jnp.concatenate(
        [
            jnp.concatenate([ref[k, i, which * rows : (which + 1) * rows, :] for i in range(n)], axis=0)
            for k in range(blocks)
        ],
        axis=1,
    )


def apart(ref, at, value):
    width = ref.shape[2]
    for i in range(ref.shape[0]):
        ref[i, at, :] = value[:, i * width : (i + 1) * width]


def beside(ref, info, nc, rw):
    def place(i):
        row = jnp.bitwise_xor(info[1], i // nc)
        return ref.at[i % nc, :, pl.ds(pl.multiple_of(row * rw, rw), rw)]

    return place


def below(ref, info, nc, rw):
    def place(i):
        row = jnp.bitwise_xor(info[1], i // nc)
        return ref.at[i % nc, pl.ds(pl.multiple_of(row * rw, rw), rw)]

    return place


def attend_kernel(nc, hw, rw, fl, fw, info, both, even, odd, *refs):
    pieces = refs[:10]
    x_ref, a_ref, qkv_out, lse_ref, o_ref, pd, pf = refs[10:17]
    qkv_ref, ga, ka, qa, ga_sem, out_sem = refs[17:]
    unit = o_ref.shape[1]
    fetch(pieces, 4 * hw, ((0, 3 * hw, beside(ga, info, nc, rw), ga_sem),))
    for i in range(2 * nc):
        tile = (even, odd)[i % 2][i // 2]
        pd[pl.ds(pl.multiple_of(jnp.bitwise_xor(info[0], i) * fl, fl), fl), 0:6] = tile[:, 0:6]
        if i < nc:
            for k in range(hw // fl):
                pd[i * hw + k * fl : i * hw + (k + 1) * fl, 6:10] = tile[:, 6 + 4 * k : 10 + 4 * k]
            for k in range(fw // fl):
                first = 6 + 4 * (hw // fl) + 3 * k
                pf[i, k * fl : (k + 1) * fl, 0:3] = tile[:, first : first + 3]
    x_ref[...] = unit_of(both, 0)
    norm(a_ref, x_ref, pd, 0, 1)
    for_keys, for_queries = segment_rows(info, unit)
    ka[HEAD:, :] = for_keys.astype(bf16)
    qa[HEAD:, :] = for_queries.astype(bf16)

    def per_block(c, carry):
        for i in (c, nc + c):
            arrive(ga.at[c, :, pl.ds(0, rw)], ga_sem.at[i])
        trip = dot(ga[c], a_ref[...], 1, 0)
        at = pl.multiple_of(c * hw, hw)
        qkv_ref[c, 0:hw, :] = (trip[0:hw] + pd[pl.ds(at, hw), 6:7]).astype(bf16)
        qkv_ref[c, hw : 2 * hw, :] = trip[hw : 2 * hw].astype(bf16)
        qkv_ref[c, 2 * hw :, :] = (trip[2 * hw :] + pd[pl.ds(at, hw), 7:8]).astype(bf16)
        move(qkv_ref.at[c], qkv_out.at[c], out_sem.at[c])
        for h in range(hw // HEAD):
            qa[0:HEAD, :] = qkv_ref[c, h * HEAD : (h + 1) * HEAD, :] * jnp.bfloat16(score_scale)
            ka[0:HEAD, :] = qkv_ref[c, hw + h * HEAD : hw + (h + 1) * HEAD, :]
            v = qkv_ref[c, 2 * hw + h * HEAD : 2 * hw + (h + 1) * HEAD, :]
            s = dot(ka[...], qa[...], 0, 0)
            top = jnp.max(s, axis=0, keepdims=True)
            e = jnp.exp(s - top)
            den = token_sum(e)
            o = dot(v, e.astype(bf16), 1, 0) * (1.0 / den)
            o_ref[pl.ds(pl.multiple_of(c * hw + h * HEAD, HEAD), HEAD), :] = o
            lse_ref[c, h : h + 1, :] = top + jnp.log(den)
        return carry

    lax.fori_loop(0, nc, per_block, 0)
    for c in range(nc):
        arrive(qkv_ref.at[c], out_sem.at[c])


def output_kernel(nc, hw, rw, info, x_ref, o_ref, pd, *refs):
    pieces = refs[:10]
    on_ref, x1_ref, b_ref, go, go_sem = refs[10:]
    fetch(pieces, 4 * hw, ((3 * hw, 4 * hw, lambda i: go.at[i // nc, pl.ds(i % nc * hw, hw)], go_sem),))
    my_row = info[1]
    norm(on_ref, o_ref, pd, 8, 9)
    for i in range(2 * nc):
        arrive(go.at[i // nc, pl.ds(i % nc * hw, hw)], go_sem.at[i])

    def one(r, carry):
        rows = pl.ds(pl.multiple_of(r * rw, rw), rw)
        x1_ref[rows, :] = dot(go[jnp.bitwise_xor(my_row, r)], on_ref[...], 0, 0) + up(x_ref[rows, :]) + pd[rows, 2:3]
        return carry

    lax.fori_loop(0, 2, one, 0)
    norm(b_ref, x1_ref, pd, 3, 4)


def expand_kernel(nc, rw, fw, info, b_ref, pf, *refs):
    pieces = refs[:10]
    gn_ref, vh_out, slope_out, st_ref = refs[10:14]
    vh_ref, slope_ref, g_ref, ge, ge_sem, out_sem = refs[14:]
    fetch(pieces, rw, ((0, rw, below(ge, info, nc, rw), ge_sem),))
    unit = b_ref.shape[1]
    total = nc * fw

    def first(c, s):
        for i in (c, nc + c):
            arrive(ge.at[c, pl.ds(0, rw)], ge_sem.at[i])
        f = dot(ge[c], b_ref[...], 0, 0) + pf[c, :, 0:1]
        phi = 0.5 * (1.0 + lax.erf(f * root_half))
        g = f * phi
        g_ref[c] = g
        slope_ref[c] = (phi + f * (jnp.exp(-0.5 * f * f) * root_tau)).astype(bf16)
        move(slope_ref.at[c], slope_out.at[c], out_sem.at[c])
        return s + token_sum(g)

    mu = lax.fori_loop(0, nc, first, jnp.zeros((1, unit), f32)) * (1.0 / total)

    def second(c, s):
        def square(at, t):
            d = g_ref[c, at, :] - mu
            return t + token_sum(d * d)

        return over(fw, square, s)

    r = lax.rsqrt(lax.fori_loop(0, nc, second, jnp.zeros((1, unit), f32)) * (1.0 / total) + eps)
    st_ref[...] = jnp.broadcast_to(r, st_ref.shape)

    def third(c, carry):
        def one(at, t):
            vh = (g_ref[c, at, :] - mu) * r
            vh_ref[c, at, :] = vh.astype(bf16)
            gn_ref[c, at, :] = (vh * pf[c, at, 1:2] + pf[c, at, 2:3]).astype(bf16)
            return t

        over(fw, one)
        move(vh_ref.at[c], vh_out.at[c], out_sem.at[nc + c])
        return carry

    lax.fori_loop(0, nc, third, 0)
    for c in range(nc):
        arrive(slope_ref.at[c], out_sem.at[c])
        arrive(vh_ref.at[c], out_sem.at[nc + c])


def store_blocks(nc, blocks, keep, send):
    def one(k, carry):
        for ref, c in ((send, 2 * k + 1), (keep, 2 * k)):
            blocks(c, lambda row: ref.at[row, k])
        return carry

    lax.fori_loop(0, nc // 2, one, 0)


def shrink_grads_kernel(nc, rw, info, gn_ref, both, e2_ref, keep, send):
    my_row = info[1]
    e2_ref[...] = unit_of(both, 1)

    def blocks(c, place):
        grad = dot(gn_ref[c], e2_ref[...], 1, 1).astype(bf16)
        for r in range(2):
            place(jnp.bitwise_xor(my_row, r))[...] = grad[:, r * rw : (r + 1) * rw]

    store_blocks(nc, blocks, keep, send)


def add_blocks(left, right, outs):
    h = left.shape[2] // 2
    for j in range(4):
        r, c = j // 2, j % 2
        outs[r][c] = (up(left[r, c, :h]) + up(right[r, c, :h])).astype(bf16)
        outs[2 + c][r] = (up(left[r, c, h:]) + up(right[r, c, h:])).astype(bf16)


def hidden_back_kernel(nc, rw, fw, info, st_ref, e2_ref, pf, left, right, vh_in, slope_in, *refs):
    pieces = refs[:10]
    df_ref, gf_ref, p0, p1, q0, q1 = refs[10:16]
    vh_ref, slope_ref, gs, dgn, gs_sem, vh_sem, slope_sem = refs[16:]
    fetch(pieces, fw, ((0, fw, beside(gs, info, nc, rw), gs_sem),))
    for c in range(nc):
        move(vh_in.at[c], vh_ref.at[c], vh_sem.at[c])
    for c in range(nc):
        move(slope_in.at[c], slope_ref.at[c], slope_sem.at[c])
    add_blocks(left, right, (p0, p1, q0, q1))
    r = st_ref[0:1, :]
    unit = e2_ref.shape[1]
    total = nc * fw

    def first(c, s):
        for i in (c, nc + c):
            arrive(gs.at[c, :, pl.ds(0, rw)], gs_sem.at[i])
        arrive(vh_ref.at[c], vh_sem.at[c])
        dgn[c] = dot(gs[c], e2_ref[...], 1, 0)

        def one(at, t):
            d = dgn[c, at, :]
            dv = d * up(vh_ref[c, at, :])
            gf_ref[c, at, 0:1] = lane_sum(dv)
            gf_ref[c, at, 1:2] = lane_sum(d)
            gain = pf[c, at, 1:2]
            return t[0] + token_sum(d * gain), t[1] + token_sum(dv * gain)

        return over(fw, one, s)

    zero = jnp.zeros((1, unit), f32)
    m1, m2 = lax.fori_loop(0, nc, first, (zero, zero))
    m1, m2 = m1 * (1.0 / total), m2 * (1.0 / total)

    def second(c, carry):
        arrive(slope_ref.at[c], slope_sem.at[c])

        def one(at, t):
            dg = r * (dgn[c, at, :] * pf[c, at, 1:2] - m1 - up(vh_ref[c, at, :]) * m2)
            df = (dg * up(slope_ref[c, at, :])).astype(bf16)
            df_ref[c, at, :] = df
            gf_ref[c, at, 2:3] = lane_sum(up(df))
            return t

        over(fw, one)
        return carry

    lax.fori_loop(0, nc, second, 0)


def middle_back_kernel(nc, rw, fw, info, df_ref, x1_ref, e2_ref, pd, *refs):
    pieces = refs[:10]
    dx1_ref, e1_ref, gd_ref, ge, db, ge_sem = refs[10:]
    fetch(pieces, rw, ((0, rw, below(ge, info, nc, rw), ge_sem),))
    db[...] = jnp.zeros(db.shape, f32)

    def one(c, carry):
        for i in (c, nc + c):
            arrive(ge.at[c, pl.ds(0, rw)], ge_sem.at[i])
        db[...] += dot(ge[c], df_ref[c], 1, 0)
        return carry

    lax.fori_loop(0, nc, one, 0)

    def emit(at, dx):
        dy = up(e2_ref[at, :])
        dx1 = dy + dx
        dx1_ref[at, :] = dx1
        e1 = dx1.astype(bf16)
        e1_ref[at, :] = e1
        gd_ref[at, 2:3] = lane_sum(up(e1))
        gd_ref[at, 3:4] = lane_sum(dy)

    norm_back(db, x1_ref, pd, 3, gd_ref, emit)


def middle_grads_kernel(
    nc, hw, rw, fw, info, b_ref, df_ref, on_ref, e1_ref, keep, send,
):
    my_row = info[1]

    def blocks(c, place):
        grad = dot(b_ref[...], df_ref[c], 1, 1).astype(bf16)
        out_grad = dot(on_ref[c], e1_ref[...], 1, 1).astype(bf16)
        half = fw // 2
        for r in range(2):
            ref = place(jnp.bitwise_xor(my_row, r))
            for k in range(2):
                ref[k * rw : (k + 1) * rw, :] = grad[r * rw : (r + 1) * rw, k * half : (k + 1) * half]
            ref[2 * rw :, :] = out_grad[:, r * rw : (r + 1) * rw]

    store_blocks(nc, blocks, keep, send)


def heads_back(first, last, hw, info, qkv_ref, lse_ref, o_ref, do_ref, dqkv_ref, gh_ref, ka, qa, va, oa):
    unit = o_ref.shape[1]
    for_keys, for_queries = segment_rows(info, unit)
    slot = lax.broadcasted_iota(jnp.int32, (16, unit), 0)
    ka[HEAD:, :] = jnp.where(jnp.logical_and(slot >= 4, slot < 7), 1.0, for_keys).astype(bf16)
    va[HEAD:, :] = jnp.where(slot < 3, 1.0, 0.0).astype(bf16)
    nothing = jnp.zeros((16, unit), f32)

    def per_block(c, carry):
        to = lambda j, h: pl.ds(pl.multiple_of(c * 3 * hw + j * hw + h * HEAD, HEAD), HEAD)
        for h in range(hw // HEAD):
            rows = pl.ds(pl.multiple_of(c * hw + h * HEAD, HEAD), HEAD)
            q = qkv_ref[c, h * HEAD : (h + 1) * HEAD, :] * jnp.bfloat16(score_scale)
            k = qkv_ref[c, hw + h * HEAD : hw + (h + 1) * HEAD, :]
            d = do_ref[rows, :]
            inner = jnp.sum(up(d) * o_ref[rows, :], axis=0, keepdims=True)
            qa[0:HEAD, :] = q
            qa[HEAD:, :] = three_rows(for_queries, -lse_ref[c, h : h + 1, :], 4).astype(bf16)
            ka[0:HEAD, :] = k
            va[0:HEAD, :] = qkv_ref[c, 2 * hw + h * HEAD : 2 * hw + (h + 1) * HEAD, :]
            oa[0:HEAD, :] = d
            oa[HEAD:, :] = three_rows(nothing, -inner, 0).astype(bf16)
            p = jnp.exp(dot(ka[...], qa[...], 0, 0))
            ds = (p * dot(va[...], oa[...], 0, 0)).astype(bf16)
            dv = dot(d, p.astype(bf16), 1, 1).astype(bf16)
            dq = (dot(k, ds, 1, 0) * score_scale).astype(bf16)
            dk = dot(q, ds, 1, 1).astype(bf16)
            dqkv_ref[to(0, h), :] = dq
            dqkv_ref[to(1, h), :] = dk
            dqkv_ref[to(2, h), :] = dv
            gh_ref[c, h * HEAD : (h + 1) * HEAD, 0:1] = lane_sum(up(dq))
            gh_ref[c, h * HEAD : (h + 1) * HEAD, 1:2] = lane_sum(up(dv))
        return carry

    lax.fori_loop(first, last, per_block, 0)


def attend_back_kernel(nc, hw, rw, info, e1_ref, o_ref, lse_ref, pd, left, right, qkv_in, *refs):
    pieces = refs[:10]
    dqkv_ref, gd_ref, gh_ref, do_ref, qkv_ref, p0, p1, q0, q1, go, don, ka, qa, va, oa, go_sem, in_sem = refs[10:]
    qkv_copy = move(qkv_in, qkv_ref, in_sem)

    def place(i):
        row = jnp.bitwise_xor(info[1], i // nc)
        return go.at[pl.ds(i % nc * hw, hw), pl.ds(pl.multiple_of(row * rw, rw), rw)]

    fetch(pieces, 4 * hw, ((3 * hw, 4 * hw, place, go_sem),))
    add_blocks(left, right, (p0, p1, q0, q1))
    for i in range(2 * nc):
        arrive(go.at[pl.ds(0, hw), pl.ds(0, rw)], go_sem.at[i])
    don[...] = dot(go[...], e1_ref[...], 1, 0)

    def emit(at, dx):
        do_ref[at, :] = dx.astype(bf16)

    norm_back(don, o_ref, pd, 8, gd_ref, emit)
    qkv_copy.wait()
    heads_back(0, nc // 2, hw, info, qkv_ref, lse_ref, o_ref, do_ref, dqkv_ref, gh_ref, ka, qa, va, oa)


def attend_back_rest_kernel(nc, hw, info, o_ref, qkv_ref, lse_ref, do_ref, _, __, dqkv_ref, gh_ref, ka, qa, va, oa):
    heads_back(nc // 2, nc, hw, info, qkv_ref, lse_ref, o_ref, do_ref, dqkv_ref, gh_ref, ka, qa, va, oa)


def input_back_kernel(nc, hw, rw, info, dqkv, x_ref, dx1_ref, pd, *refs):
    pieces = refs[:10]
    outs_ref, gd_ref, ga, da, ga_sem = refs[10:]

    def place(i):
        row = jnp.bitwise_xor(info[1], i // nc)
        c = i % nc
        rows = pl.ds(c % 2 * 3 * hw, 3 * hw)
        return ga.at[c // 2, rows, pl.ds(pl.multiple_of(row * rw, rw), rw)]

    fetch(pieces, 4 * hw, ((0, 3 * hw, place, ga_sem),))
    for i in range(2 * nc):
        arrive(ga.at[0, pl.ds(0, 3 * hw), pl.ds(0, rw)], ga_sem.at[i])
    da[...] = jnp.zeros(da.shape, f32)

    def one(k, carry):
        rows = pl.ds(pl.multiple_of(k * 6 * hw, 6 * hw), 6 * hw)
        da[...] += dot(ga[k], dqkv[rows, :], 0, 0)
        return carry

    lax.fori_loop(0, nc // 2, one, 0)

    def emit(at, dx):
        apart(outs_ref, at, (dx1_ref[at, :] + dx).astype(bf16))

    norm_back(da, x_ref, pd, 0, gd_ref, emit)


def attend_grads_kernel(
    nc, hw, rw, fl, fw, info, dqkv, a_ref, gd_in, gd_mid, gd_mix, gh, gf_ref, keep, send, wide, thin,
):
    my_row = info[1]
    lane = lax.broadcasted_iota(jnp.int32, (fl, 128), 1)

    def own(i, carry):
        at = pl.ds(pl.multiple_of(i * fl, fl), fl)
        tile = jnp.zeros((fl, 128), f32)
        for k, (ref, j) in enumerate(((gd_in, 0), (gd_in, 1), (gd_mid, 2), (gd_mid, 0), (gd_mid, 1), (gd_mid, 3))):
            tile = jnp.where(lane == k, ref[at, j : j + 1], tile)
        wide[at, :] = tile
        return carry

    lax.fori_loop(0, 2 * nc, own, 0)

    def columns(c, carry):
        tile = jnp.zeros((fl, 128), f32)
        at = 6
        for k in range(hw // fl):
            rows = slice(k * fl, (k + 1) * fl)
            deep = pl.ds(pl.multiple_of(c * hw + k * fl, fl), fl)
            for column in (gh[c, rows, 0:1], gh[c, rows, 1:2], gd_mix[deep, 0:1], gd_mix[deep, 1:2]):
                tile = jnp.where(lane == at, column, tile)
                at += 1
        for k in range(fw // fl):
            rows = slice(k * fl, (k + 1) * fl)
            for column in (gf_ref[c, rows, 2:3], gf_ref[c, rows, 0:1], gf_ref[c, rows, 1:2]):
                tile = jnp.where(lane == at, column, tile)
                at += 1
        thin[c] = tile
        return carry

    lax.fori_loop(0, nc, columns, 0)

    def blocks(c, place):
        grad = dot(dqkv[pl.ds(pl.multiple_of(c * 3 * hw, 3 * hw), 3 * hw), :], a_ref[...], 1, 1).astype(bf16)
        for row in range(2):
            place(jnp.bitwise_xor(my_row, row))[0 : 3 * hw, :] = grad[:, row * rw : (row + 1) * rw]
        for row in range(2):
            block = jnp.bitwise_xor(info[0], row * nc + c)
            tile = thin[c] + wide[pl.ds(pl.multiple_of(block * fl, fl), fl), :]
            third = fl // 3
            tile = jnp.concatenate([tile[m * third : (m + 1) * third] for m in range(3)], axis=1)
            place(row)[3 * hw :, :] = tile.astype(bf16)

    store_blocks(nc, blocks, keep, send)


def shrink_kernel(nc, rw, fw, info, pd, gn_ref, x1_ref, *refs):
    pieces = refs[:10]
    y_ref, gs, gs_sem = refs[10:]
    fetch(pieces, fw, ((0, fw, lambda i: gs.at[i // nc, pl.ds(i % nc * fw, fw)], gs_sem),))
    my_row = info[1]
    for i in range(2 * nc):
        arrive(gs.at[i // nc, pl.ds(i % nc * fw, fw)], gs_sem.at[i])

    def one(r, carry):
        rows = pl.ds(pl.multiple_of(r * rw, rw), rw)
        part = dot(gs[jnp.bitwise_xor(my_row, r)], gn_ref[...], 0, 0)
        apart(y_ref, rows, (x1_ref[rows, :] + part + pd[rows, 5:6]).astype(bf16))
        return carry

    lax.fori_loop(0, 2, one, 0)


def body(
    tokens,
    cotangent,
    holder_of,
    lengths,
    input_gain,
    input_shift,
    attend_weight,
    attend_bias,
    mixed_gain,
    mixed_shift,
    output_weight,
    output_bias,
    middle_gain,
    middle_shift,
    expand_weight,
    expand_bias,
    hidden_gain,
    hidden_shift,
    shrink_weight,
    shrink_bias,
):
    holders = lax.axis_size("dp")
    half = holders // 2
    nr, nc = lax.axis_size("row"), lax.axis_size("col")
    n = nr * nc
    micro = holder_of.shape[0]
    assert micro == n and nr == 2 and nc == 4
    fl = tokens.shape[0]
    pairs = micro * half
    blk = tokens.shape[1] // pairs
    unit = half * blk
    dp = lax.axis_index("dp")
    side, pos = dp // half, dp % half
    my_row, my_col = lax.axis_index("row"), lax.axis_index("col")
    rc = my_row * nc + my_col
    groups = [list(range(s * half * n, (s + 1) * half * n)) for s in range(2)]
    hw, rw, fw = output_weight.shape[0], output_weight.shape[1], shrink_weight.shape[0]

    def flip_row(v):
        return lax.ppermute(v, "row", [(i, i ^ 1) for i in range(nr)])

    def flip_chip(v):
        return lax.ppermute(v, "col", [(i, i ^ 2) for i in range(nc)])

    def flip_core(v):
        return lax.ppermute(v, "col", [(i, i ^ 1) for i in range(nc)])

    def flip_dp(v, step):
        return lax.ppermute(v, "dp", [(i, i ^ step) for i in range(holders)])

    def exchange(v):
        return lax.all_to_all(v, ("dp",) + RC, 0, 0, axis_index_groups=groups, tiled=True)

    lanes = blk % 128 == 0

    def by_target(v):
        v = jnp.transpose(v.reshape(2, fl, half * n, blk), (2, 0, 1, 3))
        return v.reshape(half * n, 2 * fl, blk)

    def exchange_units(v):
        v = exchange(v).reshape(half, n, 2 * fl, blk)
        return v if lanes else jnp.transpose(v, (1, 2, 0, 3)).reshape(1, n, 2 * fl, unit)

    def from_unit(v):
        if not lanes:
            v = jnp.transpose(v.reshape(n * fl, half, blk), (1, 0, 2))
        v = exchange(v.reshape(half * n, fl, blk))
        return jnp.transpose(v, (1, 0, 2)).reshape(tokens.shape)

    def tie(*values):
        return lax.optimization_barrier(values)

    def near(v):
        return flip_row(v), flip_chip(v)

    def far(v, by_row, by_chip):
        h = v.shape[0] // 2
        return flip_row(by_chip[:h]), flip_chip(by_row[h:])

    def near_flips(v, near_v):
        return tuple(flip_core(p) for p in (v, near_v[1], near_v[0]))

    def pieces_of(v, near_v, flips, far_v):
        v1, c1, r1 = flips
        f1, g1 = (flip_core(p) for p in far_v)
        return (v, v1, near_v[1], c1, near_v[0], r1, far_v[0], far_v[1], f1, g1)

    w1 = jnp.concatenate([attend_weight.reshape(3 * hw, rw), output_weight], axis=0)
    near1 = near(w1)
    tile = jnp.concatenate(
        [
            jnp.stack([input_gain, input_shift, output_bias, middle_gain, middle_shift, shrink_bias]),
            jnp.transpose(
                jnp.stack([attend_bias[0], attend_bias[1], mixed_gain, mixed_shift]).reshape(4, -1, fl), (1, 0, 2)
            ).reshape(-1, fl),
            jnp.transpose(jnp.stack([expand_bias, hidden_gain, hidden_shift]).reshape(3, -1, fl), (1, 0, 2)).reshape(-1, fl),
        ]
    )
    tile = jnp.transpose(jnp.pad(tile, ((0, 128 - tile.shape[0]), (0, 0))))
    ready = by_target(jnp.concatenate([tokens, cotangent], axis=0))
    near1, tile, ready = tie(near1, tile, ready)
    far1 = far(w1, *near1)
    both = exchange_units(ready)
    tile_row, tile_chip = near(tile)
    even = jnp.stack([tile, tile_chip, tile_row, flip_row(tile_chip)])
    odd = flip_core(even)
    flips1 = near_flips(w1, near1)
    far1, flips1, both, odd, w2 = tie(far1, flips1, both, odd, expand_weight)
    near2 = near(w2)
    g1 = pieces_of(w1, near1, flips1, far1)

    k_unit = 2 * (pos * n + rc) + side
    own = lengths[k_unit // holders, holder_of[k_unit // holders, k_unit % holders]]
    info = jnp.concatenate([jnp.stack([rc, my_row]), jnp.cumsum(own)[:-1]]).astype(jnp.int32)

    d = n * fl
    split = lambda v: v.reshape(nr, rw, unit)
    dma = pltpu.SemaphoreType.DMA
    weight_flops = 2 * unit * d * nc * fw

    dp_odd = dp % 2 == 1

    def reduce_rest(v):
        step = 2
        while 2 * step < holders:
            v = v + flip_dp(v, step)
            step *= 2
        return v, flip_dp(v, step) if step < holders else jnp.zeros_like(v)

    def spread(v):
        return v, flip_dp(v, 1)

    def whole(v, got):
        return jnp.concatenate([jnp.where(dp_odd, got, v), jnp.where(dp_odd, v, got)], axis=0).astype(f32)

    vm = lambda shape, dtype=bf16: pltpu.VMEM(shape, dtype)
    act, act32, hid = (d, unit), (nc * hw, unit), (nc, fw, unit)
    part1, part2, part3 = (nr, nc // 2, 4 * hw, rw), (nr, nc // 2, rw, fw), (nr, nc // 2, fw, rw)

    def time_us(t):
        return dict(flops=int(t * 1e9), moved=int(t * 1e6))

    extra = vm((HEAD + 16, unit))
    x, a, qkv, lse, o, pd, pf = call(
        functools.partial(attend_kernel, nc, hw, rw, fl, fw),
        (
            sds(act, bf16), sds(act, bf16), sds((nc, 3 * hw, unit), bf16), sds((nc, 8, unit), f32), sds(act, f32),
            sds((d, 16), f32), sds((nc, fw, 8), f32),
        ),
        [SMEM] + [VMEM] * 3 + [HBM] * 10,
        [VMEM, VMEM, HBM, VMEM, VMEM, VMEM, VMEM],
        [
            vm((nc, 3 * hw, unit)), vm((nc, 3 * hw, nr * rw)), extra, extra,
            dma((n,)), dma((nc,)),
        ],
        **time_us(13), name="attend",
    )(info, both, even, odd, *g1)

    o, near2 = tie(o, near2)
    far2 = far(w2, *near2)
    flips2 = near_flips(w2, near2)

    on, x1, b = call(
        functools.partial(output_kernel, nc, hw, rw),
        (sds(act, bf16), sds(act, f32), sds(act, bf16)),
        [SMEM] + [VMEM] * 3 + [HBM] * 10,
        [VMEM] * 3,
        [vm((nr, nc * hw, rw)), dma((n,))],
        **time_us(5), name="output",
    )(info, x, o, pd, *g1)

    b, far2, flips2, w3 = tie(b, far2, flips2, shrink_weight)
    near3 = near(w3)
    g2 = pieces_of(w2, near2, flips2, far2)

    gn, vh, slope, st = call(
        functools.partial(expand_kernel, nc, rw, fw),
        (sds(hid, bf16), sds(hid, bf16), sds(hid, bf16), sds((8, unit), f32)),
        [SMEM, VMEM, VMEM] + [HBM] * 10,
        [VMEM, HBM, HBM, VMEM],
        [vm(hid), vm(hid), vm(hid, f32), vm((nc, nr * rw, fw)), dma((n,)), dma((2 * nc,))],
        **time_us(13), name="expand",
    )(info, b, pf, *g2)

    gn, near3 = tie(gn, near3)
    far3 = far(w3, *near3)
    flips3 = near_flips(w3, near3)

    e2, shr_keep, shr_send = call(
        functools.partial(shrink_grads_kernel, nc, rw),
        (sds(act, bf16), sds(part3, bf16), sds(part3, bf16)),
        [SMEM] + [VMEM] * 2,
        [VMEM] * 3,
        **time_us(7), name="shrink_grads",
    )(info, gn, both)

    shr_send, far3, flips3 = tie(shr_send, far3, flips3)
    g3 = pieces_of(w3, near3, flips3, far3)
    shr_got = flip_core(shr_send)

    def reduce_near(v):
        return flip_row(v[1]), flip_chip(v[3])

    def reduce_far(v, got):
        p, q = v[0] + got[0], v[2] + got[1]
        return (p[0], q[0]), (flip_chip(p[1]), flip_row(q[1]))

    def reduce_dp(v, got):
        p, q = v[0] + got[0], v[1] + got[1]
        return jnp.where(dp_odd, q, p), flip_dp(jnp.where(dp_odd, p, q), 1)

    sum3 = (nc // 2, fw // 2, rw)
    df, gf, *shr = call(
        functools.partial(hidden_back_kernel, nc, rw, fw),
        (sds(hid, bf16), sds((nc, fw, 8), f32)) + (sds(sum3, bf16),) * 4,
        [SMEM] + [VMEM] * 5 + [HBM] * 12,
        [VMEM] * 6,
        [vm(hid), vm(hid), vm((nc, fw, nr * rw)), vm(hid, f32), dma((n,)), dma((nc,)), dma((nc,))],
        **time_us(13), name="hidden_back",
    )(info, st, e2, pf, shr_keep, shr_got, vh, slope, *g3)

    shr_near = reduce_near(shr)

    dx1, e1, gd_mid = call(
        functools.partial(middle_back_kernel, nc, rw, fw),
        (sds(act, f32), sds(act, bf16), sds((d, 8), f32)),
        [SMEM] + [VMEM] * 4 + [HBM] * 10,
        [VMEM] * 3,
        [vm((nc, nr * rw, fw)), vm(act, f32), dma((n,))],
        **time_us(8), name="middle_back",
    )(info, df, x1, e2, pd, *g2)

    rows2 = 2 * rw + hw
    part2 = (nr, nc // 2, rows2, rw)
    sum2 = (nc // 2, rows2 // 2, rw)
    mid_keep, mid_send = call(
        functools.partial(middle_grads_kernel, nc, hw, rw, fw),
        (sds(part2, bf16), sds(part2, bf16)),
        [SMEM] + [VMEM] * 4,
        [VMEM] * 2,
        **time_us(7), name="middle_grads",
    )(info, b, df, on.reshape(nc, hw, unit), e1)

    e1, mid_send, shr_near = tie(e1, mid_send, shr_near)
    mid_got = flip_core(mid_send)
    shr_stay, shr_far = reduce_far(shr, shr_near)

    all_heads = (nc * 3 * hw, unit)
    dqkv, gd_mix, gh, do, qkv, *mid = call(
        functools.partial(attend_back_kernel, nc, hw, rw),
        (sds(all_heads, bf16), sds((d, 8), f32), sds((nc, hw, 8), f32), sds(act, bf16), sds(qkv.shape, bf16))
        + (sds(sum2, bf16),) * 4,
        [SMEM] + [VMEM] * 6 + [HBM] * 11,
        [VMEM] * 9,
        [vm((nc * hw, nr * rw)), vm(act, f32), extra, extra, extra, extra, dma((n,)), dma(())],
        **time_us(11), name="attend_back",
    )(info, e1, o, lse, pd, mid_keep, mid_got, qkv, *g1)

    do, shr_far, mid = tie(do, shr_far, mid)
    shr, shr_dp = reduce_dp(shr_stay, shr_far)
    mid_near = reduce_near(mid)

    dqkv, gh = call(
        functools.partial(attend_back_rest_kernel, nc, hw),
        (sds(all_heads, bf16), sds((nc, hw, 8), f32)),
        [SMEM] + [VMEM] * 6,
        [VMEM] * 2,
        [extra, extra, extra, extra],
        **time_us(8), name="attend_back_rest", aliases={5: 0, 6: 1},
    )(info, o, qkv, lse, do, dqkv, gh)

    dqkv, shr_dp = tie(dqkv, shr_dp)
    shr, shr_rest = reduce_rest(shr + shr_dp)

    input_grad, gd_in = call(
        functools.partial(input_back_kernel, nc, hw, rw),
        (sds((half if lanes else 1, d, blk if lanes else unit), bf16), sds((d, 8), f32)),
        [SMEM] + [VMEM] * 4 + [HBM] * 10,
        [VMEM] * 2,
        [vm((2, nc // 2 * 3 * hw, nr * rw)), vm(act, f32), dma((n,))],
        **time_us(7), name="input_back",
    )(info, dqkv, x, dx1, pd, *g1)

    gd_in, mid_near = tie(gd_in, mid_near)
    mid_stay, mid_far = reduce_far(mid, mid_near)

    rows1 = 3 * hw + fl // 3
    part1 = (nr, nc // 2, rows1, rw)
    att_keep, att_send = call(
        functools.partial(attend_grads_kernel, nc, hw, rw, fl, fw),
        (sds(part1, bf16), sds(part1, bf16)),
        [SMEM] + [VMEM] * 7,
        [VMEM] * 2,
        [vm((d, 128), f32), vm((nc, fl, 128), f32)],
        **time_us(7), name="attend_grads",
    )(info, dqkv, a, gd_in, gd_mid, gd_mix, gh, gf)

    att_send, shr_rest, mid_far = tie(att_send, shr_rest, mid_far)
    att_got = flip_core(att_send)
    mid, mid_dp = reduce_dp(mid_stay, mid_far)
    shr, shr_got = spread(shr + shr_rest)
    h = rows1 // 2
    p1, q1 = att_keep[1, :, :h] + att_got[1, :, :h], att_keep[:, 1, h:] + att_got[:, 1, h:]
    p1, q1, y_in = tie(p1, q1, gn)
    p_row, q_chip = flip_row(p1), flip_chip(q1)

    y = call(
        functools.partial(shrink_kernel, nc, rw, fw),
        sds(input_grad.shape, bf16),
        [SMEM] + [VMEM] * 3 + [HBM] * 10,
        VMEM,
        [vm((nr, nc * fw, rw)), dma((n,))],
        **time_us(8), name="shrink",
    )(info, pd, y_in.reshape(nc * fw, unit), x1, *g3)

    y, mid_dp, shr_got, input_grad = tie(y, mid_dp, shr_got, input_grad)
    mid, mid_rest = reduce_rest(mid + mid_dp)
    mid, p_row, q_chip = tie(mid, p_row, q_chip)
    p = att_keep[0, :, :h] + att_got[0, :, :h] + p_row
    q = att_keep[:, 0, h:] + att_got[:, 0, h:] + q_chip
    att_far = flip_chip(p[1]), flip_row(q[1])
    input_grad = from_unit(input_grad)
    att, att_dp = reduce_dp((p[0], q[0]), att_far)
    att_dp, mid_rest, y = tie(att_dp, mid_rest, y)
    block_out = from_unit(y)
    att, att_rest = reduce_rest(att + att_dp)
    mid, mid_got = spread(mid + mid_rest)
    att, att_got = spread(att + att_rest)
    att_got, mid_got, shr_got = tie(att_got, mid_got, shr_got)
    att, mid, shr_w_g = whole(att, att_got), whole(mid, mid_got), whole(shr, shr_got)
    exp_w_g = jnp.concatenate([mid[:rw], mid[rw : 2 * rw]], axis=1)

    thin = att[3 * hw :]
    thin = jnp.transpose(jnp.concatenate([thin[:, k * 128 : (k + 1) * 128] for k in range(3)], axis=0))
    in_g_g, in_s_g, out_b_g, mid_g_g, mid_s_g, shr_b_g = (thin[i] for i in range(6))
    at = 6 + 4 * (hw // fl)
    heads_g = jnp.transpose(thin[6:at].reshape(-1, 4, fl), (1, 0, 2)).reshape(4, hw)
    hidden_g = jnp.transpose(thin[at : at + 3 * (fw // fl)].reshape(-1, 3, fl), (1, 0, 2)).reshape(3, fw)
    q_b_g, v_b_g, mix_g_g, mix_s_g = heads_g
    exp_b_g, hid_g_g, hid_s_g = hidden_g
    return (
        block_out,
        input_grad,
        in_g_g,
        in_s_g,
        att[: 3 * hw].reshape(attend_weight.shape),
        jnp.stack([q_b_g, v_b_g]),
        mix_g_g,
        mix_s_g,
        mid[2 * rw :],
        out_b_g,
        mid_g_g,
        mid_s_g,
        exp_w_g,
        exp_b_g,
        hid_g_g,
        hid_s_g,
        shr_w_g,
        shr_b_g,
    )


def solution(mesh):
    wide, narrow = P(RC), P("col")
    in_specs = (
        P(RC, "dp"), P(RC, "dp"), P(), P(), wide, wide, P(None, "col", "row"), P(None, "col"),
        narrow, narrow, P("col", "row"), wide, wide, wide, P("row", "col"), narrow, narrow, narrow,
        P("col", "row"), wide,
    )
    out_specs = (
        P(RC, "dp"), P(RC, "dp"), wide, wide, P(None, "col", "row"), P(None, "col"), narrow, narrow,
        P("col", "row"), wide, wide, wide, P("row", "col"), narrow, narrow, narrow, P("col", "row"),
        wide,
    )
    return jax.shard_map(body, mesh=mesh, in_specs=in_specs, out_specs=out_specs, check_vma=False)
```

```python
import functools
import math

import jax
import jax.numpy as jnp
from jax import lax
from jax.experimental import pallas as pl
from jax.experimental.pallas import tpu as pltpu
from jax.sharding import PartitionSpec as P

HEAD = 64
eps = 1e-05
masked_score = -1e30
f32 = jnp.float32
bf16 = jnp.bfloat16
RC = ("row", "col")
HBM = pl.BlockSpec(memory_space=pltpu.HBM)
SMEM = pl.BlockSpec(memory_space=pltpu.SMEM)
VMEM = pl.BlockSpec(memory_space=pltpu.VMEM)
root_half = math.sqrt(0.5)
root_tau = 1.0 / math.sqrt(2.0 * math.pi)
score_scale = 1.0 / math.sqrt(HEAD)


def dot(a, b, ca, cb):
    return lax.dot_general(a, b, (((ca,), (cb,)), ((), ())), preferred_element_type=f32)


def up(v):
    return v.astype(f32)


def lane_sum(v):
    return jnp.sum(v, axis=1, keepdims=True)


def token_sum(v):
    return jnp.sum(v, axis=0, keepdims=True)


CHUNK = 768
ROOM = 8


def over(rows, step, init=0, chunk=CHUNK):
    def one(i, carry):
        return step(pl.ds(pl.multiple_of(i * chunk, chunk), chunk), carry)

    return lax.fori_loop(0, rows // chunk, one, init)


def moments(ref, chunk=CHUNK):
    rows, unit = ref.shape
    zero = jnp.zeros((1, unit), f32)
    mu = over(rows, lambda at, s: s + token_sum(up(ref[at, :])), zero, chunk) * (1.0 / rows)

    def square(at, s):
        d = up(ref[at, :]) - mu
        return s + token_sum(d * d)

    return mu, lax.rsqrt(over(rows, square, zero, chunk) * (1.0 / rows) + eps)


def norm(out, ref, pd, gain, shift):
    mu, r = moments(ref, CHUNK // 2)

    def one(at, carry):
        out[at, :] = ((up(ref[at, :]) - mu) * r * pd[at, gain : gain + 1] + pd[at, shift : shift + 1]).astype(bf16)
        return carry

    over(ref.shape[0], one, chunk=CHUNK // 2)


def norm_back(grad, ref, pd, gain, gd, emit):
    rows, unit = ref.shape
    mu, r = moments(ref, CHUNK // 2)
    zero = jnp.zeros((1, unit), f32)

    def first(at, s):
        g = grad[at, :]
        gv = g * ((up(ref[at, :]) - mu) * r)
        gd[at, 0:1] = lane_sum(gv)
        gd[at, 1:2] = lane_sum(g)
        k = pd[at, gain : gain + 1]
        return s[0] + token_sum(g * k), s[1] + token_sum(gv * k)

    m1, m2 = over(rows, first, (zero, zero))
    m1, m2 = m1 * (1.0 / rows), m2 * (1.0 / rows)

    def second(at, carry):
        vh = (up(ref[at, :]) - mu) * r
        emit(at, r * (grad[at, :] * pd[at, gain : gain + 1] - m1 - vh * m2))
        return carry

    over(rows, second)


PIECES = ((0, None), (1, None), (2, None), (3, None), (4, None), (5, None), (6, 0), (6, 1), (7, 0), (7, 1))


def fetch(pieces, rows, parts):
    for ref, (block, half) in zip(pieces, PIECES):
        first, last = (0, rows) if half is None else (half * rows // 2, (half + 1) * rows // 2)
        for lo, hi, place, sem in parts:
            a, b = max(lo, first), min(hi, last)
            if a < b:
                pltpu.make_async_copy(
                    ref.at[pl.ds(a - first, b - a)], place(block).at[pl.ds(a - lo, b - a)], sem.at[block]
                ).start()


def arrive(ref, sem):
    pltpu.make_async_copy(ref, ref, sem).wait()


def move(src, dst, sem):
    copy = pltpu.make_async_copy(src, dst, sem)
    copy.start()
    return copy


def vmem_bytes(shape, dtype):
    size = jnp.dtype(dtype).itemsize
    sublanes, lanes = 32 // size, 128
    *lead, rows, columns = (1,) * max(0, 2 - len(shape)) + tuple(shape)
    return math.prod(lead) * (-(-rows // sublanes) * sublanes) * (-(-columns // lanes) * lanes) * size


def pinned(spec):
    return pltpu.VMEM if spec is VMEM else pltpu.HBM


def call(kernel, outs, in_specs, out_specs, scratch=(), flops=0, moved=0, name=None, aliases=None):
    held = [v for v in scratch if v.memory_space == pltpu.VMEM]
    limit = sum(vmem_bytes(v.shape, v.dtype) for v in held) + (ROOM << 20)
    single = not isinstance(outs, tuple)
    places = [pinned(spec)(v.shape, v.dtype) for v, spec in zip((outs,) if single else outs, (out_specs,) if single else out_specs)]

    def run(*args):
        args = [v if spec is SMEM else pltpu.with_memory_space_constraint(v, pinned(spec)) for v, spec in zip(args, in_specs)]
        return pl.pallas_call(
            kernel,
            out_shape=places[0] if single else tuple(places),
            in_specs=in_specs,
            out_specs=out_specs,
            scratch_shapes=list(scratch),
            compiler_params=pltpu.CompilerParams(vmem_limit_bytes=limit),
            cost_estimate=pl.CostEstimate(flops=flops, bytes_accessed=moved, transcendentals=0),
            name=name,
            input_output_aliases=aliases or {},
        )(*args)

    return run


def sds(shape, dtype):
    return jax.ShapeDtypeStruct(shape, dtype)


def segment_rows(info, unit):
    t = lax.broadcasted_iota(jnp.int32, (16, unit), 1)
    slot = lax.broadcasted_iota(jnp.int32, (16, unit), 0)
    one = lambda b: jnp.where(t >= b, 1, 0)
    seg = one(info[2]) + one(info[3]) + one(info[4])
    same = seg == slot
    for_keys = jnp.where(same, 1.0, 0.0)
    for_queries = jnp.where(jnp.logical_and(slot < 4, jnp.logical_not(same)), masked_score, 0.0)
    return for_keys, for_queries


def split3(v):
    hi = v.astype(bf16)
    v = v - up(hi)
    mid = v.astype(bf16)
    return hi, mid, (v - up(mid)).astype(bf16)


def three_rows(base, v, first):
    row = lax.broadcasted_iota(jnp.int32, base.shape, 0)
    for i, part in enumerate(split3(v)):
        base = jnp.where(row == first + i, up(part), base)
    return base


def unit_of(ref, which):
    blocks, n, rows, _ = ref.shape
    rows //= 2
    return jnp.concatenate(
        [
            jnp.concatenate([ref[k, i, which * rows : (which + 1) * rows, :] for i in range(n)], axis=0)
            for k in range(blocks)
        ],
        axis=1,
    )


def apart(ref, at, value):
    width = ref.shape[2]
    for i in range(ref.shape[0]):
        ref[i, at, :] = value[:, i * width : (i + 1) * width]


def beside(ref, info, nc, rw):
    def place(i):
        row = jnp.bitwise_xor(info[1], i // nc)
        return ref.at[i % nc, :, pl.ds(pl.multiple_of(row * rw, rw), rw)]

    return place


def below(ref, info, nc, rw):
    def place(i):
        row = jnp.bitwise_xor(info[1], i // nc)
        return ref.at[i % nc, pl.ds(pl.multiple_of(row * rw, rw), rw)]

    return place


def attend_kernel(nc, hw, rw, fl, fw, info, both, even, odd, *refs):
    pieces = refs[:10]
    x_ref, a_ref, qkv_out, lse_ref, o_ref, pd, pf = refs[10:17]
    qkv_ref, ga, ka, qa, ga_sem, out_sem = refs[17:]
    unit = o_ref.shape[1]
    fetch(pieces, 4 * hw, ((0, 3 * hw, beside(ga, info, nc, rw), ga_sem),))
    for i in range(2 * nc):
        tile = (even, odd)[i % 2][i // 2]
        pd[pl.ds(pl.multiple_of(jnp.bitwise_xor(info[0], i) * fl, fl), fl), 0:6] = tile[:, 0:6]
        if i < nc:
            for k in range(hw // fl):
                pd[i * hw + k * fl : i * hw + (k + 1) * fl, 6:10] = tile[:, 6 + 4 * k : 10 + 4 * k]
            for k in range(fw // fl):
                first = 6 + 4 * (hw // fl) + 3 * k
                pf[i, k * fl : (k + 1) * fl, 0:3] = tile[:, first : first + 3]
    x_ref[...] = unit_of(both, 0)
    norm(a_ref, x_ref, pd, 0, 1)
    for_keys, for_queries = segment_rows(info, unit)
    ka[HEAD:, :] = for_keys.astype(bf16)
    qa[HEAD:, :] = for_queries.astype(bf16)

    def per_block(c, carry):
        for i in (c, nc + c):
            arrive(ga.at[c, :, pl.ds(0, rw)], ga_sem.at[i])
        trip = dot(ga[c], a_ref[...], 1, 0)
        at = pl.multiple_of(c * hw, hw)
        qkv_ref[c, 0:hw, :] = (trip[0:hw] + pd[pl.ds(at, hw), 6:7]).astype(bf16)
        qkv_ref[c, hw : 2 * hw, :] = trip[hw : 2 * hw].astype(bf16)
        qkv_ref[c, 2 * hw :, :] = (trip[2 * hw :] + pd[pl.ds(at, hw), 7:8]).astype(bf16)
        move(qkv_ref.at[c], qkv_out.at[c], out_sem.at[c])
        for h in range(hw // HEAD):
            qa[0:HEAD, :] = qkv_ref[c, h * HEAD : (h + 1) * HEAD, :] * jnp.bfloat16(score_scale)
            ka[0:HEAD, :] = qkv_ref[c, hw + h * HEAD : hw + (h + 1) * HEAD, :]
            v = qkv_ref[c, 2 * hw + h * HEAD : 2 * hw + (h + 1) * HEAD, :]
            s = dot(ka[...], qa[...], 0, 0)
            top = jnp.max(s, axis=0, keepdims=True)
            e = jnp.exp(s - top)
            den = token_sum(e)
            o = dot(v, e.astype(bf16), 1, 0) * (1.0 / den)
            o_ref[pl.ds(pl.multiple_of(c * hw + h * HEAD, HEAD), HEAD), :] = o
            lse_ref[c, h : h + 1, :] = top + jnp.log(den)
        return carry

    lax.fori_loop(0, nc, per_block, 0)
    for c in range(nc):
        arrive(qkv_ref.at[c], out_sem.at[c])


def output_kernel(nc, hw, rw, info, x_ref, o_ref, pd, *refs):
    pieces = refs[:10]
    on_ref, x1_ref, b_ref, go, go_sem = refs[10:]
    fetch(pieces, 4 * hw, ((3 * hw, 4 * hw, lambda i: go.at[i // nc, pl.ds(i % nc * hw, hw)], go_sem),))
    my_row = info[1]
    norm(on_ref, o_ref, pd, 8, 9)
    for i in range(2 * nc):
        arrive(go.at[i // nc, pl.ds(i % nc * hw, hw)], go_sem.at[i])

    def one(r, carry):
        rows = pl.ds(pl.multiple_of(r * rw, rw), rw)
        x1_ref[rows, :] = dot(go[jnp.bitwise_xor(my_row, r)], on_ref[...], 0, 0) + up(x_ref[rows, :]) + pd[rows, 2:3]
        return carry

    lax.fori_loop(0, 2, one, 0)
    norm(b_ref, x1_ref, pd, 3, 4)


def expand_kernel(nc, rw, fw, info, b_ref, pf, *refs):
    pieces = refs[:10]
    gn_ref, vh_out, slope_out, st_ref = refs[10:14]
    vh_ref, slope_ref, g_ref, ge, ge_sem, out_sem = refs[14:]
    fetch(pieces, rw, ((0, rw, below(ge, info, nc, rw), ge_sem),))
    unit = b_ref.shape[1]
    total = nc * fw

    def first(c, s):
        for i in (c, nc + c):
            arrive(ge.at[c, pl.ds(0, rw)], ge_sem.at[i])
        f = dot(ge[c], b_ref[...], 0, 0) + pf[c, :, 0:1]
        phi = 0.5 * (1.0 + lax.erf(f * root_half))
        g = f * phi
        g_ref[c] = g
        slope_ref[c] = (phi + f * (jnp.exp(-0.5 * f * f) * root_tau)).astype(bf16)
        move(slope_ref.at[c], slope_out.at[c], out_sem.at[c])
        return s + token_sum(g)

    mu = lax.fori_loop(0, nc, first, jnp.zeros((1, unit), f32)) * (1.0 / total)

    def second(c, s):
        def square(at, t):
            d = g_ref[c, at, :] - mu
            return t + token_sum(d * d)

        return over(fw, square, s)

    r = lax.rsqrt(lax.fori_loop(0, nc, second, jnp.zeros((1, unit), f32)) * (1.0 / total) + eps)
    st_ref[...] = jnp.broadcast_to(r, st_ref.shape)

    def third(c, carry):
        def one(at, t):
            vh = (g_ref[c, at, :] - mu) * r
            vh_ref[c, at, :] = vh.astype(bf16)
            gn_ref[c, at, :] = (vh * pf[c, at, 1:2] + pf[c, at, 2:3]).astype(bf16)
            return t

        over(fw, one)
        move(vh_ref.at[c], vh_out.at[c], out_sem.at[nc + c])
        return carry

    lax.fori_loop(0, nc, third, 0)
    for c in range(nc):
        arrive(slope_ref.at[c], out_sem.at[c])
        arrive(vh_ref.at[c], out_sem.at[nc + c])


def store_blocks(nc, blocks, keep, send):
    def one(k, carry):
        for ref, c in ((send, 2 * k + 1), (keep, 2 * k)):
            blocks(c, lambda row: ref.at[row, k])
        return carry

    lax.fori_loop(0, nc // 2, one, 0)


def shrink_grads_kernel(nc, rw, info, gn_ref, both, e2_ref, keep, send):
    my_row = info[1]
    e2_ref[...] = unit_of(both, 1)

    def blocks(c, place):
        grad = dot(gn_ref[c], e2_ref[...], 1, 1).astype(bf16)
        for r in range(2):
            place(jnp.bitwise_xor(my_row, r))[...] = grad[:, r * rw : (r + 1) * rw]

    store_blocks(nc, blocks, keep, send)


def add_blocks(left, right, outs):
    h = left.shape[2] // 2
    for j in range(4):
        r, c = j // 2, j % 2
        outs[r][c] = (up(left[r, c, :h]) + up(right[r, c, :h])).astype(bf16)
        outs[2 + c][r] = (up(left[r, c, h:]) + up(right[r, c, h:])).astype(bf16)


def sum_near_kernel(row_own, row_got, chip_own, chip_got, p0, p1, q0, q1):
    for own, got, outs in ((row_own, row_got, (p0, p1)), (chip_own, chip_got, (q0, q1))):
        for i in range(2):
            outs[i][...] = (up(own[i]) + up(got[i])).astype(bf16)


def hidden_back_kernel(nc, rw, fw, info, st_ref, e2_ref, pf, left, right, vh_in, slope_in, *refs):
    pieces = refs[:10]
    df_ref, gf_ref, p0, p1, q0, q1 = refs[10:16]
    vh_ref, slope_ref, gs, dgn, gs_sem, vh_sem, slope_sem = refs[16:]
    fetch(pieces, fw, ((0, fw, beside(gs, info, nc, rw), gs_sem),))
    for c in range(nc):
        move(vh_in.at[c], vh_ref.at[c], vh_sem.at[c])
    for c in range(nc):
        move(slope_in.at[c], slope_ref.at[c], slope_sem.at[c])
    add_blocks(left, right, (p0, p1, q0, q1))
    r = st_ref[0:1, :]
    unit = e2_ref.shape[1]
    total = nc * fw

    def first(c, s):
        for i in (c, nc + c):
            arrive(gs.at[c, :, pl.ds(0, rw)], gs_sem.at[i])
        arrive(vh_ref.at[c], vh_sem.at[c])
        dgn[c] = dot(gs[c], e2_ref[...], 1, 0)

        def one(at, t):
            d = dgn[c, at, :]
            dv = d * up(vh_ref[c, at, :])
            gf_ref[c, at, 0:1] = lane_sum(dv)
            gf_ref[c, at, 1:2] = lane_sum(d)
            gain = pf[c, at, 1:2]
            return t[0] + token_sum(d * gain), t[1] + token_sum(dv * gain)

        return over(fw, one, s)

    zero = jnp.zeros((1, unit), f32)
    m1, m2 = lax.fori_loop(0, nc, first, (zero, zero))
    m1, m2 = m1 * (1.0 / total), m2 * (1.0 / total)

    def second(c, carry):
        arrive(slope_ref.at[c], slope_sem.at[c])

        def one(at, t):
            dg = r * (dgn[c, at, :] * pf[c, at, 1:2] - m1 - up(vh_ref[c, at, :]) * m2)
            df = (dg * up(slope_ref[c, at, :])).astype(bf16)
            df_ref[c, at, :] = df
            gf_ref[c, at, 2:3] = lane_sum(up(df))
            return t

        over(fw, one)
        return carry

    lax.fori_loop(0, nc, second, 0)


def middle_back_kernel(nc, rw, fw, info, df_ref, x1_ref, e2_ref, pd, *refs):
    pieces = refs[:10]
    dx1_ref, e1_ref, gd_ref, ge, db, ge_sem = refs[10:]
    fetch(pieces, rw, ((0, rw, below(ge, info, nc, rw), ge_sem),))
    db[...] = jnp.zeros(db.shape, f32)

    def one(c, carry):
        for i in (c, nc + c):
            arrive(ge.at[c, pl.ds(0, rw)], ge_sem.at[i])
        db[...] += dot(ge[c], df_ref[c], 1, 0)
        return carry

    lax.fori_loop(0, nc, one, 0)

    def emit(at, dx):
        dy = up(e2_ref[at, :])
        dx1 = dy + dx
        dx1_ref[at, :] = dx1
        e1 = dx1.astype(bf16)
        e1_ref[at, :] = e1
        gd_ref[at, 2:3] = lane_sum(up(e1))
        gd_ref[at, 3:4] = lane_sum(dy)

    norm_back(db, x1_ref, pd, 3, gd_ref, emit)


def middle_grads_kernel(
    nc, hw, rw, fw, info, b_ref, df_ref, on_ref, e1_ref, keep, send,
):
    my_row = info[1]

    def blocks(c, place):
        grad = dot(b_ref[...], df_ref[c], 1, 1).astype(bf16)
        out_grad = dot(on_ref[c], e1_ref[...], 1, 1).astype(bf16)
        half = fw // 2
        for r in range(2):
            ref = place(jnp.bitwise_xor(my_row, r))
            for k in range(2):
                ref[k * rw : (k + 1) * rw, :] = grad[r * rw : (r + 1) * rw, k * half : (k + 1) * half]
            ref[2 * rw :, :] = out_grad[:, r * rw : (r + 1) * rw]

    store_blocks(nc, blocks, keep, send)


def heads_back(first, last, hw, info, qkv_ref, lse_ref, o_ref, do_ref, dqkv_ref, gh_ref, ka, qa, va, oa):
    unit = o_ref.shape[1]
    for_keys, for_queries = segment_rows(info, unit)
    slot = lax.broadcasted_iota(jnp.int32, (16, unit), 0)
    ka[HEAD:, :] = jnp.where(jnp.logical_and(slot >= 4, slot < 7), 1.0, for_keys).astype(bf16)
    va[HEAD:, :] = jnp.where(slot < 3, 1.0, 0.0).astype(bf16)
    nothing = jnp.zeros((16, unit), f32)

    def per_block(c, carry):
        to = lambda j, h: pl.ds(pl.multiple_of(c * 3 * hw + j * hw + h * HEAD, HEAD), HEAD)
        for h in range(hw // HEAD):
            rows = pl.ds(pl.multiple_of(c * hw + h * HEAD, HEAD), HEAD)
            q = qkv_ref[c, h * HEAD : (h + 1) * HEAD, :] * jnp.bfloat16(score_scale)
            k = qkv_ref[c, hw + h * HEAD : hw + (h + 1) * HEAD, :]
            d = do_ref[rows, :]
            inner = jnp.sum(up(d) * o_ref[rows, :], axis=0, keepdims=True)
            qa[0:HEAD, :] = q
            qa[HEAD:, :] = three_rows(for_queries, -lse_ref[c, h : h + 1, :], 4).astype(bf16)
            ka[0:HEAD, :] = k
            va[0:HEAD, :] = qkv_ref[c, 2 * hw + h * HEAD : 2 * hw + (h + 1) * HEAD, :]
            oa[0:HEAD, :] = d
            oa[HEAD:, :] = three_rows(nothing, -inner, 0).astype(bf16)
            p = jnp.exp(dot(ka[...], qa[...], 0, 0))
            ds = (p * dot(va[...], oa[...], 0, 0)).astype(bf16)
            dv = dot(d, p.astype(bf16), 1, 1).astype(bf16)
            dq = (dot(k, ds, 1, 0) * score_scale).astype(bf16)
            dk = dot(q, ds, 1, 1).astype(bf16)
            dqkv_ref[to(0, h), :] = dq
            dqkv_ref[to(1, h), :] = dk
            dqkv_ref[to(2, h), :] = dv
            gh_ref[c, h * HEAD : (h + 1) * HEAD, 0:1] = lane_sum(up(dq))
            gh_ref[c, h * HEAD : (h + 1) * HEAD, 1:2] = lane_sum(up(dv))
        return carry

    lax.fori_loop(first, last, per_block, 0)


def attend_back_kernel(nc, hw, rw, info, e1_ref, o_ref, lse_ref, pd, left, right, qkv_in, *refs):
    pieces = refs[:10]
    dqkv_ref, gd_ref, gh_ref, do_ref, qkv_ref, p0, p1, q0, q1, go, don, ka, qa, va, oa, go_sem, in_sem = refs[10:]
    qkv_copy = move(qkv_in, qkv_ref, in_sem)

    def place(i):
        row = jnp.bitwise_xor(info[1], i // nc)
        return go.at[pl.ds(i % nc * hw, hw), pl.ds(pl.multiple_of(row * rw, rw), rw)]

    fetch(pieces, 4 * hw, ((3 * hw, 4 * hw, place, go_sem),))
    add_blocks(left, right, (p0, p1, q0, q1))
    for i in range(2 * nc):
        arrive(go.at[pl.ds(0, hw), pl.ds(0, rw)], go_sem.at[i])
    don[...] = dot(go[...], e1_ref[...], 1, 0)

    def emit(at, dx):
        do_ref[at, :] = dx.astype(bf16)

    norm_back(don, o_ref, pd, 8, gd_ref, emit)
    qkv_copy.wait()
    heads_back(0, nc // 2, hw, info, qkv_ref, lse_ref, o_ref, do_ref, dqkv_ref, gh_ref, ka, qa, va, oa)


def attend_back_rest_kernel(nc, hw, info, o_ref, qkv_ref, lse_ref, do_ref, _, __, dqkv_ref, gh_ref, ka, qa, va, oa):
    heads_back(nc // 2, nc, hw, info, qkv_ref, lse_ref, o_ref, do_ref, dqkv_ref, gh_ref, ka, qa, va, oa)


def input_back_kernel(nc, hw, rw, info, dqkv, x_ref, dx1_ref, pd, *refs):
    pieces = refs[:10]
    outs_ref, gd_ref, ga, da, ga_sem = refs[10:]

    def place(i):
        row = jnp.bitwise_xor(info[1], i // nc)
        c = i % nc
        rows = pl.ds(c % 2 * 3 * hw, 3 * hw)
        return ga.at[c // 2, rows, pl.ds(pl.multiple_of(row * rw, rw), rw)]

    fetch(pieces, 4 * hw, ((0, 3 * hw, place, ga_sem),))
    for i in range(2 * nc):
        arrive(ga.at[0, pl.ds(0, 3 * hw), pl.ds(0, rw)], ga_sem.at[i])
    da[...] = jnp.zeros(da.shape, f32)

    def one(k, carry):
        rows = pl.ds(pl.multiple_of(k * 6 * hw, 6 * hw), 6 * hw)
        da[...] += dot(ga[k], dqkv[rows, :], 0, 0)
        return carry

    lax.fori_loop(0, nc // 2, one, 0)

    def emit(at, dx):
        apart(outs_ref, at, (dx1_ref[at, :] + dx).astype(bf16))

    norm_back(da, x_ref, pd, 0, gd_ref, emit)


def attend_grads_kernel(
    nc, hw, rw, fl, fw, info, dqkv, a_ref, gd_in, gd_mid, gd_mix, gh, gf_ref, keep, send, wide, thin,
):
    my_row = info[1]
    lane = lax.broadcasted_iota(jnp.int32, (fl, 128), 1)

    def own(i, carry):
        at = pl.ds(pl.multiple_of(i * fl, fl), fl)
        tile = jnp.zeros((fl, 128), f32)
        for k, (ref, j) in enumerate(((gd_in, 0), (gd_in, 1), (gd_mid, 2), (gd_mid, 0), (gd_mid, 1), (gd_mid, 3))):
            tile = jnp.where(lane == k, ref[at, j : j + 1], tile)
        wide[at, :] = tile
        return carry

    lax.fori_loop(0, 2 * nc, own, 0)

    def columns(c, carry):
        tile = jnp.zeros((fl, 128), f32)
        at = 6
        for k in range(hw // fl):
            rows = slice(k * fl, (k + 1) * fl)
            deep = pl.ds(pl.multiple_of(c * hw + k * fl, fl), fl)
            for column in (gh[c, rows, 0:1], gh[c, rows, 1:2], gd_mix[deep, 0:1], gd_mix[deep, 1:2]):
                tile = jnp.where(lane == at, column, tile)
                at += 1
        for k in range(fw // fl):
            rows = slice(k * fl, (k + 1) * fl)
            for column in (gf_ref[c, rows, 2:3], gf_ref[c, rows, 0:1], gf_ref[c, rows, 1:2]):
                tile = jnp.where(lane == at, column, tile)
                at += 1
        thin[c] = tile
        return carry

    lax.fori_loop(0, nc, columns, 0)

    def blocks(c, place):
        grad = dot(dqkv[pl.ds(pl.multiple_of(c * 3 * hw, 3 * hw), 3 * hw), :], a_ref[...], 1, 1).astype(bf16)
        for row in range(2):
            place(jnp.bitwise_xor(my_row, row))[0 : 3 * hw, :] = grad[:, row * rw : (row + 1) * rw]
        for row in range(2):
            block = jnp.bitwise_xor(info[0], row * nc + c)
            tile = thin[c] + wide[pl.ds(pl.multiple_of(block * fl, fl), fl), :]
            third = fl // 3
            tile = jnp.concatenate([tile[m * third : (m + 1) * third] for m in range(3)], axis=1)
            place(row)[3 * hw :, :] = tile.astype(bf16)

    store_blocks(nc, blocks, keep, send)


def shrink_kernel(nc, rw, fw, info, pd, gn_ref, x1_ref, *refs):
    pieces = refs[:10]
    y_ref, gs, gs_sem = refs[10:]
    fetch(pieces, fw, ((0, fw, lambda i: gs.at[i // nc, pl.ds(i % nc * fw, fw)], gs_sem),))
    my_row = info[1]
    for i in range(2 * nc):
        arrive(gs.at[i // nc, pl.ds(i % nc * fw, fw)], gs_sem.at[i])

    def one(r, carry):
        rows = pl.ds(pl.multiple_of(r * rw, rw), rw)
        part = dot(gs[jnp.bitwise_xor(my_row, r)], gn_ref[...], 0, 0)
        apart(y_ref, rows, (x1_ref[rows, :] + part + pd[rows, 5:6]).astype(bf16))
        return carry

    lax.fori_loop(0, 2, one, 0)


def body(
    tokens,
    cotangent,
    holder_of,
    lengths,
    input_gain,
    input_shift,
    attend_weight,
    attend_bias,
    mixed_gain,
    mixed_shift,
    output_weight,
    output_bias,
    middle_gain,
    middle_shift,
    expand_weight,
    expand_bias,
    hidden_gain,
    hidden_shift,
    shrink_weight,
    shrink_bias,
):
    holders = lax.axis_size("dp")
    half = holders // 2
    nr, nc = lax.axis_size("row"), lax.axis_size("col")
    n = nr * nc
    micro = holder_of.shape[0]
    assert micro == n and nr == 2 and nc == 4
    fl = tokens.shape[0]
    pairs = micro * half
    blk = tokens.shape[1] // pairs
    unit = half * blk
    dp = lax.axis_index("dp")
    side, pos = dp // half, dp % half
    my_row, my_col = lax.axis_index("row"), lax.axis_index("col")
    rc = my_row * nc + my_col
    groups = [list(range(s * half * n, (s + 1) * half * n)) for s in range(2)]
    hw, rw, fw = output_weight.shape[0], output_weight.shape[1], shrink_weight.shape[0]

    def flip_row(v):
        return lax.ppermute(v, "row", [(i, i ^ 1) for i in range(nr)])

    def flip_chip(v):
        return lax.ppermute(v, "col", [(i, i ^ 2) for i in range(nc)])

    def flip_core(v):
        return lax.ppermute(v, "col", [(i, i ^ 1) for i in range(nc)])

    def flip_dp(v, step):
        return lax.ppermute(v, "dp", [(i, i ^ step) for i in range(holders)])

    def exchange(v):
        return lax.all_to_all(v, ("dp",) + RC, 0, 0, axis_index_groups=groups, tiled=True)

    lanes = blk % 128 == 0

    def by_target(v):
        v = jnp.transpose(v.reshape(2, fl, half * n, blk), (2, 0, 1, 3))
        return v.reshape(half * n, 2 * fl, blk)

    def exchange_units(v):
        v = exchange(v).reshape(half, n, 2 * fl, blk)
        return v if lanes else jnp.transpose(v, (1, 2, 0, 3)).reshape(1, n, 2 * fl, unit)

    def from_unit(v):
        if not lanes:
            v = jnp.transpose(v.reshape(n * fl, half, blk), (1, 0, 2))
        v = exchange(v.reshape(half * n, fl, blk))
        return jnp.transpose(v, (1, 0, 2)).reshape(tokens.shape)

    def tie(*values):
        return lax.optimization_barrier(values)

    def near(v):
        return flip_row(v), flip_chip(v)

    def far(v, by_row, by_chip):
        h = v.shape[0] // 2
        return flip_row(by_chip[:h]), flip_chip(by_row[h:])

    def near_flips(v, near_v):
        return tuple(flip_core(p) for p in (v, near_v[1], near_v[0]))

    def pieces_of(v, near_v, flips, far_v):
        v1, c1, r1 = flips
        f1, g1 = (flip_core(p) for p in far_v)
        return (v, v1, near_v[1], c1, near_v[0], r1, far_v[0], far_v[1], f1, g1)

    w1 = jnp.concatenate([attend_weight.reshape(3 * hw, rw), output_weight], axis=0)
    near1 = near(w1)
    tile = jnp.concatenate(
        [
            jnp.stack([input_gain, input_shift, output_bias, middle_gain, middle_shift, shrink_bias]),
            jnp.transpose(
                jnp.stack([attend_bias[0], attend_bias[1], mixed_gain, mixed_shift]).reshape(4, -1, fl), (1, 0, 2)
            ).reshape(-1, fl),
            jnp.transpose(jnp.stack([expand_bias, hidden_gain, hidden_shift]).reshape(3, -1, fl), (1, 0, 2)).reshape(-1, fl),
        ]
    )
    tile = jnp.transpose(jnp.pad(tile, ((0, 128 - tile.shape[0]), (0, 0))))
    ready = by_target(jnp.concatenate([tokens, cotangent], axis=0))
    near1, tile, ready = tie(near1, tile, ready)
    far1 = far(w1, *near1)
    both = exchange_units(ready)
    tile_row, tile_chip = near(tile)
    even = jnp.stack([tile, tile_chip, tile_row, flip_row(tile_chip)])
    odd = flip_core(even)
    flips1 = near_flips(w1, near1)
    far1, flips1, both, odd, w2 = tie(far1, flips1, both, odd, expand_weight)
    near2 = near(w2)
    g1 = pieces_of(w1, near1, flips1, far1)

    k_unit = 2 * (pos * n + rc) + side
    own = lengths[k_unit // holders, holder_of[k_unit // holders, k_unit % holders]]
    info = jnp.concatenate([jnp.stack([rc, my_row]), jnp.cumsum(own)[:-1]]).astype(jnp.int32)

    d = n * fl
    split = lambda v: v.reshape(nr, rw, unit)
    dma = pltpu.SemaphoreType.DMA
    weight_flops = 2 * unit * d * nc * fw

    dp_odd = dp % 2 == 1

    def reduce_rest(v):
        step = 2
        while 2 * step < holders:
            v = v + flip_dp(v, step)
            step *= 2
        return v, flip_dp(v, step) if step < holders else jnp.zeros_like(v)

    def spread(v):
        return v, flip_dp(v, 1)

    def whole(v, got):
        return jnp.concatenate([jnp.where(dp_odd, got, v), jnp.where(dp_odd, v, got)], axis=0).astype(f32)

    vm = lambda shape, dtype=bf16: pltpu.VMEM(shape, dtype)
    act, act32, hid = (d, unit), (nc * hw, unit), (nc, fw, unit)
    part1, part2, part3 = (nr, nc // 2, 4 * hw, rw), (nr, nc // 2, rw, fw), (nr, nc // 2, fw, rw)

    def time_us(t):
        return dict(flops=int(t * 1e9), moved=int(t * 1e6))

    extra = vm((HEAD + 16, unit))
    x, a, qkv, lse, o, pd, pf = call(
        functools.partial(attend_kernel, nc, hw, rw, fl, fw),
        (
            sds(act, bf16), sds(act, bf16), sds((nc, 3 * hw, unit), bf16), sds((nc, 8, unit), f32), sds(act, f32),
            sds((d, 16), f32), sds((nc, fw, 8), f32),
        ),
        [SMEM] + [VMEM] * 3 + [HBM] * 10,
        [VMEM, VMEM, HBM, VMEM, VMEM, VMEM, VMEM],
        [
            vm((nc, 3 * hw, unit)), vm((nc, 3 * hw, nr * rw)), extra, extra,
            dma((n,)), dma((nc,)),
        ],
        **time_us(13), name="attend",
    )(info, both, even, odd, *g1)

    o, near2 = tie(o, near2)
    far2 = far(w2, *near2)
    flips2 = near_flips(w2, near2)

    on, x1, b = call(
        functools.partial(output_kernel, nc, hw, rw),
        (sds(act, bf16), sds(act, f32), sds(act, bf16)),
        [SMEM] + [VMEM] * 3 + [HBM] * 10,
        [VMEM] * 3,
        [vm((nr, nc * hw, rw)), dma((n,))],
        **time_us(5), name="output",
    )(info, x, o, pd, *g1)

    b, far2, flips2, w3 = tie(b, far2, flips2, shrink_weight)
    near3 = near(w3)
    g2 = pieces_of(w2, near2, flips2, far2)

    gn, vh, slope, st = call(
        functools.partial(expand_kernel, nc, rw, fw),
        (sds(hid, bf16), sds(hid, bf16), sds(hid, bf16), sds((8, unit), f32)),
        [SMEM, VMEM, VMEM] + [HBM] * 10,
        [VMEM, HBM, HBM, VMEM],
        [vm(hid), vm(hid), vm(hid, f32), vm((nc, nr * rw, fw)), dma((n,)), dma((2 * nc,))],
        **time_us(13), name="expand",
    )(info, b, pf, *g2)

    gn, near3 = tie(gn, near3)
    far3 = far(w3, *near3)
    flips3 = near_flips(w3, near3)

    e2, shr_keep, shr_send = call(
        functools.partial(shrink_grads_kernel, nc, rw),
        (sds(act, bf16), sds(part3, bf16), sds(part3, bf16)),
        [SMEM] + [VMEM] * 2,
        [VMEM] * 3,
        **time_us(7), name="shrink_grads",
    )(info, gn, both)

    shr_send, far3, flips3 = tie(shr_send, far3, flips3)
    g3 = pieces_of(w3, near3, flips3, far3)
    shr_got = flip_core(shr_send)

    def reduce_near(v):
        return flip_row(v[1]), flip_chip(v[3])

    def reduce_far(v, got, name):
        one = sds(v[0].shape[1:], bf16)
        p0, p1, q0, q1 = call(
            sum_near_kernel, (one, one, one, one), [VMEM] * 4, [VMEM] * 4, **time_us(2), name=name
        )(v[0], got[0], v[2], got[1])
        return (p0, q0), (flip_chip(p1), flip_row(q1))

    def reduce_dp(v, got):
        p, q = v[0] + got[0], v[1] + got[1]
        return jnp.where(dp_odd, q, p), flip_dp(jnp.where(dp_odd, p, q), 1)

    sum3 = (nc // 2, fw // 2, rw)
    df, gf, *shr = call(
        functools.partial(hidden_back_kernel, nc, rw, fw),
        (sds(hid, bf16), sds((nc, fw, 8), f32)) + (sds(sum3, bf16),) * 4,
        [SMEM] + [VMEM] * 5 + [HBM] * 12,
        [VMEM] * 6,
        [vm(hid), vm(hid), vm((nc, fw, nr * rw)), vm(hid, f32), dma((n,)), dma((nc,)), dma((nc,))],
        **time_us(13), name="hidden_back",
    )(info, st, e2, pf, shr_keep, shr_got, vh, slope, *g3)

    shr_near = reduce_near(shr)

    dx1, e1, gd_mid = call(
        functools.partial(middle_back_kernel, nc, rw, fw),
        (sds(act, f32), sds(act, bf16), sds((d, 8), f32)),
        [SMEM] + [VMEM] * 4 + [HBM] * 10,
        [VMEM] * 3,
        [vm((nc, nr * rw, fw)), vm(act, f32), dma((n,))],
        **time_us(8), name="middle_back",
    )(info, df, x1, e2, pd, *g2)

    rows2 = 2 * rw + hw
    part2 = (nr, nc // 2, rows2, rw)
    sum2 = (nc // 2, rows2 // 2, rw)
    mid_keep, mid_send = call(
        functools.partial(middle_grads_kernel, nc, hw, rw, fw),
        (sds(part2, bf16), sds(part2, bf16)),
        [SMEM] + [VMEM] * 4,
        [VMEM] * 2,
        **time_us(7), name="middle_grads",
    )(info, b, df, on.reshape(nc, hw, unit), e1)

    e1, mid_send, shr_near = tie(e1, mid_send, shr_near)
    mid_got = flip_core(mid_send)
    shr_stay, shr_far = reduce_far(shr, shr_near, "shrink_sum")

    all_heads = (nc * 3 * hw, unit)
    dqkv, gd_mix, gh, do, qkv, *mid = call(
        functools.partial(attend_back_kernel, nc, hw, rw),
        (sds(all_heads, bf16), sds((d, 8), f32), sds((nc, hw, 8), f32), sds(act, bf16), sds(qkv.shape, bf16))
        + (sds(sum2, bf16),) * 4,
        [SMEM] + [VMEM] * 6 + [HBM] * 11,
        [VMEM] * 9,
        [vm((nc * hw, nr * rw)), vm(act, f32), extra, extra, extra, extra, dma((n,)), dma(())],
        **time_us(11), name="attend_back",
    )(info, e1, o, lse, pd, mid_keep, mid_got, qkv, *g1)

    do, shr_far, mid = tie(do, shr_far, mid)
    shr, shr_dp = reduce_dp(shr_stay, shr_far)
    mid_near = reduce_near(mid)

    dqkv, gh = call(
        functools.partial(attend_back_rest_kernel, nc, hw),
        (sds(all_heads, bf16), sds((nc, hw, 8), f32)),
        [SMEM] + [VMEM] * 6,
        [VMEM] * 2,
        [extra, extra, extra, extra],
        **time_us(8), name="attend_back_rest", aliases={5: 0, 6: 1},
    )(info, o, qkv, lse, do, dqkv, gh)

    dqkv, shr_dp = tie(dqkv, shr_dp)
    shr, shr_rest = reduce_rest(shr + shr_dp)

    input_grad, gd_in = call(
        functools.partial(input_back_kernel, nc, hw, rw),
        (sds((half if lanes else 1, d, blk if lanes else unit), bf16), sds((d, 8), f32)),
        [SMEM] + [VMEM] * 4 + [HBM] * 10,
        [VMEM] * 2,
        [vm((2, nc // 2 * 3 * hw, nr * rw)), vm(act, f32), dma((n,))],
        **time_us(7), name="input_back",
    )(info, dqkv, x, dx1, pd, *g1)

    gd_in, mid_near = tie(gd_in, mid_near)
    p, q = mid[0] + mid_near[0], mid[2] + mid_near[1]
    mid_stay, mid_far = (p[0], q[0]), (flip_chip(p[1]), flip_row(q[1]))

    rows1 = 3 * hw + fl // 3
    part1 = (nr, nc // 2, rows1, rw)
    att_keep, att_send = call(
        functools.partial(attend_grads_kernel, nc, hw, rw, fl, fw),
        (sds(part1, bf16), sds(part1, bf16)),
        [SMEM] + [VMEM] * 7,
        [VMEM] * 2,
        [vm((d, 128), f32), vm((nc, fl, 128), f32)],
        **time_us(7), name="attend_grads",
    )(info, dqkv, a, gd_in, gd_mid, gd_mix, gh, gf)

    att_send, shr_rest, mid_far = tie(att_send, shr_rest, mid_far)
    att_got = flip_core(att_send)
    mid, mid_dp = reduce_dp(mid_stay, mid_far)
    shr, shr_got = spread(shr + shr_rest)
    h = rows1 // 2
    p1, q1 = att_keep[1, :, :h] + att_got[1, :, :h], att_keep[:, 1, h:] + att_got[:, 1, h:]
    p1, q1, y_in = tie(p1, q1, gn)
    p_row, q_chip = flip_row(p1), flip_chip(q1)

    y = call(
        functools.partial(shrink_kernel, nc, rw, fw),
        sds(input_grad.shape, bf16),
        [SMEM] + [VMEM] * 3 + [HBM] * 10,
        VMEM,
        [vm((nr, nc * fw, rw)), dma((n,))],
        **time_us(8), name="shrink",
    )(info, pd, y_in.reshape(nc * fw, unit), x1, *g3)

    y, mid_dp, shr_got, input_grad = tie(y, mid_dp, shr_got, input_grad)
    mid, mid_rest = reduce_rest(mid + mid_dp)
    mid, p_row, q_chip = tie(mid, p_row, q_chip)
    p = att_keep[0, :, :h] + att_got[0, :, :h] + p_row
    q = att_keep[:, 0, h:] + att_got[:, 0, h:] + q_chip
    att_far = flip_chip(p[1]), flip_row(q[1])
    input_grad = from_unit(input_grad)
    att, att_dp = reduce_dp((p[0], q[0]), att_far)
    att_dp, mid_rest, y = tie(att_dp, mid_rest, y)
    block_out = from_unit(y)
    att, att_rest = reduce_rest(att + att_dp)
    mid, mid_got = spread(mid + mid_rest)
    att, att_got = spread(att + att_rest)
    att_got, mid_got, shr_got = tie(att_got, mid_got, shr_got)
    att, mid, shr_w_g = whole(att, att_got), whole(mid, mid_got), whole(shr, shr_got)
    exp_w_g = jnp.concatenate([mid[:rw], mid[rw : 2 * rw]], axis=1)

    thin = att[3 * hw :]
    thin = jnp.transpose(jnp.concatenate([thin[:, k * 128 : (k + 1) * 128] for k in range(3)], axis=0))
    in_g_g, in_s_g, out_b_g, mid_g_g, mid_s_g, shr_b_g = (thin[i] for i in range(6))
    at = 6 + 4 * (hw // fl)
    heads_g = jnp.transpose(thin[6:at].reshape(-1, 4, fl), (1, 0, 2)).reshape(4, hw)
    hidden_g = jnp.transpose(thin[at : at + 3 * (fw // fl)].reshape(-1, 3, fl), (1, 0, 2)).reshape(3, fw)
    q_b_g, v_b_g, mix_g_g, mix_s_g = heads_g
    exp_b_g, hid_g_g, hid_s_g = hidden_g
    return (
        block_out,
        input_grad,
        in_g_g,
        in_s_g,
        att[: 3 * hw].reshape(attend_weight.shape),
        jnp.stack([q_b_g, v_b_g]),
        mix_g_g,
        mix_s_g,
        mid[2 * rw :],
        out_b_g,
        mid_g_g,
        mid_s_g,
        exp_w_g,
        exp_b_g,
        hid_g_g,
        hid_s_g,
        shr_w_g,
        shr_b_g,
    )


def solution(mesh):
    wide, narrow = P(RC), P("col")
    in_specs = (
        P(RC, "dp"), P(RC, "dp"), P(), P(), wide, wide, P(None, "col", "row"), P(None, "col"),
        narrow, narrow, P("col", "row"), wide, wide, wide, P("row", "col"), narrow, narrow, narrow,
        P("col", "row"), wide,
    )
    out_specs = (
        P(RC, "dp"), P(RC, "dp"), wide, wide, P(None, "col", "row"), P(None, "col"), narrow, narrow,
        P("col", "row"), wide, wide, wide, P("row", "col"), narrow, narrow, narrow, P("col", "row"),
        wide,
    )
    return jax.shard_map(body, mesh=mesh, in_specs=in_specs, out_specs=out_specs, check_vma=False)
```

```python
import functools
import math

import jax
import jax.numpy as jnp
from jax import lax
from jax.experimental import pallas as pl
from jax.experimental.pallas import tpu as pltpu
from jax.sharding import PartitionSpec as P

HEAD = 64
eps = 1e-05
masked_score = -1e30
f32 = jnp.float32
bf16 = jnp.bfloat16
RC = ("row", "col")
HBM = pl.BlockSpec(memory_space=pltpu.HBM)
SMEM = pl.BlockSpec(memory_space=pltpu.SMEM)
VMEM = pl.BlockSpec(memory_space=pltpu.VMEM)
LOOSE = pl.BlockSpec(memory_space=pltpu.VMEM)
root_half = math.sqrt(0.5)
root_tau = 1.0 / math.sqrt(2.0 * math.pi)
score_scale = 1.0 / math.sqrt(HEAD)


def dot(a, b, ca, cb):
    return lax.dot_general(a, b, (((ca,), (cb,)), ((), ())), preferred_element_type=f32)


def up(v):
    return v.astype(f32)


def lane_sum(v):
    return jnp.sum(v, axis=1, keepdims=True)


def token_sum(v):
    return jnp.sum(v, axis=0, keepdims=True)


CHUNK = 768
ROOM = 8


def over(rows, step, init=0, chunk=CHUNK):
    def one(i, carry):
        return step(pl.ds(pl.multiple_of(i * chunk, chunk), chunk), carry)

    return lax.fori_loop(0, rows // chunk, one, init)


def moments(ref, chunk=CHUNK):
    rows, unit = ref.shape
    zero = jnp.zeros((1, unit), f32)
    mu = over(rows, lambda at, s: s + token_sum(up(ref[at, :])), zero, chunk) * (1.0 / rows)

    def square(at, s):
        d = up(ref[at, :]) - mu
        return s + token_sum(d * d)

    return mu, lax.rsqrt(over(rows, square, zero, chunk) * (1.0 / rows) + eps)


def norm(out, ref, pd, gain, shift):
    mu, r = moments(ref, CHUNK // 2)

    def one(at, carry):
        out[at, :] = ((up(ref[at, :]) - mu) * r * pd[at, gain : gain + 1] + pd[at, shift : shift + 1]).astype(bf16)
        return carry

    over(ref.shape[0], one, chunk=CHUNK // 2)


def norm_back(grad, ref, pd, gain, gd, emit):
    rows, unit = ref.shape
    mu, r = moments(ref, CHUNK // 2)
    zero = jnp.zeros((1, unit), f32)

    def first(at, s):
        g = grad[at, :]
        gv = g * ((up(ref[at, :]) - mu) * r)
        gd[at, 0:1] = lane_sum(gv)
        gd[at, 1:2] = lane_sum(g)
        k = pd[at, gain : gain + 1]
        return s[0] + token_sum(g * k), s[1] + token_sum(gv * k)

    m1, m2 = over(rows, first, (zero, zero))
    m1, m2 = m1 * (1.0 / rows), m2 * (1.0 / rows)

    def second(at, carry):
        vh = (up(ref[at, :]) - mu) * r
        emit(at, r * (grad[at, :] * pd[at, gain : gain + 1] - m1 - vh * m2))
        return carry

    over(rows, second)


PIECES = ((0, None), (1, None), (2, None), (3, None), (4, None), (5, None), (6, 0), (6, 1), (7, 0), (7, 1))


def fetch(pieces, rows, parts):
    for ref, (block, half) in zip(pieces, PIECES):
        first, last = (0, rows) if half is None else (half * rows // 2, (half + 1) * rows // 2)
        for lo, hi, place, sem in parts:
            a, b = max(lo, first), min(hi, last)
            if a < b:
                pltpu.make_async_copy(
                    ref.at[pl.ds(a - first, b - a)], place(block).at[pl.ds(a - lo, b - a)], sem.at[block]
                ).start()


def arrive(ref, sem):
    pltpu.make_async_copy(ref, ref, sem).wait()


def move(src, dst, sem):
    copy = pltpu.make_async_copy(src, dst, sem)
    copy.start()
    return copy


def vmem_bytes(shape, dtype):
    size = jnp.dtype(dtype).itemsize
    sublanes, lanes = 32 // size, 128
    *lead, rows, columns = (1,) * max(0, 2 - len(shape)) + tuple(shape)
    return math.prod(lead) * (-(-rows // sublanes) * sublanes) * (-(-columns // lanes) * lanes) * size


def pinned(spec):
    return pltpu.VMEM if spec is VMEM else pltpu.HBM


def call(kernel, outs, in_specs, out_specs, scratch=(), flops=0, moved=0, name=None, aliases=None):
    held = [v for v in scratch if v.memory_space == pltpu.VMEM]
    limit = sum(vmem_bytes(v.shape, v.dtype) for v in held) + (ROOM << 20)
    single = not isinstance(outs, tuple)
    places = [v if spec is LOOSE else pinned(spec)(v.shape, v.dtype) for v, spec in zip((outs,) if single else outs, (out_specs,) if single else out_specs)]

    def run(*args):
        args = [v if spec is SMEM or spec is LOOSE else pltpu.with_memory_space_constraint(v, pinned(spec)) for v, spec in zip(args, in_specs)]
        return pl.pallas_call(
            kernel,
            out_shape=places[0] if single else tuple(places),
            in_specs=in_specs,
            out_specs=out_specs,
            scratch_shapes=list(scratch),
            compiler_params=pltpu.CompilerParams(vmem_limit_bytes=limit),
            cost_estimate=pl.CostEstimate(flops=flops, bytes_accessed=moved, transcendentals=0),
            name=name,
            input_output_aliases=aliases or {},
        )(*args)

    return run


def sds(shape, dtype):
    return jax.ShapeDtypeStruct(shape, dtype)


def segment_rows(info, unit):
    t = lax.broadcasted_iota(jnp.int32, (16, unit), 1)
    slot = lax.broadcasted_iota(jnp.int32, (16, unit), 0)
    one = lambda b: jnp.where(t >= b, 1, 0)
    seg = one(info[2]) + one(info[3]) + one(info[4])
    same = seg == slot
    for_keys = jnp.where(same, 1.0, 0.0)
    for_queries = jnp.where(jnp.logical_and(slot < 4, jnp.logical_not(same)), masked_score, 0.0)
    return for_keys, for_queries


def split3(v):
    hi = v.astype(bf16)
    v = v - up(hi)
    mid = v.astype(bf16)
    return hi, mid, (v - up(mid)).astype(bf16)


def three_rows(base, v, first):
    row = lax.broadcasted_iota(jnp.int32, base.shape, 0)
    for i, part in enumerate(split3(v)):
        base = jnp.where(row == first + i, up(part), base)
    return base


def unit_of(ref, which):
    blocks, n, rows, _ = ref.shape
    rows //= 2
    return jnp.concatenate(
        [
            jnp.concatenate([ref[k, i, which * rows : (which + 1) * rows, :] for i in range(n)], axis=0)
            for k in range(blocks)
        ],
        axis=1,
    )


def apart(ref, at, value):
    width = ref.shape[2]
    for i in range(ref.shape[0]):
        ref[i, at, :] = value[:, i * width : (i + 1) * width]


def beside(ref, info, nc, rw):
    def place(i):
        row = jnp.bitwise_xor(info[1], i // nc)
        return ref.at[i % nc, :, pl.ds(pl.multiple_of(row * rw, rw), rw)]

    return place


def below(ref, info, nc, rw):
    def place(i):
        row = jnp.bitwise_xor(info[1], i // nc)
        return ref.at[i % nc, pl.ds(pl.multiple_of(row * rw, rw), rw)]

    return place


def attend_kernel(nc, hw, rw, fl, fw, info, both, even, odd, *refs):
    pieces = refs[:10]
    x_ref, a_ref, qkv_out, lse_ref, o_ref, pd, pf = refs[10:17]
    qkv_ref, ga, ka, qa, ga_sem, out_sem = refs[17:]
    unit = o_ref.shape[1]
    fetch(pieces, 4 * hw, ((0, 3 * hw, beside(ga, info, nc, rw), ga_sem),))
    for i in range(2 * nc):
        tile = (even, odd)[i % 2][i // 2]
        pd[pl.ds(pl.multiple_of(jnp.bitwise_xor(info[0], i) * fl, fl), fl), 0:6] = tile[:, 0:6]
        if i < nc:
            for k in range(hw // fl):
                pd[i * hw + k * fl : i * hw + (k + 1) * fl, 6:10] = tile[:, 6 + 4 * k : 10 + 4 * k]
            for k in range(fw // fl):
                first = 6 + 4 * (hw // fl) + 3 * k
                pf[i, k * fl : (k + 1) * fl, 0:3] = tile[:, first : first + 3]
    x_ref[...] = unit_of(both, 0)
    norm(a_ref, x_ref, pd, 0, 1)
    for_keys, for_queries = segment_rows(info, unit)
    ka[HEAD:, :] = for_keys.astype(bf16)
    qa[HEAD:, :] = for_queries.astype(bf16)

    def per_block(c, carry):
        for i in (c, nc + c):
            arrive(ga.at[c, :, pl.ds(0, rw)], ga_sem.at[i])
        trip = dot(ga[c], a_ref[...], 1, 0)
        at = pl.multiple_of(c * hw, hw)
        qkv_ref[c, 0:hw, :] = (trip[0:hw] + pd[pl.ds(at, hw), 6:7]).astype(bf16)
        qkv_ref[c, hw : 2 * hw, :] = trip[hw : 2 * hw].astype(bf16)
        qkv_ref[c, 2 * hw :, :] = (trip[2 * hw :] + pd[pl.ds(at, hw), 7:8]).astype(bf16)
        move(qkv_ref.at[c], qkv_out.at[c], out_sem.at[c])
        for h in range(hw // HEAD):
            qa[0:HEAD, :] = qkv_ref[c, h * HEAD : (h + 1) * HEAD, :] * jnp.bfloat16(score_scale)
            ka[0:HEAD, :] = qkv_ref[c, hw + h * HEAD : hw + (h + 1) * HEAD, :]
            v = qkv_ref[c, 2 * hw + h * HEAD : 2 * hw + (h + 1) * HEAD, :]
            s = dot(ka[...], qa[...], 0, 0)
            top = jnp.max(s, axis=0, keepdims=True)
            e = jnp.exp(s - top)
            den = token_sum(e)
            o = dot(v, e.astype(bf16), 1, 0) * (1.0 / den)
            o_ref[pl.ds(pl.multiple_of(c * hw + h * HEAD, HEAD), HEAD), :] = o
            lse_ref[c, h : h + 1, :] = top + jnp.log(den)
        return carry

    lax.fori_loop(0, nc, per_block, 0)
    for c in range(nc):
        arrive(qkv_ref.at[c], out_sem.at[c])


def output_kernel(nc, hw, rw, info, x_ref, o_ref, pd, *refs):
    pieces = refs[:10]
    on_ref, x1_ref, b_ref, go, go_sem = refs[10:]
    fetch(pieces, 4 * hw, ((3 * hw, 4 * hw, lambda i: go.at[i // nc, pl.ds(i % nc * hw, hw)], go_sem),))
    my_row = info[1]
    norm(on_ref, o_ref, pd, 8, 9)
    for i in range(2 * nc):
        arrive(go.at[i // nc, pl.ds(i % nc * hw, hw)], go_sem.at[i])

    def one(r, carry):
        rows = pl.ds(pl.multiple_of(r * rw, rw), rw)
        x1_ref[rows, :] = dot(go[jnp.bitwise_xor(my_row, r)], on_ref[...], 0, 0) + up(x_ref[rows, :]) + pd[rows, 2:3]
        return carry

    lax.fori_loop(0, 2, one, 0)
    norm(b_ref, x1_ref, pd, 3, 4)


def expand_kernel(nc, rw, fw, info, b_ref, pf, *refs):
    pieces = refs[:10]
    gn_ref, vh_out, slope_out, st_ref = refs[10:14]
    vh_ref, slope_ref, g_ref, ge, ge_sem, out_sem = refs[14:]
    fetch(pieces, rw, ((0, rw, below(ge, info, nc, rw), ge_sem),))
    unit = b_ref.shape[1]
    total = nc * fw

    def first(c, s):
        for i in (c, nc + c):
            arrive(ge.at[c, pl.ds(0, rw)], ge_sem.at[i])
        f = dot(ge[c], b_ref[...], 0, 0) + pf[c, :, 0:1]
        phi = 0.5 * (1.0 + lax.erf(f * root_half))
        g = f * phi
        g_ref[c] = g
        slope_ref[c] = (phi + f * (jnp.exp(-0.5 * f * f) * root_tau)).astype(bf16)
        move(slope_ref.at[c], slope_out.at[c], out_sem.at[c])
        return s + token_sum(g)

    mu = lax.fori_loop(0, nc, first, jnp.zeros((1, unit), f32)) * (1.0 / total)

    def second(c, s):
        def square(at, t):
            d = g_ref[c, at, :] - mu
            return t + token_sum(d * d)

        return over(fw, square, s)

    r = lax.rsqrt(lax.fori_loop(0, nc, second, jnp.zeros((1, unit), f32)) * (1.0 / total) + eps)
    st_ref[...] = jnp.broadcast_to(r, st_ref.shape)

    def third(c, carry):
        def one(at, t):
            vh = (g_ref[c, at, :] - mu) * r
            vh_ref[c, at, :] = vh.astype(bf16)
            gn_ref[c, at, :] = (vh * pf[c, at, 1:2] + pf[c, at, 2:3]).astype(bf16)
            return t

        over(fw, one)
        move(vh_ref.at[c], vh_out.at[c], out_sem.at[nc + c])
        return carry

    lax.fori_loop(0, nc, third, 0)
    for c in range(nc):
        arrive(slope_ref.at[c], out_sem.at[c])
        arrive(vh_ref.at[c], out_sem.at[nc + c])


def store_blocks(nc, blocks, keep, send):
    def one(k, carry):
        for ref, c in ((send, 2 * k + 1), (keep, 2 * k)):
            blocks(c, lambda row: ref.at[row, k])
        return carry

    lax.fori_loop(0, nc // 2, one, 0)


def shrink_grads_kernel(nc, rw, info, gn_ref, both, e2_ref, keep, send):
    my_row = info[1]
    e2_ref[...] = unit_of(both, 1)

    def blocks(c, place):
        grad = dot(gn_ref[c], e2_ref[...], 1, 1).astype(bf16)
        for r in range(2):
            place(jnp.bitwise_xor(my_row, r))[...] = grad[:, r * rw : (r + 1) * rw]

    store_blocks(nc, blocks, keep, send)


def add_blocks(left, right, outs):
    h = left.shape[2] // 2
    for j in range(4):
        r, c = j // 2, j % 2
        outs[r][c] = (up(left[r, c, :h]) + up(right[r, c, :h])).astype(bf16)
        outs[2 + c][r] = (up(left[r, c, h:]) + up(right[r, c, h:])).astype(bf16)


def sum_near_kernel(row_own, row_got, chip_own, chip_got, p0, p1, q0, q1):
    for own, got, outs in ((row_own, row_got, (p0, p1)), (chip_own, chip_got, (q0, q1))):
        for i in range(2):
            outs[i][...] = (up(own[i]) + up(got[i])).astype(bf16)


def hidden_back_kernel(nc, rw, fw, info, st_ref, e2_ref, pf, left, right, vh_in, slope_in, *refs):
    pieces = refs[:10]
    df_ref, gf_ref, p0, p1, q0, q1 = refs[10:16]
    vh_ref, slope_ref, gs, dgn, gs_sem, vh_sem, slope_sem = refs[16:]
    fetch(pieces, fw, ((0, fw, beside(gs, info, nc, rw), gs_sem),))
    for c in range(nc):
        move(vh_in.at[c], vh_ref.at[c], vh_sem.at[c])
    for c in range(nc):
        move(slope_in.at[c], slope_ref.at[c], slope_sem.at[c])
    add_blocks(left, right, (p0, p1, q0, q1))
    r = st_ref[0:1, :]
    unit = e2_ref.shape[1]
    total = nc * fw

    def first(c, s):
        for i in (c, nc + c):
            arrive(gs.at[c, :, pl.ds(0, rw)], gs_sem.at[i])
        arrive(vh_ref.at[c], vh_sem.at[c])
        dgn[c] = dot(gs[c], e2_ref[...], 1, 0)

        def one(at, t):
            d = dgn[c, at, :]
            dv = d * up(vh_ref[c, at, :])
            gf_ref[c, at, 0:1] = lane_sum(dv)
            gf_ref[c, at, 1:2] = lane_sum(d)
            gain = pf[c, at, 1:2]
            return t[0] + token_sum(d * gain), t[1] + token_sum(dv * gain)

        return over(fw, one, s)

    zero = jnp.zeros((1, unit), f32)
    m1, m2 = lax.fori_loop(0, nc, first, (zero, zero))
    m1, m2 = m1 * (1.0 / total), m2 * (1.0 / total)

    def second(c, carry):
        arrive(slope_ref.at[c], slope_sem.at[c])

        def one(at, t):
            dg = r * (dgn[c, at, :] * pf[c, at, 1:2] - m1 - up(vh_ref[c, at, :]) * m2)
            df = (dg * up(slope_ref[c, at, :])).astype(bf16)
            df_ref[c, at, :] = df
            gf_ref[c, at, 2:3] = lane_sum(up(df))
            return t

        over(fw, one)
        return carry

    lax.fori_loop(0, nc, second, 0)


def middle_back_kernel(nc, rw, fw, info, df_ref, x1_ref, e2_ref, pd, *refs):
    pieces = refs[:10]
    dx1_ref, e1_ref, gd_ref, ge, db, ge_sem = refs[10:]
    fetch(pieces, rw, ((0, rw, below(ge, info, nc, rw), ge_sem),))
    db[...] = jnp.zeros(db.shape, f32)

    def one(c, carry):
        for i in (c, nc + c):
            arrive(ge.at[c, pl.ds(0, rw)], ge_sem.at[i])
        db[...] += dot(ge[c], df_ref[c], 1, 0)
        return carry

    lax.fori_loop(0, nc, one, 0)

    def emit(at, dx):
        dy = up(e2_ref[at, :])
        dx1 = dy + dx
        dx1_ref[at, :] = dx1
        e1 = dx1.astype(bf16)
        e1_ref[at, :] = e1
        gd_ref[at, 2:3] = lane_sum(up(e1))
        gd_ref[at, 3:4] = lane_sum(dy)

    norm_back(db, x1_ref, pd, 3, gd_ref, emit)


def middle_grads_kernel(
    nc, hw, rw, fw, info, b_ref, df_ref, on_ref, e1_ref, keep, send,
):
    my_row = info[1]

    def blocks(c, place):
        grad = dot(b_ref[...], df_ref[c], 1, 1).astype(bf16)
        out_grad = dot(on_ref[c], e1_ref[...], 1, 1).astype(bf16)
        half = fw // 2
        for r in range(2):
            ref = place(jnp.bitwise_xor(my_row, r))
            for k in range(2):
                ref[k * rw : (k + 1) * rw, :] = grad[r * rw : (r + 1) * rw, k * half : (k + 1) * half]
            ref[2 * rw :, :] = out_grad[:, r * rw : (r + 1) * rw]

    store_blocks(nc, blocks, keep, send)


def heads_back(first, last, hw, info, qkv_ref, lse_ref, o_ref, do_ref, dqkv_ref, gh_ref, ka, qa, va, oa):
    unit = o_ref.shape[1]
    for_keys, for_queries = segment_rows(info, unit)
    slot = lax.broadcasted_iota(jnp.int32, (16, unit), 0)
    ka[HEAD:, :] = jnp.where(jnp.logical_and(slot >= 4, slot < 7), 1.0, for_keys).astype(bf16)
    va[HEAD:, :] = jnp.where(slot < 3, 1.0, 0.0).astype(bf16)
    nothing = jnp.zeros((16, unit), f32)

    def per_block(c, carry):
        to = lambda j, h: pl.ds(pl.multiple_of(c * 3 * hw + j * hw + h * HEAD, HEAD), HEAD)
        for h in range(hw // HEAD):
            rows = pl.ds(pl.multiple_of(c * hw + h * HEAD, HEAD), HEAD)
            q = qkv_ref[c, h * HEAD : (h + 1) * HEAD, :] * jnp.bfloat16(score_scale)
            k = qkv_ref[c, hw + h * HEAD : hw + (h + 1) * HEAD, :]
            d = do_ref[rows, :]
            inner = jnp.sum(up(d) * o_ref[rows, :], axis=0, keepdims=True)
            qa[0:HEAD, :] = q
            qa[HEAD:, :] = three_rows(for_queries, -lse_ref[c, h : h + 1, :], 4).astype(bf16)
            ka[0:HEAD, :] = k
            va[0:HEAD, :] = qkv_ref[c, 2 * hw + h * HEAD : 2 * hw + (h + 1) * HEAD, :]
            oa[0:HEAD, :] = d
            oa[HEAD:, :] = three_rows(nothing, -inner, 0).astype(bf16)
            p = jnp.exp(dot(ka[...], qa[...], 0, 0))
            ds = (p * dot(va[...], oa[...], 0, 0)).astype(bf16)
            dv = dot(d, p.astype(bf16), 1, 1).astype(bf16)
            dq = (dot(k, ds, 1, 0) * score_scale).astype(bf16)
            dk = dot(q, ds, 1, 1).astype(bf16)
            dqkv_ref[to(0, h), :] = dq
            dqkv_ref[to(1, h), :] = dk
            dqkv_ref[to(2, h), :] = dv
            gh_ref[c, h * HEAD : (h + 1) * HEAD, 0:1] = lane_sum(up(dq))
            gh_ref[c, h * HEAD : (h + 1) * HEAD, 1:2] = lane_sum(up(dv))
        return carry

    lax.fori_loop(first, last, per_block, 0)


def attend_back_kernel(nc, hw, rw, info, e1_ref, o_ref, lse_ref, pd, left, right, qkv_in, *refs):
    pieces = refs[:10]
    dqkv_ref, gd_ref, gh_ref, do_ref, qkv_ref, p0, p1, q0, q1, go, don, ka, qa, va, oa, go_sem, in_sem = refs[10:]
    qkv_copy = move(qkv_in, qkv_ref, in_sem)

    def place(i):
        row = jnp.bitwise_xor(info[1], i // nc)
        return go.at[pl.ds(i % nc * hw, hw), pl.ds(pl.multiple_of(row * rw, rw), rw)]

    fetch(pieces, 4 * hw, ((3 * hw, 4 * hw, place, go_sem),))
    add_blocks(left, right, (p0, p1, q0, q1))
    for i in range(2 * nc):
        arrive(go.at[pl.ds(0, hw), pl.ds(0, rw)], go_sem.at[i])
    don[...] = dot(go[...], e1_ref[...], 1, 0)

    def emit(at, dx):
        do_ref[at, :] = dx.astype(bf16)

    norm_back(don, o_ref, pd, 8, gd_ref, emit)
    qkv_copy.wait()
    heads_back(0, nc // 2, hw, info, qkv_ref, lse_ref, o_ref, do_ref, dqkv_ref, gh_ref, ka, qa, va, oa)


def attend_back_rest_kernel(nc, hw, info, o_ref, qkv_ref, lse_ref, do_ref, _, __, dqkv_ref, gh_ref, ka, qa, va, oa):
    heads_back(nc // 2, nc, hw, info, qkv_ref, lse_ref, o_ref, do_ref, dqkv_ref, gh_ref, ka, qa, va, oa)


def input_back_kernel(nc, hw, rw, info, dqkv, x_ref, dx1_ref, pd, *refs):
    pieces = refs[:10]
    outs_ref, gd_ref, ga, da, ga_sem = refs[10:]

    def place(i):
        row = jnp.bitwise_xor(info[1], i // nc)
        c = i % nc
        rows = pl.ds(c % 2 * 3 * hw, 3 * hw)
        return ga.at[c // 2, rows, pl.ds(pl.multiple_of(row * rw, rw), rw)]

    fetch(pieces, 4 * hw, ((0, 3 * hw, place, ga_sem),))
    for i in range(2 * nc):
        arrive(ga.at[0, pl.ds(0, 3 * hw), pl.ds(0, rw)], ga_sem.at[i])
    da[...] = jnp.zeros(da.shape, f32)

    def one(k, carry):
        rows = pl.ds(pl.multiple_of(k * 6 * hw, 6 * hw), 6 * hw)
        da[...] += dot(ga[k], dqkv[rows, :], 0, 0)
        return carry

    lax.fori_loop(0, nc // 2, one, 0)

    def emit(at, dx):
        apart(outs_ref, at, (dx1_ref[at, :] + dx).astype(bf16))

    norm_back(da, x_ref, pd, 0, gd_ref, emit)


def attend_grads_kernel(
    nc, hw, rw, fl, fw, info, dqkv, a_ref, gd_in, gd_mid, gd_mix, gh, gf_ref, keep, send, wide, thin,
):
    my_row = info[1]
    lane = lax.broadcasted_iota(jnp.int32, (fl, 128), 1)

    def own(i, carry):
        at = pl.ds(pl.multiple_of(i * fl, fl), fl)
        tile = jnp.zeros((fl, 128), f32)
        for k, (ref, j) in enumerate(((gd_in, 0), (gd_in, 1), (gd_mid, 2), (gd_mid, 0), (gd_mid, 1), (gd_mid, 3))):
            tile = jnp.where(lane == k, ref[at, j : j + 1], tile)
        wide[at, :] = tile
        return carry

    lax.fori_loop(0, 2 * nc, own, 0)

    def columns(c, carry):
        tile = jnp.zeros((fl, 128), f32)
        at = 6
        for k in range(hw // fl):
            rows = slice(k * fl, (k + 1) * fl)
            deep = pl.ds(pl.multiple_of(c * hw + k * fl, fl), fl)
            for column in (gh[c, rows, 0:1], gh[c, rows, 1:2], gd_mix[deep, 0:1], gd_mix[deep, 1:2]):
                tile = jnp.where(lane == at, column, tile)
                at += 1
        for k in range(fw // fl):
            rows = slice(k * fl, (k + 1) * fl)
            for column in (gf_ref[c, rows, 2:3], gf_ref[c, rows, 0:1], gf_ref[c, rows, 1:2]):
                tile = jnp.where(lane == at, column, tile)
                at += 1
        thin[c] = tile
        return carry

    lax.fori_loop(0, nc, columns, 0)

    def blocks(c, place):
        grad = dot(dqkv[pl.ds(pl.multiple_of(c * 3 * hw, 3 * hw), 3 * hw), :], a_ref[...], 1, 1).astype(bf16)
        for row in range(2):
            place(jnp.bitwise_xor(my_row, row))[0 : 3 * hw, :] = grad[:, row * rw : (row + 1) * rw]
        for row in range(2):
            block = jnp.bitwise_xor(info[0], row * nc + c)
            tile = thin[c] + wide[pl.ds(pl.multiple_of(block * fl, fl), fl), :]
            third = fl // 3
            tile = jnp.concatenate([tile[m * third : (m + 1) * third] for m in range(3)], axis=1)
            place(row)[3 * hw :, :] = tile.astype(bf16)

    store_blocks(nc, blocks, keep, send)


def shrink_kernel(nc, rw, fw, info, pd, gn_ref, x1_ref, *refs):
    pieces = refs[:10]
    y_ref, gs, gs_sem = refs[10:]
    fetch(pieces, fw, ((0, fw, lambda i: gs.at[i // nc, pl.ds(i % nc * fw, fw)], gs_sem),))
    my_row = info[1]
    for i in range(2 * nc):
        arrive(gs.at[i // nc, pl.ds(i % nc * fw, fw)], gs_sem.at[i])

    def one(r, carry):
        rows = pl.ds(pl.multiple_of(r * rw, rw), rw)
        part = dot(gs[jnp.bitwise_xor(my_row, r)], gn_ref[...], 0, 0)
        apart(y_ref, rows, (x1_ref[rows, :] + part + pd[rows, 5:6]).astype(bf16))
        return carry

    lax.fori_loop(0, 2, one, 0)


def body(
    tokens,
    cotangent,
    holder_of,
    lengths,
    input_gain,
    input_shift,
    attend_weight,
    attend_bias,
    mixed_gain,
    mixed_shift,
    output_weight,
    output_bias,
    middle_gain,
    middle_shift,
    expand_weight,
    expand_bias,
    hidden_gain,
    hidden_shift,
    shrink_weight,
    shrink_bias,
):
    holders = lax.axis_size("dp")
    half = holders // 2
    nr, nc = lax.axis_size("row"), lax.axis_size("col")
    n = nr * nc
    micro = holder_of.shape[0]
    assert micro == n and nr == 2 and nc == 4
    fl = tokens.shape[0]
    pairs = micro * half
    blk = tokens.shape[1] // pairs
    unit = half * blk
    dp = lax.axis_index("dp")
    side, pos = dp // half, dp % half
    my_row, my_col = lax.axis_index("row"), lax.axis_index("col")
    rc = my_row * nc + my_col
    groups = [list(range(s * half * n, (s + 1) * half * n)) for s in range(2)]
    hw, rw, fw = output_weight.shape[0], output_weight.shape[1], shrink_weight.shape[0]

    def flip_row(v):
        return lax.ppermute(v, "row", [(i, i ^ 1) for i in range(nr)])

    def flip_chip(v):
        return lax.ppermute(v, "col", [(i, i ^ 2) for i in range(nc)])

    def flip_core(v):
        return lax.ppermute(v, "col", [(i, i ^ 1) for i in range(nc)])

    def flip_dp(v, step):
        return lax.ppermute(v, "dp", [(i, i ^ step) for i in range(holders)])

    def exchange(v):
        return lax.all_to_all(v, ("dp",) + RC, 0, 0, axis_index_groups=groups, tiled=True)

    lanes = blk % 128 == 0

    def by_target(v):
        v = jnp.transpose(v.reshape(2, fl, half * n, blk), (2, 0, 1, 3))
        return v.reshape(half * n, 2 * fl, blk)

    def exchange_units(v):
        v = exchange(v).reshape(half, n, 2 * fl, blk)
        return v if lanes else jnp.transpose(v, (1, 2, 0, 3)).reshape(1, n, 2 * fl, unit)

    def from_unit(v):
        if not lanes:
            v = jnp.transpose(v.reshape(n * fl, half, blk), (1, 0, 2))
        v = exchange(v.reshape(half * n, fl, blk))
        return jnp.transpose(v, (1, 0, 2)).reshape(tokens.shape)

    def tie(*values):
        return lax.optimization_barrier(values)

    def near(v):
        return flip_row(v), flip_chip(v)

    def far(v, by_row, by_chip):
        h = v.shape[0] // 2
        return flip_row(by_chip[:h]), flip_chip(by_row[h:])

    def near_flips(v, near_v):
        return tuple(flip_core(p) for p in (v, near_v[1], near_v[0]))

    def pieces_of(v, near_v, flips, far_v):
        v1, c1, r1 = flips
        f1, g1 = (flip_core(p) for p in far_v)
        return (v, v1, near_v[1], c1, near_v[0], r1, far_v[0], far_v[1], f1, g1)

    w1 = jnp.concatenate([attend_weight.reshape(3 * hw, rw), output_weight], axis=0)
    near1 = near(w1)
    tile = jnp.concatenate(
        [
            jnp.stack([input_gain, input_shift, output_bias, middle_gain, middle_shift, shrink_bias]),
            jnp.transpose(
                jnp.stack([attend_bias[0], attend_bias[1], mixed_gain, mixed_shift]).reshape(4, -1, fl), (1, 0, 2)
            ).reshape(-1, fl),
            jnp.transpose(jnp.stack([expand_bias, hidden_gain, hidden_shift]).reshape(3, -1, fl), (1, 0, 2)).reshape(-1, fl),
        ]
    )
    tile = jnp.transpose(jnp.pad(tile, ((0, 128 - tile.shape[0]), (0, 0))))
    ready = by_target(jnp.concatenate([tokens, cotangent], axis=0))
    near1, tile, ready = tie(near1, tile, ready)
    far1 = far(w1, *near1)
    both = exchange_units(ready)
    tile_row, tile_chip = near(tile)
    even = jnp.stack([tile, tile_chip, tile_row, flip_row(tile_chip)])
    odd = flip_core(even)
    flips1 = near_flips(w1, near1)
    far1, flips1, both, odd, w2 = tie(far1, flips1, both, odd, expand_weight)
    near2 = near(w2)
    g1 = pieces_of(w1, near1, flips1, far1)

    k_unit = 2 * (pos * n + rc) + side
    own = lengths[k_unit // holders, holder_of[k_unit // holders, k_unit % holders]]
    info = jnp.concatenate([jnp.stack([rc, my_row]), jnp.cumsum(own)[:-1]]).astype(jnp.int32)

    d = n * fl
    split = lambda v: v.reshape(nr, rw, unit)
    dma = pltpu.SemaphoreType.DMA
    weight_flops = 2 * unit * d * nc * fw

    dp_odd = dp % 2 == 1

    def reduce_rest(v):
        step = 2
        while 2 * step < holders:
            v = v + flip_dp(v, step)
            step *= 2
        return v, flip_dp(v, step) if step < holders else jnp.zeros_like(v)

    def spread(v):
        return v, flip_dp(v, 1)

    def whole(v, got):
        return jnp.concatenate([jnp.where(dp_odd, got, v), jnp.where(dp_odd, v, got)], axis=0).astype(f32)

    vm = lambda shape, dtype=bf16: pltpu.VMEM(shape, dtype)
    act, act32, hid = (d, unit), (nc * hw, unit), (nc, fw, unit)
    part1, part2, part3 = (nr, nc // 2, 4 * hw, rw), (nr, nc // 2, rw, fw), (nr, nc // 2, fw, rw)

    def time_us(t):
        return dict(flops=int(t * 1e9), moved=int(t * 1e6))

    extra = vm((HEAD + 16, unit))
    x, a, qkv, lse, o, pd, pf = call(
        functools.partial(attend_kernel, nc, hw, rw, fl, fw),
        (
            sds(act, bf16), sds(act, bf16), sds((nc, 3 * hw, unit), bf16), sds((nc, 8, unit), f32), sds(act, f32),
            sds((d, 16), f32), sds((nc, fw, 8), f32),
        ),
        [SMEM] + [VMEM] * 3 + [HBM] * 10,
        [VMEM, VMEM, HBM, VMEM, VMEM, VMEM, VMEM],
        [
            vm((nc, 3 * hw, unit)), vm((nc, 3 * hw, nr * rw)), extra, extra,
            dma((n,)), dma((nc,)),
        ],
        **time_us(13), name="attend",
    )(info, both, even, odd, *g1)

    o, near2 = tie(o, near2)
    far2 = far(w2, *near2)
    flips2 = near_flips(w2, near2)

    on, x1, b = call(
        functools.partial(output_kernel, nc, hw, rw),
        (sds(act, bf16), sds(act, f32), sds(act, bf16)),
        [SMEM] + [VMEM] * 3 + [HBM] * 10,
        [VMEM] * 3,
        [vm((nr, nc * hw, rw)), dma((n,))],
        **time_us(5), name="output",
    )(info, x, o, pd, *g1)

    b, far2, flips2, w3 = tie(b, far2, flips2, shrink_weight)
    near3 = near(w3)
    g2 = pieces_of(w2, near2, flips2, far2)

    gn, vh, slope, st = call(
        functools.partial(expand_kernel, nc, rw, fw),
        (sds(hid, bf16), sds(hid, bf16), sds(hid, bf16), sds((8, unit), f32)),
        [SMEM, VMEM, VMEM] + [HBM] * 10,
        [VMEM, HBM, HBM, VMEM],
        [vm(hid), vm(hid), vm(hid, f32), vm((nc, nr * rw, fw)), dma((n,)), dma((2 * nc,))],
        **time_us(13), name="expand",
    )(info, b, pf, *g2)

    gn, near3 = tie(gn, near3)
    far3 = far(w3, *near3)
    flips3 = near_flips(w3, near3)

    e2, shr_keep, shr_send = call(
        functools.partial(shrink_grads_kernel, nc, rw),
        (sds(act, bf16), sds(part3, bf16), sds(part3, bf16)),
        [SMEM] + [VMEM] * 2,
        [VMEM] * 3,
        **time_us(7), name="shrink_grads",
    )(info, gn, both)

    shr_send, far3, flips3 = tie(shr_send, far3, flips3)
    g3 = pieces_of(w3, near3, flips3, far3)
    shr_got = flip_core(shr_send)

    def reduce_near(v):
        return flip_row(v[1]), flip_chip(v[3])

    def reduce_far(v, got, name):
        one = sds(v[0].shape[1:], bf16)
        p0, p1, q0, q1 = call(
            sum_near_kernel, (one, one, one, one), [LOOSE] * 4, [LOOSE] * 4, **time_us(2), name=name
        )(v[0], got[0], v[2], got[1])
        return (p0, q0), (flip_chip(p1), flip_row(q1))

    def reduce_dp(v, got):
        p, q = v[0] + got[0], v[1] + got[1]
        return jnp.where(dp_odd, q, p), flip_dp(jnp.where(dp_odd, p, q), 1)

    sum3 = (nc // 2, fw // 2, rw)
    df, gf, *shr = call(
        functools.partial(hidden_back_kernel, nc, rw, fw),
        (sds(hid, bf16), sds((nc, fw, 8), f32)) + (sds(sum3, bf16),) * 4,
        [SMEM] + [VMEM] * 5 + [HBM] * 12,
        [VMEM] * 2 + [LOOSE] * 4,
        [vm(hid), vm(hid), vm((nc, fw, nr * rw)), vm(hid, f32), dma((n,)), dma((nc,)), dma((nc,))],
        **time_us(13), name="hidden_back",
    )(info, st, e2, pf, shr_keep, shr_got, vh, slope, *g3)

    shr_near = reduce_near(shr)

    dx1, e1, gd_mid = call(
        functools.partial(middle_back_kernel, nc, rw, fw),
        (sds(act, f32), sds(act, bf16), sds((d, 8), f32)),
        [SMEM] + [VMEM] * 4 + [HBM] * 10,
        [VMEM] * 3,
        [vm((nc, nr * rw, fw)), vm(act, f32), dma((n,))],
        **time_us(8), name="middle_back",
    )(info, df, x1, e2, pd, *g2)

    rows2 = 2 * rw + hw
    part2 = (nr, nc // 2, rows2, rw)
    sum2 = (nc // 2, rows2 // 2, rw)
    mid_keep, mid_send = call(
        functools.partial(middle_grads_kernel, nc, hw, rw, fw),
        (sds(part2, bf16), sds(part2, bf16)),
        [SMEM] + [VMEM] * 4,
        [VMEM] * 2,
        **time_us(7), name="middle_grads",
    )(info, b, df, on.reshape(nc, hw, unit), e1)

    e1, mid_send, shr_near = tie(e1, mid_send, shr_near)
    mid_got = flip_core(mid_send)
    shr_stay, shr_far = reduce_far(shr, shr_near, "shrink_sum")

    all_heads = (nc * 3 * hw, unit)
    dqkv, gd_mix, gh, do, qkv, *mid = call(
        functools.partial(attend_back_kernel, nc, hw, rw),
        (sds(all_heads, bf16), sds((d, 8), f32), sds((nc, hw, 8), f32), sds(act, bf16), sds(qkv.shape, bf16))
        + (sds(sum2, bf16),) * 4,
        [SMEM] + [VMEM] * 6 + [HBM] * 11,
        [VMEM] * 9,
        [vm((nc * hw, nr * rw)), vm(act, f32), extra, extra, extra, extra, dma((n,)), dma(())],
        **time_us(11), name="attend_back",
    )(info, e1, o, lse, pd, mid_keep, mid_got, qkv, *g1)

    do, shr_far, mid = tie(do, shr_far, mid)
    shr, shr_dp = reduce_dp(shr_stay, shr_far)
    mid_near = reduce_near(mid)

    dqkv, gh = call(
        functools.partial(attend_back_rest_kernel, nc, hw),
        (sds(all_heads, bf16), sds((nc, hw, 8), f32)),
        [SMEM] + [VMEM] * 6,
        [VMEM] * 2,
        [extra, extra, extra, extra],
        **time_us(8), name="attend_back_rest", aliases={5: 0, 6: 1},
    )(info, o, qkv, lse, do, dqkv, gh)

    dqkv, shr_dp = tie(dqkv, shr_dp)
    shr, shr_rest = reduce_rest(shr + shr_dp)

    input_grad, gd_in = call(
        functools.partial(input_back_kernel, nc, hw, rw),
        (sds((half if lanes else 1, d, blk if lanes else unit), bf16), sds((d, 8), f32)),
        [SMEM] + [VMEM] * 4 + [HBM] * 10,
        [VMEM] * 2,
        [vm((2, nc // 2 * 3 * hw, nr * rw)), vm(act, f32), dma((n,))],
        **time_us(7), name="input_back",
    )(info, dqkv, x, dx1, pd, *g1)

    gd_in, mid_near = tie(gd_in, mid_near)
    p, q = mid[0] + mid_near[0], mid[2] + mid_near[1]
    mid_stay, mid_far = (p[0], q[0]), (flip_chip(p[1]), flip_row(q[1]))

    rows1 = 3 * hw + fl // 3
    part1 = (nr, nc // 2, rows1, rw)
    att_keep, att_send = call(
        functools.partial(attend_grads_kernel, nc, hw, rw, fl, fw),
        (sds(part1, bf16), sds(part1, bf16)),
        [SMEM] + [VMEM] * 7,
        [VMEM] * 2,
        [vm((d, 128), f32), vm((nc, fl, 128), f32)],
        **time_us(7), name="attend_grads",
    )(info, dqkv, a, gd_in, gd_mid, gd_mix, gh, gf)

    att_send, shr_rest, mid_far = tie(att_send, shr_rest, mid_far)
    att_got = flip_core(att_send)
    mid, mid_dp = reduce_dp(mid_stay, mid_far)
    shr, shr_got = spread(shr + shr_rest)
    h = rows1 // 2
    p1, q1 = att_keep[1, :, :h] + att_got[1, :, :h], att_keep[:, 1, h:] + att_got[:, 1, h:]
    p1, q1, y_in = tie(p1, q1, gn)
    p_row, q_chip = flip_row(p1), flip_chip(q1)

    y = call(
        functools.partial(shrink_kernel, nc, rw, fw),
        sds(input_grad.shape, bf16),
        [SMEM] + [VMEM] * 3 + [HBM] * 10,
        VMEM,
        [vm((nr, nc * fw, rw)), dma((n,))],
        **time_us(8), name="shrink",
    )(info, pd, y_in.reshape(nc * fw, unit), x1, *g3)

    y, mid_dp, shr_got, input_grad = tie(y, mid_dp, shr_got, input_grad)
    mid, mid_rest = reduce_rest(mid + mid_dp)
    mid, p_row, q_chip = tie(mid, p_row, q_chip)
    p = att_keep[0, :, :h] + att_got[0, :, :h] + p_row
    q = att_keep[:, 0, h:] + att_got[:, 0, h:] + q_chip
    att_far = flip_chip(p[1]), flip_row(q[1])
    input_grad = from_unit(input_grad)
    att, att_dp = reduce_dp((p[0], q[0]), att_far)
    att_dp, mid_rest, y = tie(att_dp, mid_rest, y)
    block_out = from_unit(y)
    att, att_rest = reduce_rest(att + att_dp)
    mid, mid_got = spread(mid + mid_rest)
    att, att_got = spread(att + att_rest)
    att_got, mid_got, shr_got = tie(att_got, mid_got, shr_got)
    att, mid, shr_w_g = whole(att, att_got), whole(mid, mid_got), whole(shr, shr_got)
    exp_w_g = jnp.concatenate([mid[:rw], mid[rw : 2 * rw]], axis=1)

    thin = att[3 * hw :]
    thin = jnp.transpose(jnp.concatenate([thin[:, k * 128 : (k + 1) * 128] for k in range(3)], axis=0))
    in_g_g, in_s_g, out_b_g, mid_g_g, mid_s_g, shr_b_g = (thin[i] for i in range(6))
    at = 6 + 4 * (hw // fl)
    heads_g = jnp.transpose(thin[6:at].reshape(-1, 4, fl), (1, 0, 2)).reshape(4, hw)
    hidden_g = jnp.transpose(thin[at : at + 3 * (fw // fl)].reshape(-1, 3, fl), (1, 0, 2)).reshape(3, fw)
    q_b_g, v_b_g, mix_g_g, mix_s_g = heads_g
    exp_b_g, hid_g_g, hid_s_g = hidden_g
    return (
        block_out,
        input_grad,
        in_g_g,
        in_s_g,
        att[: 3 * hw].reshape(attend_weight.shape),
        jnp.stack([q_b_g, v_b_g]),
        mix_g_g,
        mix_s_g,
        mid[2 * rw :],
        out_b_g,
        mid_g_g,
        mid_s_g,
        exp_w_g,
        exp_b_g,
        hid_g_g,
        hid_s_g,
        shr_w_g,
        shr_b_g,
    )


def solution(mesh):
    wide, narrow = P(RC), P("col")
    in_specs = (
        P(RC, "dp"), P(RC, "dp"), P(), P(), wide, wide, P(None, "col", "row"), P(None, "col"),
        narrow, narrow, P("col", "row"), wide, wide, wide, P("row", "col"), narrow, narrow, narrow,
        P("col", "row"), wide,
    )
    out_specs = (
        P(RC, "dp"), P(RC, "dp"), wide, wide, P(None, "col", "row"), P(None, "col"), narrow, narrow,
        P("col", "row"), wide, wide, wide, P("row", "col"), narrow, narrow, narrow, P("col", "row"),
        wide,
    )
    return jax.shard_map(body, mesh=mesh, in_specs=in_specs, out_specs=out_specs, check_vma=False)
```
